32 devices in a mesh: dp: 8 (over z, x), tensor: 4 (over y, core).
Axes of the slice: x: 2, y: 2, z: 4, core: 2. Of those that a mesh axis runs over, the one named last changes fastest.
Arguments:
- tokens: bfloat16 [8192, 768], P(('dp', 'tensor')), may hold values from -6 to 6
- timestep: int32 [8], P('dp'), may hold values from 0 to 999
- block_size: int32 [8], P('dp'), may hold values from 128 to 512, as said below
- table: bfloat16 [1000, 768], replicated, may hold values from -6 to 6
- ln1_gain: bfloat16 [2, 768], replicated, may hold values from 0.5 to 1.5
- ln1_bias: bfloat16 [2, 768], replicated, may hold values from -3 to 3
- w_qkv: bfloat16 [2, 768, 3, 768], P(None, None, None, 'tensor'), may hold values from -0.21875 to 0.21875
- w_out: bfloat16 [2, 768, 768], P(None, 'tensor'), may hold values from -0.875 to 0.875
- b_out: bfloat16 [2, 768], replicated, may hold values from -3 to 3
- ln2_gain: bfloat16 [2, 768], replicated, may hold values from 0.5 to 1.5
- ln2_bias: bfloat16 [2, 768], replicated, may hold values from -3 to 3
- w_up: bfloat16 [2, 768, 3072], P(None, None, 'tensor'), may hold values from -0.21875 to 0.21875
- b_up: bfloat16 [2, 3072], P(None, 'tensor'), may hold values from -3 to 3
- w_down: bfloat16 [2, 3072, 768], P(None, 'tensor'), may hold values from -0.109375 to 0.109375
- b_down: bfloat16 [2, 768], replicated, may hold values from -3 to 3
- cotangent: bfloat16 [8192, 768], P(('dp', 'tensor')), may hold values from -6 to 6
Outputs:
- output: bfloat16 [8192, 768], P(('dp', 'tensor'))
- grad_tokens: float32 [8192, 768], P(('dp', 'tensor'))
- grad_table: float32 [1000, 768], P(None, 'dp')
- grad_ln1_gain: float32 [2, 768], P(None, 'dp')
- grad_ln1_bias: float32 [2, 768], P(None, 'dp')
- grad_w_qkv: float32 [2, 768, 3, 768], P(None, 'dp', None, 'tensor')
- grad_w_out: float32 [2, 768, 768], P(None, 'tensor', 'dp')
- grad_b_out: float32 [2, 768], P(None, 'dp')
- grad_ln2_gain: float32 [2, 768], P(None, 'dp')
- grad_ln2_bias: float32 [2, 768], P(None, 'dp')
- grad_w_up: float32 [2, 768, 3072], P(None, 'dp', 'tensor')
- grad_b_up: float32 [2, 3072], P(None, ('tensor', 'dp'))
- grad_w_down: float32 [2, 3072, 768], P(None, 'tensor', 'dp')
- grad_b_down: float32 [2, 768], P(None, 'dp')
The draws below stay inside these ranges and needn't reach their ends.
Inputs may be any that keep to these rules, and one draw needn't show every extreme that they name: `block_size`: every sequence's block length is 128, 256 or 512, and all three occur.
All inputs are finite; a program needn't handle non-finite values.
Results may differ from the reference program's by a relative error of at most 0.019.
Values may be sent and summed in bfloat16 or wider, within the bound.
A program may use at most 192 MiB of HBM per device.

```python
import jax
import jax.numpy as jnp
from jax import lax

D = 768
HEADS = 12
HEAD_DIM = 64
FF = 3072
TSTEPS = 1000
LAYERS = 2
LEN = 1024
SEQS = 8
TOKENS = 8192


def draw_block_size(key, part):
    order = jax.random.permutation(key, SEQS)
    level = order % 3
    return jnp.where(level == 0, LEN // 8, jnp.where(level == 1, LEN // 4, LEN // 2)).astype(jnp.int32)


def place_ends(array, own_key, least, largest):
    spot = [jax.random.randint(jax.random.fold_in(own_key, axis), (), 0, length) for axis, length in enumerate(array.shape)]
    main_axis = array.shape.index(max(array.shape))
    beside = spot[:main_axis] + [(spot[main_axis] + 1) % array.shape[main_axis]] + spot[main_axis + 1:]
    return array.at[tuple(spot)].set(least).at[tuple(beside)].set(largest)


def steps_of(own_key, extent, pieces, low, largest):
    loudness = 1.0
    for axis_at, parts in pieces:
        heights = jax.random.uniform(jax.random.fold_in(jax.random.fold_in(own_key, 6), axis_at), (parts,), jnp.float32, low / len(pieces), largest / len(pieces))
        loudness = loudness * jnp.repeat(jnp.exp(heights), extent[axis_at] // parts).reshape((-1,) + (1,) * (len(extent) - 1 - axis_at))
    return loudness


def noise(own_key, shape, scale, bound, cuts=(), kind=jnp.bfloat16):
    values = jax.random.normal(own_key, shape, jnp.float32) * scale
    if len(cuts) > 0:
        values = steps_of(own_key, shape, cuts, -0.22, 0.18) * values
    return jnp.clip(values, min=-bound, max=bound).astype(kind)


def setup_inputs(seed: int = 0) -> dict:
    arg_keys = jax.random.split(jax.random.key(seed), 17)
    return {
        "tokens": noise(arg_keys[0], (TOKENS, D), 1.0, 6.0, ((0, 32),)),
        "timestep": place_ends(jax.random.randint(arg_keys[1], (SEQS,), 0, TSTEPS), jax.random.fold_in(arg_keys[1], 1), 0, TSTEPS - 1).astype(jnp.int32),
        "block_size": draw_block_size(jax.random.fold_in(arg_keys[16], 71), 0),
        "table": noise(arg_keys[3], (TSTEPS, D), 1.0, 6.0),
        "ln1_gain": jnp.clip(jax.random.uniform(arg_keys[4], (LAYERS, D), jnp.float32, 0.5, 1.5), 0.5, 1.5).astype(jnp.bfloat16),
        "ln1_bias": noise(arg_keys[5], (LAYERS, D), 0.5, 3.0),
        "w_qkv": noise(arg_keys[6], (LAYERS, D, 3, D), D ** -0.5, 0.21875, ((3, 4),)),
        "w_out": noise(arg_keys[7], (LAYERS, D, D), (D // 16) ** -0.5, 0.875, ((1, 4),)),
        "b_out": noise(arg_keys[8], (LAYERS, D), 0.5, 3.0),
        "ln2_gain": jnp.clip(jax.random.uniform(arg_keys[9], (LAYERS, D), jnp.float32, 0.5, 1.5), 0.5, 1.5).astype(jnp.bfloat16),
        "ln2_bias": noise(arg_keys[10], (LAYERS, D), 0.5, 3.0),
        "w_up": noise(arg_keys[11], (LAYERS, D, FF), D ** -0.5, 0.21875, ((2, 4),)),
        "b_up": noise(arg_keys[12], (LAYERS, FF), 0.5, 3.0, ((1, 4),)),
        "w_down": noise(arg_keys[13], (LAYERS, FF, D), FF ** -0.5, 0.109375, ((1, 4),)),
        "b_down": noise(arg_keys[14], (LAYERS, D), 0.5, 3.0),
        "cotangent": noise(arg_keys[15], (TOKENS, D), 1.0, 6.0, ((0, 32),)),
    }


@jax.custom_vjp
def low(v):
    return lax.optimization_barrier(v.astype(jnp.bfloat16)).astype(jnp.float32)

@jax.custom_vjp
def low_back(v):
    return v

def low_keep(v):
    return (low(v), None)

def low_pass(kept, grad):
    return (grad,)

def back_keep(v):
    return (v, None)

def back_low(kept, grad):
    return (low(grad),)
low.defvjp(low_keep, low_pass)
low_back.defvjp(back_keep, back_low)
HIGH = lax.Precision.HIGHEST
EPSILON = 1e-05
NEGATIVE = -1e+30

def norm_apply(hidden, gain, bias):
    mean = lax.optimization_barrier(jnp.mean(hidden, axis=-1, keepdims=True))
    centred = hidden - mean
    spread = lax.optimization_barrier(jnp.mean(centred * centred, axis=-1, keepdims=True))
    return centred * lax.rsqrt(spread + EPSILON) * gain + bias

def block_mask(block):
    where = jnp.arange(LEN, dtype=jnp.int32) // block
    return where[None, :] <= where[:, None]

def one_layer(hidden, params, block):
    gain_one, bias_one, w_qkv, w_out, b_out, gain_two, bias_two, w_up, b_up, w_down, b_down = params
    normed = low(norm_apply(hidden, gain_one, bias_one))
    projected = low_back(low(jnp.einsum('td,dcf->tcf', normed, w_qkv, precision=HIGH)))
    split = projected.reshape(LEN, 3, HEADS, HEAD_DIM)
    visible = block_mask(block)
    scaling = HEAD_DIM ** (-0.5)

    def one_head(query, keys, values):
        scores = low_back(jnp.dot(query, keys.T, precision=HIGH) * scaling)
        scores = jnp.where(visible, scores, NEGATIVE)
        weights = low(jax.nn.softmax(scores, axis=-1))
        return jnp.dot(weights, values, precision=HIGH)
    mixed = jax.vmap(one_head, in_axes=(1, 1, 1), out_axes=1)(split[:, 0], split[:, 1], split[:, 2])
    mixed = low_back(low(mixed.reshape(LEN, D)))
    attended = low_back(jnp.dot(mixed, w_out, precision=HIGH) + b_out)
    middle = hidden + attended
    normed_two = low(norm_apply(middle, gain_two, bias_two))
    pre_act = low_back(jnp.dot(normed_two, w_up, precision=HIGH) + b_up)
    activated = low(jax.nn.gelu(pre_act, approximate=False))
    return middle + low_back(jnp.dot(activated, w_down, precision=HIGH) + b_down)

def reference(tokens, timestep, block_size, table, ln1_gain, ln1_bias, w_qkv, w_out, b_out, ln2_gain, ln2_bias, w_up, b_up, w_down, b_down, cotangent):
    layer_params = tuple((p.astype(jnp.float32) for p in (ln1_gain, ln1_bias, w_qkv, w_out, b_out, ln2_gain, ln2_bias, w_up, b_up, w_down, b_down)))
    table_full = table.astype(jnp.float32)
    sequences = tokens.reshape(SEQS, LEN, D)
    cotangents = cotangent.reshape(SEQS, LEN, D)

    def visit(totals, entry):
        seq_tokens, step_index, block, seq_cot = entry

        def forward(inputs, table_in, params):
            hidden = inputs + table_in[step_index][None, :]
            for layer_index in range(LAYERS):
                hidden = one_layer(hidden, tuple((p[layer_index] for p in params)), block)
            return hidden
        result, pull = jax.vjp(forward, seq_tokens.astype(jnp.float32), table_full, layer_params)
        grad_inputs, grad_tab, grad_params = pull(seq_cot.astype(jnp.float32))
        totals = jax.tree.map(lambda left, right: left + right, totals, (grad_tab, grad_params))
        return (totals, (result.astype(jnp.bfloat16), grad_inputs))
    zeros = jax.tree.map(jnp.zeros_like, (table_full, layer_params))
    totals, (results, grad_rows) = lax.scan(visit, zeros, (sequences, timestep, block_size, cotangents))
    grad_tab, grad_params = totals
    return (results.reshape(TOKENS, D), grad_rows.reshape(TOKENS, D), grad_tab, grad_params[0], grad_params[1], grad_params[2], grad_params[3], grad_params[4], grad_params[5], grad_params[6], grad_params[7], grad_params[8], grad_params[9], grad_params[10])
```

```python
import functools

import jax
import jax.numpy as jnp
from jax import lax
from jax.experimental import pallas as pl
from jax.experimental.pallas import tpu as pltpu
from jax.sharding import PartitionSpec as P

HEAD_DIM = 64
EPSILON = 1e-05
NEGATIVE = -1e30
MESH = pl.DeviceIdType.MESH
BF = jnp.bfloat16
F32 = jnp.float32
INV_SQRT2 = 0.7071067811865476
INV_SQRT2PI = 0.3989422804014327

NN = (((1,), (0,)), ((), ()))
NT = (((1,), (1,)), ((), ()))
TN = (((0,), (0,)), ((), ()))


def mm(a, b, dims=NN):
    return lax.dot_general(a, b, dims, preferred_element_type=F32)


def step_kernel(dim, *refs):
    (
        bs_ref, tok_in, cot_in, emb_in, vec_in, bup_in,
        wqkv_h, wout_h, wup_h, wdown_h,
        out_o, gtok_o, small_o, bupg_o, g_o,
        wqkv, wout, wup, wdown, tokf, cotf,
        a_b, a2_b, g_b, gp_b, qkvT, kv_b, oT_b, lse_b, h_b, m_b,
        df_b, dz_b, du_b, dh_b, doT_b, dqT_b, dkv_acc,
        ysend, yrecv, csend, crecv, part, s_b, p_b, ds_b, gtmp, gstage,
        small, smallr, bupg, outst,
        wsem, tsem_s, tsem_r, ysem_s, ysem_r, casem_s, casem_r, cpsem_s, cpsem_r,
        lsem, osem, gsem, ssem,
    ) = refs
    D, FL, HL, HP, R, L = dim["D"], dim["FL"], dim["HL"], dim["HP"], dim["R"], dim["L"]
    T = 4 * R
    NH = HL // HEAD_DIM
    CH = 2 * R
    NB = D // 256
    FB = FL // 256
    t = lax.axis_index("tensor")
    y = lax.div(t, 2)
    c = lax.rem(t, 2)
    ypeer = lax.rem(t + 2, 4)
    cpeer = t + 1 - 2 * c

    def own(r):
        return pl.multiple_of(R * (2 * r + c), R)

    def oth(r):
        return pl.multiple_of(R * (2 * r + 1 - c), R)

    def remote(src, dst, ss, rs, peer):
        return pltpu.make_async_remote_copy(
            src_ref=src, dst_ref=dst, send_sem=ss, recv_sem=rs,
            device_id={"tensor": peer}, device_id_type=MESH)

    bar = pltpu.get_barrier_semaphore()
    pl.semaphore_signal(bar, inc=1, device_id={"tensor": ypeer}, device_id_type=MESH)
    pl.semaphore_signal(bar, inc=1, device_id={"tensor": cpeer}, device_id_type=MESH)

    wcopies = []
    for l in range(L):
        row = []
        for i, (src, dst) in enumerate(((wqkv_h, wqkv), (wout_h, wout), (wup_h, wup), (wdown_h, wdown))):
            cp = pltpu.make_async_copy(src.at[l], dst.at[l], wsem.at[l, i])
            cp.start()
            row.append(cp)
        wcopies.append(row)
    loc = [pltpu.make_async_copy(tok_in, tokf.at[y], lsem.at[0]),
           pltpu.make_async_copy(cot_in, cotf.at[y], lsem.at[1])]
    for cp in loc:
        cp.start()
    pl.semaphore_wait(bar, 2)
    tcp = [remote(tok_in, tokf.at[y], tsem_s.at[0], tsem_r.at[0], ypeer),
           remote(cot_in, cotf.at[y], tsem_s.at[1], tsem_r.at[1], ypeer)]
    for cp in tcp:
        cp.start()

    small[...] = jnp.zeros_like(small)
    bupg[...] = jnp.zeros_like(bupg)
    dqT_b[...] = jnp.zeros_like(dqT_b)
    oT_b[...] = jnp.zeros_like(oT_b)
    bs = bs_ref[0]

    yc = {}
    pending = {}

    def y_copy(par, r):
        return remote(ysend.at[par, r], yrecv.at[par, r], ysem_s.at[par, r], ysem_r.at[par, r], ypeer)

    def tile_copy(buf, r):
        return remote(buf.at[pl.ds(own(r), R), :], buf.at[pl.ds(own(r), R), :],
                      casem_s.at[r], casem_r.at[r], cpeer)

    def part_copy(r):
        return remote(csend.at[r], crecv.at[r], cpsem_s.at[r], cpsem_r.at[r], cpeer)

    BLK = 32

    def rowloop(fn, init=0):
        return lax.fori_loop(0, R // BLK, lambda i, cy: fn(pl.multiple_of(i * BLK, BLK), cy), init)

    def ln_stats(x):
        mean = jnp.sum(x, axis=-1, keepdims=True) * (1.0 / D)
        xc = x - mean
        var = jnp.sum(xc * xc, axis=-1, keepdims=True) * (1.0 / D)
        return xc, lax.rsqrt(var + EPSILON)

    def enter_fwd(l, r, src, gi, dst_h, dst_a):
        gain = vec_in[l, gi : gi + 1, :]
        bias = vec_in[l, gi + 1 : gi + 2, :]

        def blk(i, cy):
            x = src(i)
            dst_h[l, r, pl.ds(i, BLK), :] = x
            xc, rstd = ln_stats(x)
            dst_a[l, pl.ds(pl.multiple_of(own(r) + i, BLK), BLK), :] = (xc * rstd * gain + bias).astype(BF)
            return cy

        rowloop(blk)
        cp = tile_copy(dst_a.at[l], r)
        cp.start()
        return cp

    def ysum(par, r, i):
        return ysend[par, r, pl.ds(i, BLK), :].astype(F32) + yrecv[par, r, pl.ds(i, BLK), :].astype(F32)

    def wait_y(par, r):
        cp = y_copy(par, r)
        cp.wait_send()
        cp.wait_recv()

    def send_partner(r, fill):
        fill(csend.at[r])
        cp = part_copy(r)
        cp.start()
        return cp

    def combine(par, r, cp):
        cp.wait_recv()

        def blk(i, cy):
            v = part[pl.ds(i, BLK), :] + crecv[r, pl.ds(i, BLK), :].astype(F32)
            ysend[par, r, pl.ds(i, BLK), :] = v.astype(BF)
            return cy

        rowloop(blk)
        cp.wait_send()
        y_copy(par, r).start()

    def qkv_tile(l, q0):
        def one(cc, cy):
            o = pl.multiple_of(cc * HP, HP)
            v = mm(wqkv[l, pl.ds(o, HP), :], a_b[l, pl.ds(q0, R), :], NT).astype(BF)
            qkvT[l, pl.ds(o, HP), pl.ds(q0, R)] = v
            return cy

        q = mm(wqkv[l, 0:HP, :], a_b[l, pl.ds(q0, R), :], NT).astype(BF)
        qkvT[l, 0:HP, pl.ds(q0, R)] = q * jnp.asarray(HEAD_DIM ** -0.5, BF)
        for cc in (1, 2):
            v = mm(wqkv[l, cc * HP : cc * HP + HP, :], a_b[l, pl.ds(q0, R), :], NT)
            qkvT[l, cc * HP : cc * HP + HP, pl.ds(q0, R)] = v.astype(BF)
            kv_b[l, cc - 1, pl.ds(q0, R), :] = v.T.astype(BF)

    def hmask(h):
        rows = lax.broadcasted_iota(jnp.int32, (HP, R), 0)
        return (rows >= h * HEAD_DIM) & (rows < (h + 1) * HEAD_DIM)

    def visible(r, kb, q0):
        key = lax.broadcasted_iota(jnp.int32, (R, R), 0) + (CH * r + kb * R)
        qry = lax.broadcasted_iota(jnp.int32, (R, R), 1) + q0
        return key <= (qry | (bs - 1))

    def att_fwd_tile(l, r, q0):
        KB = 2 * (r + 1)

        def head(h, cy):
            qm = jnp.where(hmask(h), qkvT[l, 0:HP, pl.ds(q0, R)].astype(F32), 0.0).astype(BF)
            top = None
            for kb in range(KB):
                s = mm(kv_b[l, 0, kb * R : kb * R + R, :], qm)
                if kb >= 2 * r:
                    s = jnp.where(visible(r, kb - 2 * r, q0), s, NEGATIVE)
                s_b[kb * R : kb * R + R, :] = s
                mx = jnp.max(s, axis=0, keepdims=True)
                top = mx if top is None else jnp.maximum(top, mx)
            tot = None
            for kb in range(KB):
                e = jnp.exp(s_b[kb * R : kb * R + R, :] - top)
                p_b[kb * R : kb * R + R, :] = e.astype(BF)
                sm = jnp.sum(e, axis=0, keepdims=True)
                tot = sm if tot is None else tot + sm
            hr = pl.multiple_of(h * HEAD_DIM, HEAD_DIM)
            o = mm(qkvT[l, pl.ds(pl.multiple_of(2 * HP + hr, HEAD_DIM), HEAD_DIM), 0 : KB * R], p_b[0 : KB * R, :])
            oT_b[l, pl.ds(hr, HEAD_DIM), pl.ds(q0, R)] = (o * (1.0 / tot)).astype(BF)
            lse_b[l, pl.ds(h, 1), pl.ds(q0, R)] = top + jnp.log(tot)
            return cy

        lax.fori_loop(0, NH, head, 0)

    def nblocks(fn, n):
        for i in range(n):
            fn(i * 256)

    def out_tile(l, q0, dst):
        o = oT_b[l, :, pl.ds(q0, R)].astype(F32).T.astype(BF)

        def one(n):
            dst[:, n : n + 256] = mm(o, wout[l, :, n : n + 256]).astype(dst.dtype)

        nblocks(one, NB)

    def up_tile(l, q0):
        def one(n, cy):
            n = pl.multiple_of(n * 256, 256)
            u = mm(a2_b[l, pl.ds(q0, R), :], wup[l, :, pl.ds(n, 256)]) + bup_in[l, :, pl.ds(n, 256)]
            phi = 0.5 * (1.0 + lax.erf(u * INV_SQRT2))
            g_b[l, pl.ds(q0, R), pl.ds(n, 256)] = (u * phi).astype(BF)
            gp = phi + u * (jnp.exp(u * u * -0.5) * INV_SQRT2PI)
            gp_b[l, pl.ds(q0, R), pl.ds(n, 256)] = gp.astype(BF)
            return cy

        lax.fori_loop(0, FB, one, 0)

    def down_tile(l, q0, dst):
        def one(n):
            dst[:, n : n + 256] = mm(g_b[l, pl.ds(q0, R), :], wdown[l, :, n : n + 256]).astype(dst.dtype)

        nblocks(one, NB)

    def att_fwd(l, r, tile_cp):
        qkv_tile(l, own(r))
        tile_cp.wait_recv()
        qkv_tile(l, oth(r))
        att_fwd_tile(l, r, oth(r))
        cp = send_partner(r, lambda ref: out_tile(l, oth(r), ref))
        att_fwd_tile(l, r, own(r))
        out_tile(l, own(r), part)
        tile_cp.wait_send()
        combine(0, r, cp)

    def ffn_fwd(l, r, tile_cp):
        up_tile(l, own(r))
        tile_cp.wait_recv()
        up_tile(l, oth(r))
        cp = send_partner(r, lambda ref: down_tile(l, oth(r), ref))
        down_tile(l, own(r), part)
        tile_cp.wait_send()
        combine(1, r, cp)

    for l in range(L):
        for r in range(2):
            if l == 0:
                if r == 0:
                    for cp in (loc[0], wcopies[0][0]):
                        cp.wait()
                    tcp[0].wait()
                src = lambda i, r=r: tokf[r, pl.ds(i, BLK), :].astype(F32) + emb_in[...]
            else:
                wait_y(1, r)
                bd = vec_in[l - 1, 5:6, :]
                src = lambda i, r=r, l=l, bd=bd: m_b[l - 1, r, pl.ds(i, BLK), :] + (ysum(1, r, i) + bd)
            if r == 0 and l > 0:
                wcopies[l][0].wait()
            cp = enter_fwd(l, r, src, 0, h_b, a_b)
            if r == 0:
                wcopies[l][1].wait()
            att_fwd(l, r, cp)
        for r in range(2):
            wait_y(0, r)
            bo = vec_in[l, 2:3, :]
            src = lambda i, r=r, l=l, bo=bo: h_b[l, r, pl.ds(i, BLK), :] + (ysum(0, r, i) + bo)
            if r == 0:
                wcopies[l][2].wait()
                wcopies[l][3].wait()
            cp = enter_fwd(l, r, src, 3, m_b, a2_b)
            ffn_fwd(l, r, cp)

    def finish_output(r):
        wait_y(1, r)
        bd = vec_in[L - 1, 5:6, :]

        def blk(i, cy):
            v = m_b[L - 1, r, pl.ds(i, BLK), :] + (ysum(1, r, i) + bd)
            outst[r, pl.ds(i, BLK), :] = v.astype(BF)
            return cy

        rowloop(blk)

    def ln_bwd(l, r, par, gi, xbuf, emit):
        gain = vec_in[l, gi : gi + 1, :]

        def blk(i, cy):
            dg, db = cy
            x = xbuf[l, r, pl.ds(i, BLK), :]
            dy = ysum(par, r, i)
            xc, rstd = ln_stats(x)
            xh = xc * rstd
            t1 = dy * gain
            m1 = jnp.sum(t1, axis=-1, keepdims=True) * (1.0 / D)
            m2 = jnp.sum(t1 * xh, axis=-1, keepdims=True) * (1.0 / D)
            dx = rstd * (t1 - m1 - xh * m2)
            emit(i, dx)
            dg = dg + jnp.sum(dy * xh, axis=0, keepdims=True)
            db = db + jnp.sum(dy, axis=0, keepdims=True)
            return (dg, db)

        z = jnp.zeros((1, D), F32)
        dg, db = rowloop(blk, (z, z))
        small[l, gi : gi + 1, :] = small[l, gi : gi + 1, :] + dg
        small[l, gi + 1 : gi + 2, :] = small[l, gi + 1 : gi + 2, :] + db

    def colsum_own(buf, r, l, row):
        def blk(i, cy):
            return cy + jnp.sum(buf[pl.ds(pl.multiple_of(own(r) + i, BLK), BLK), :].astype(F32), axis=0, keepdims=True)

        v = rowloop(blk, jnp.zeros((1, D), F32))
        small[l, row : row + 1, :] = small[l, row : row + 1, :] + v

    def enter_b1(l, r):
        if l == L - 1:
            def blk(i, cy):
                v = cotf[r, pl.ds(i, BLK), :]
                dh_b[r, pl.ds(i, BLK), :] = v.astype(F32)
                df_b[pl.ds(pl.multiple_of(own(r) + i, BLK), BLK), :] = v
                return cy

            rowloop(blk)
        else:
            wait_y(1, r)

            def emit(i, dx):
                v = dh_b[r, pl.ds(i, BLK), :] + dx
                dh_b[r, pl.ds(i, BLK), :] = v
                df_b[pl.ds(pl.multiple_of(own(r) + i, BLK), BLK), :] = v.astype(BF)

            ln_bwd(l + 1, r, 1, 0, h_b, emit)
        cp = tile_copy(df_b, r)
        cp.start()
        colsum_own(df_b, r, l, 5)
        return cp

    def du_tile(l, q0):
        def one(n, cy):
            n = pl.multiple_of(n * 256, 256)
            dg = mm(df_b[pl.ds(q0, R), :], wdown[l, pl.ds(n, 256), :], NT)
            du = (dg * gp_b[l, pl.ds(q0, R), pl.ds(n, 256)].astype(F32)).astype(BF)
            du_b[pl.ds(q0, R), pl.ds(n, 256)] = du
            bupg[l, :, pl.ds(n, 256)] = bupg[l, :, pl.ds(n, 256)] + jnp.sum(du.astype(F32), axis=0, keepdims=True)
            return cy

        lax.fori_loop(0, FB, one, 0)

    def da2_tile(l, q0, dst):
        def one(n):
            dst[:, n : n + 256] = mm(du_b[pl.ds(q0, R), :], wup[l, n : n + 256, :], NT).astype(dst.dtype)

        nblocks(one, NB)

    def ffn_bwd(l, r, tile_cp):
        du_tile(l, own(r))
        tile_cp.wait_recv()
        du_tile(l, oth(r))
        cp = send_partner(r, lambda ref: da2_tile(l, oth(r), ref))
        da2_tile(l, own(r), part)
        tile_cp.wait_send()
        combine(0, r, cp)

    def enter_b2(l, r):
        wait_y(0, r)

        def emit(i, dx):
            v = dh_b[r, pl.ds(i, BLK), :] + dx
            dh_b[r, pl.ds(i, BLK), :] = v
            dz_b[pl.ds(pl.multiple_of(own(r) + i, BLK), BLK), :] = v.astype(BF)

        ln_bwd(l, r, 0, 3, m_b, emit)
        cp = tile_copy(dz_b, r)
        cp.start()
        colsum_own(dz_b, r, l, 2)
        return cp

    def do_tile(l, q0):
        doT_b[:, pl.ds(q0, R)] = mm(wout[l], dz_b[pl.ds(q0, R), :], NT).astype(BF)

    def att_bwd_tile(l, r, q0):
        KB = 2 * (r + 1)
        KN = KB * R

        def head(h, cy):
            hr = pl.multiple_of(h * HEAD_DIM, HEAD_DIM)
            hm = hmask(h)
            qm = jnp.where(hm, qkvT[l, 0:HP, pl.ds(q0, R)].astype(F32), 0.0).astype(BF)
            dom = jnp.where(hm, doT_b[:, pl.ds(q0, R)].astype(F32), 0.0).astype(BF)
            do_h = doT_b[pl.ds(hr, HEAD_DIM), pl.ds(q0, R)]
            q_h = qkvT[l, pl.ds(hr, HEAD_DIM), pl.ds(q0, R)]
            o_h = oT_b[l, pl.ds(hr, HEAD_DIM), pl.ds(q0, R)]
            dsum = jnp.sum(do_h.astype(F32) * o_h.astype(F32), axis=0, keepdims=True)
            lse = lse_b[l, pl.ds(h, 1), pl.ds(q0, R)]
            for kb in range(KB):
                ks = slice(kb * R, kb * R + R)
                s = mm(kv_b[l, 0, ks, :], qm)
                p = jnp.exp(s - lse)
                if kb >= 2 * r:
                    p = jnp.where(visible(r, kb - 2 * r, q0), p, 0.0)
                p_b[ks, :] = p.astype(BF)
                dp = mm(kv_b[l, 1, ks, :], dom)
                ds_b[ks, :] = (p * (dp - dsum)).astype(BF)
            dkv_acc[1, pl.ds(hr, HEAD_DIM), 0:KN] = dkv_acc[1, pl.ds(hr, HEAD_DIM), 0:KN] + mm(do_h, p_b[0:KN, :], NT)
            dkv_acc[0, pl.ds(hr, HEAD_DIM), 0:KN] = dkv_acc[0, pl.ds(hr, HEAD_DIM), 0:KN] + mm(q_h, ds_b[0:KN, :], NT)
            k_h = qkvT[l, pl.ds(pl.multiple_of(HP + hr, HEAD_DIM), HEAD_DIM), 0:KN]
            dq = mm(k_h, ds_b[0:KN, :]) * (HEAD_DIM ** -0.5)
            dqT_b[pl.ds(hr, HEAD_DIM), pl.ds(q0, R)] = dq.astype(BF)
            return cy

        lax.fori_loop(0, NH, head, 0)

    def da_tile(l, q0, dst):
        dqkv = dqT_b[:, pl.ds(q0, R)].astype(F32).T.astype(BF)

        def one(n):
            dst[:, n : n + 256] = mm(dqkv, wqkv[l, :, n : n + 256]).astype(dst.dtype)

        nblocks(one, NB)

    def att_bwd(l, r, tile_cp):
        do_tile(l, own(r))
        att_bwd_tile(l, r, own(r))
        tile_cp.wait_recv()
        do_tile(l, oth(r))
        att_bwd_tile(l, r, oth(r))
        cs = slice(CH * r, CH * r + CH)
        for j in range(2):
            dqT_b[HP * (j + 1) : HP * (j + 1) + HL, cs] = dkv_acc[j, 0:HL, cs].astype(BF)
        cp = send_partner(r, lambda ref: da_tile(l, oth(r), ref))
        da_tile(l, own(r), part)
        tile_cp.wait_send()
        combine(1, r, cp)

    gcount = [0]

    def g_out(l, j):
        cp = pltpu.make_async_copy(gstage, g_o.at[l, j], gsem)
        cp.start()
        cp.wait()

    def wgrad_ffn(l):
        for j, (lhs, rhs) in ((1, (a2_b.at[l], du_b)), (2, (df_b, g_b.at[l]))):
            for n in range(NB):
                lt = lhs[:, n * 256 : n * 256 + 256].astype(F32).T.astype(BF)
                for f in range(FB):
                    gstage[n * 256 : n * 256 + 256, f * 256 : f * 256 + 256] = mm(lt, rhs[:, f * 256 : f * 256 + 256])
            g_out(l, j)

    def wgrad_att(l):
        for n in range(NB):
            ns = slice(n * 256, n * 256 + 256)
            for j in range(3):
                gtmp[j * HL : j * HL + HL, :] = mm(dqT_b[j * HP : j * HP + HL, :], a_b[l, :, ns])
            gtmp[3 * HL : 4 * HL, :] = mm(oT_b[l, 0:HL, :], dz_b[:, ns])
            gstage[ns, 0 : 4 * HL] = gtmp[...].T
        g_out(l, 0)

    loc[1].wait()
    tcp[1].wait()
    for l in range(L - 1, -1, -1):
        for r in (1, 0):
            cp = enter_b1(l, r)
            if l == L - 1:
                finish_output(r)
            ffn_bwd(l, r, cp)
        wgrad_ffn(l)
        dkv_acc[...] = jnp.zeros_like(dkv_acc)
        for r in (1, 0):
            cp = enter_b2(l, r)
            att_bwd(l, r, cp)
        wgrad_att(l)
    ocp = pltpu.make_async_copy(outst.at[y], out_o, osem.at[0])
    ocp.start()
    for r in (1, 0):
        wait_y(1, r)

        def emit(i, dx, r=r):
            dh_b[r, pl.ds(i, BLK), :] = dh_b[r, pl.ds(i, BLK), :] + dx

        ln_bwd(0, r, 1, 0, h_b, emit)

        def blk(i, cy, r=r):
            return cy + jnp.sum(dh_b[r, pl.ds(i, BLK), :], axis=0, keepdims=True)

        v = rowloop(blk, jnp.zeros((1, D), F32))
        small[0, 6:7, :] = small[0, 6:7, :] + v
    gcp = pltpu.make_async_copy(dh_b.at[y], gtok_o, osem.at[1])
    gcp.start()
    scp = remote(small, smallr, ssem.at[0], ssem.at[1], cpeer)
    scp.start()
    scp.wait()
    small_o[...] = small[...] + smallr[...]
    bupg_o[...] = bupg[...]
    ocp.wait()
    gcp.wait()


def run_step(bs, tok, cot, emb, vec, bup, wqkv, wout, wup, wdown):
    R, D = tok.shape
    L, _, FL = wup.shape
    HP = wout.shape[1]
    HL = dims_hl(HP)
    T = 4 * R
    dim = dict(D=D, FL=FL, HL=HL, HP=HP, R=R, L=L)
    vm = pl.BlockSpec(memory_space=pltpu.VMEM)
    any_ = pl.BlockSpec(memory_space=pl.ANY)
    dma = pltpu.SemaphoreType.DMA
    V = pltpu.VMEM
    return pl.pallas_call(
        functools.partial(step_kernel, dim),
        out_shape=(
            jax.ShapeDtypeStruct((R, D), BF),
            jax.ShapeDtypeStruct((R, D), F32),
            jax.ShapeDtypeStruct((L, 8, D), F32),
            jax.ShapeDtypeStruct((L, 1, FL), F32),
            jax.ShapeDtypeStruct((L, 3, D, FL), F32),
        ),
        in_specs=[pl.BlockSpec(memory_space=pltpu.SMEM), vm, vm, vm, vm, vm] + [any_] * 4,
        out_specs=(any_, any_, vm, vm, any_),
        scratch_shapes=[
            V((L, 3 * HP, D), BF), V((L, HP, D), BF), V((L, D, FL), BF), V((L, FL, D), BF),
            V((2, R, D), BF), V((2, R, D), BF),
            V((L, T, D), BF), V((L, T, D), BF), V((L, T, FL), BF), V((L, T, FL), BF),
            V((L, 3 * HP, T), BF), V((L, 2, T, HP), BF), V((L, HP, T), BF), V((L, 8, T), F32),
            V((L, 2, R, D), F32), V((L, 2, R, D), F32),
            V((T, D), BF), V((T, D), BF), V((T, FL), BF), V((2, R, D), F32),
            V((HP, T), BF), V((3 * HP, T), BF), V((2, HP, T), F32),
            V((2, 2, R, D), BF), V((2, 2, R, D), BF), V((2, R, D), BF), V((2, R, D), BF),
            V((R, D), F32), V((T, R), F32), V((T, R), BF), V((T, R), BF), V((4 * HL, 256), F32), V((D, FL), F32),
            V((L, 8, D), F32), V((L, 8, D), F32), V((L, 1, FL), F32), V((2, R, D), BF),
            dma((L, 4)), dma((2,)), dma((2,)), dma((2, 2)), dma((2, 2)),
            dma((2,)), dma((2,)), dma((2,)), dma((2,)),
            dma((2,)), dma((2,)), dma, dma((2,)),
        ],
        compiler_params=pltpu.CompilerParams(
            collective_id=0, has_side_effects=True, vmem_limit_bytes=67043328),
        name="layers",
    )(bs, tok, cot, emb, vec, bup, wqkv, wout, wup, wdown)


def dims_hl(hp):
    return hp - HEAD_DIM


def local(tokens, timestep, block_size, table, ln1_gain, ln1_bias, w_qkv, w_out, b_out,
          ln2_gain, ln2_bias, w_up, b_up, w_down, b_down, cotangent):
    L, D, _, HL = w_qkv.shape
    FL = w_up.shape[-1]
    R = tokens.shape[0]
    dp = lax.axis_size("dp")
    pad = HEAD_DIM
    emb = lax.dynamic_slice_in_dim(table, timestep[0], 1, 0).astype(F32)
    zero = jnp.zeros_like(b_out)
    vec = jnp.stack([ln1_gain, ln1_bias, b_out, ln2_gain, ln2_bias, b_down, zero, zero], axis=1).astype(F32)
    bup = b_up[:, None, :].astype(F32)
    wq = jnp.pad(jnp.transpose(w_qkv, (0, 2, 3, 1)), ((0, 0), (0, 0), (0, pad), (0, 0))).reshape(L, 3 * (HL + pad), D)
    wo = jnp.pad(w_out, ((0, 0), (0, pad), (0, 0)))
    out, gtok, small, bupg, g = run_step(block_size, tokens, cotangent, emb, vec, bup, wq, wo, w_up, w_down)
    per = D // dp
    gs = lax.psum_scatter(g, "dp", scatter_dimension=2, tiled=True)
    ssum = lax.psum_scatter(jnp.concatenate([small[:, :6], bupg], axis=1), "dp", scatter_dimension=2, tiled=True)
    cols = lax.all_to_all(small[0, 6:7], "dp", split_axis=1, concat_axis=0, tiled=True)
    steps = lax.all_gather(timestep, "dp", axis=0, tiled=True)
    pick = (steps[:, None] == jnp.arange(table.shape[0], dtype=jnp.int32)[None, :]).astype(F32)
    grad_table = jnp.einsum("sn,sd->nd", pick, cols, precision=lax.Precision.HIGHEST)
    gq = gs[:, 0, :, : 3 * HL].reshape(L, per, 3, HL)
    go = jnp.transpose(gs[:, 0, :, 3 * HL :], (0, 2, 1))
    gd = jnp.transpose(gs[:, 2], (0, 2, 1))
    return (out, gtok, grad_table, ssum[:, 0], ssum[:, 1], gq, go, ssum[:, 2], ssum[:, 3], ssum[:, 4],
            gs[:, 1], ssum[:, 6], gd, ssum[:, 5])


def solution(mesh):
    placed = (
        P(("dp", "tensor"), None), P("dp"), P("dp"), P(), P(), P(),
        P(None, None, None, "tensor"), P(None, "tensor", None), P(), P(), P(),
        P(None, None, "tensor"), P(None, "tensor"), P(None, "tensor", None), P(),
        P(("dp", "tensor"), None),
    )
    return jax.shard_map(
        local,
        mesh=mesh,
        in_specs=placed,
        out_specs=(
            P(("dp", "tensor"), None), P(("dp", "tensor"), None), P(None, "dp"), P(None, "dp"), P(None, "dp"),
            P(None, "dp", None, "tensor"), P(None, "tensor", "dp"), P(None, "dp"), P(None, "dp"), P(None, "dp"),
            P(None, "dp", "tensor"), P(None, ("tensor", "dp")), P(None, "tensor", "dp"), P(None, "dp"),
        ),
        check_vma=False,
    )
```

```python
import functools

import jax
import jax.numpy as jnp
from jax import lax
from jax.experimental import pallas as pl
from jax.experimental.pallas import tpu as pltpu
from jax.sharding import PartitionSpec as P

HEAD_DIM = 64
EPSILON = 1e-05
NEGATIVE = -1e30
MESH = pl.DeviceIdType.MESH
BF = jnp.bfloat16
F32 = jnp.float32
INV_SQRT2 = 0.7071067811865476
INV_SQRT2PI = 0.3989422804014327

NN = (((1,), (0,)), ((), ()))
NT = (((1,), (1,)), ((), ()))
TN = (((0,), (0,)), ((), ()))


def mm(a, b, dims=NN):
    return lax.dot_general(a, b, dims, preferred_element_type=F32)


def step_kernel(dim, *refs):
    (
        ts_ref, bs_ref, g1_in, b1_in, bo_in, g2_in, b2_in, bd_in, bup_in,
        tok_in, cot_in, table_h, wqkv_h, wout_h, wup_h, wdown_h,
        out_o, gtok_o, small_o, seq_o, g_o,
        wqkv, wout, wup, wdown, tokf, cotf,
        a_b, a2_b, g_b, gp_b, qkvT, kv_b, oT_b, lse_b, h_b, m_b,
        df_b, dz_b, dh_b, doT_b, dqT_b, dkv_acc,
        ysend, yrecv, csend, crecv, part, s_b, p_b, ds_b, gtmp, gstage,
        small, smallr, smallx, smallz, seqt, seqall, emb_b,
        send1, recv1, own1, send2, recv2, fstage,
        wsem, tsem_s, tsem_r, ysem_s, ysem_r, casem_s, casem_r, cpsem_s, cpsem_r,
        lsem, osem, gsem, ssem, qsem_s, qsem_r, x1s, x1r, x2s, x2r,
        r1s, r1r, r2s, r2r,
    ) = refs
    D, FL, HL, R, L = dim["D"], dim["FL"], dim["HL"], dim["R"], dim["L"]
    N, NI, NO, PER, FUSED = dim["N"], dim["NI"], dim["NO"], dim["PER"], dim["FUSED"]
    HP = HL
    vecs = (g1_in, b1_in, bo_in, g2_in, b2_in, bd_in)

    def vrow(i, l):
        return vecs[i][l : l + 1, :].astype(F32)

    T = 4 * R
    NH = HL // HEAD_DIM
    CH = 2 * R
    NB = D // 256
    FB = FL // 256
    t = lax.axis_index("tensor")
    d = lax.axis_index("dp")
    di = lax.rem(d, NI)
    do_ = lax.div(d, NI)
    y = lax.div(t, 2)
    c = lax.rem(t, 2)
    ypeer = lax.rem(t + 2, 4)
    cpeer = t + 1 - 2 * c

    def own(r):
        return pl.multiple_of(R * (2 * r + c), R)

    def oth(r):
        return pl.multiple_of(R * (2 * r + 1 - c), R)

    def remote(src, dst, ss, rs, peer):
        return pltpu.make_async_remote_copy(
            src_ref=src, dst_ref=dst, send_sem=ss, recv_sem=rs,
            device_id={"tensor": peer}, device_id_type=MESH)

    def dp_remote(src, dst, ss, rs, peer):
        return pltpu.make_async_remote_copy(
            src_ref=src, dst_ref=dst, send_sem=ss, recv_sem=rs,
            device_id={"dp": peer}, device_id_type=MESH)

    bar = pltpu.get_barrier_semaphore()

    def greet(k, cy):
        pl.semaphore_signal(bar, inc=1, device_id={"dp": lax.rem(d + k, N)}, device_id_type=MESH)
        return cy

    lax.fori_loop(1, N, greet, 0)
    pl.semaphore_signal(bar, inc=1, device_id={"tensor": ypeer}, device_id_type=MESH)
    pl.semaphore_signal(bar, inc=1, device_id={"tensor": cpeer}, device_id_type=MESH)

    wcopies = []
    for l in range(L):
        row = []
        for i, (src, dst) in enumerate(((wqkv_h, wqkv), (wout_h, wout), (wup_h, wup), (wdown_h, wdown))):
            cp = pltpu.make_async_copy(src.at[l], dst.at[l], wsem.at[l, i])
            cp.start()
            row.append(cp)
        wcopies.append(row)
    loc = [pltpu.make_async_copy(tok_in, tokf.at[y], lsem.at[0]),
           pltpu.make_async_copy(cot_in, cotf.at[y], lsem.at[1]),
           pltpu.make_async_copy(table_h, df_b.at[pl.ds(0, dim["TS"]), :], lsem.at[2])]
    for cp in loc:
        cp.start()
    pl.semaphore_wait(bar, N + 1)
    tcp = [remote(tok_in, tokf.at[y], tsem_s.at[0], tsem_r.at[0], ypeer),
           remote(cot_in, cotf.at[y], tsem_s.at[1], tsem_r.at[1], ypeer)]
    for cp in tcp:
        cp.start()

    small[...] = jnp.zeros_like(small)
    bs = bs_ref[0]
    loc[2].wait()
    pick = (lax.broadcasted_iota(jnp.int32, (8, dim["TS"]), 1) == ts_ref[0]).astype(BF)
    emb_b[...] = mm(pick, df_b[0 : dim["TS"], :])

    def y_copy(par, r):
        return remote(ysend.at[par, r], yrecv.at[par, r], ysem_s.at[par, r], ysem_r.at[par, r], ypeer)

    def tile_copy(buf, r):
        return remote(buf.at[pl.ds(own(r), R), :], buf.at[pl.ds(own(r), R), :],
                      casem_s.at[r], casem_r.at[r], cpeer)

    def part_copy(r):
        return remote(csend.at[r], crecv.at[r], cpsem_s.at[r], cpsem_r.at[r], cpeer)

    BLK = 32

    def rowloop(fn, init=0):
        return lax.fori_loop(0, R // BLK, lambda i, cy: fn(pl.multiple_of(i * BLK, BLK), cy), init)

    def ln_stats(x):
        mean = jnp.sum(x, axis=-1, keepdims=True) * (1.0 / D)
        xc = x - mean
        var = jnp.sum(xc * xc, axis=-1, keepdims=True) * (1.0 / D)
        return xc, lax.rsqrt(var + EPSILON)

    def enter_fwd(l, r, src, gi, dst_h, dst_a):
        gain = vrow(gi, l)
        bias = vrow(gi + 1, l)

        def blk(i, cy):
            x = src(i)
            dst_h[l, r, pl.ds(i, BLK), :] = x
            xc, rstd = ln_stats(x)
            dst_a[l, pl.ds(pl.multiple_of(own(r) + i, BLK), BLK), :] = (xc * rstd * gain + bias).astype(BF)
            return cy

        rowloop(blk)
        cp = tile_copy(dst_a.at[l], r)
        cp.start()
        return cp

    def ysum(par, r, i):
        return ysend[par, r, pl.ds(i, BLK), :].astype(F32) + yrecv[par, r, pl.ds(i, BLK), :].astype(F32)

    def wait_y(par, r):
        cp = y_copy(par, r)
        cp.wait_send()
        cp.wait_recv()

    def send_partner(r, fill):
        fill(csend.at[r])
        cp = part_copy(r)
        cp.start()
        return cp

    def combine(par, r, cp):
        cp.wait_recv()

        def blk(i, cy):
            v = part[pl.ds(i, BLK), :] + crecv[r, pl.ds(i, BLK), :].astype(F32)
            ysend[par, r, pl.ds(i, BLK), :] = v.astype(BF)
            return cy

        rowloop(blk)
        cp.wait_send()
        y_copy(par, r).start()

    def qkv_tile(l, q0):
        q = mm(wqkv[l, 0:HP, :], a_b[l, pl.ds(q0, R), :], NT).astype(BF)
        qkvT[l, 0:HP, pl.ds(q0, R)] = q * jnp.asarray(HEAD_DIM ** -0.5, BF)
        for cc in (1, 2):
            v = mm(wqkv[l, cc * HP : cc * HP + HP, :], a_b[l, pl.ds(q0, R), :], NT)
            qkvT[l, cc * HP : cc * HP + HP, pl.ds(q0, R)] = v.astype(BF)
            kv_b[l, cc - 1, pl.ds(q0, R), :] = v.T.astype(BF)

    def hmask(h):
        rows = lax.broadcasted_iota(jnp.int32, (HP, R), 0)
        return (rows >= h * HEAD_DIM) & (rows < (h + 1) * HEAD_DIM)

    def visible(r, kb, q0):
        key = lax.broadcasted_iota(jnp.int32, (R, R), 0) + (CH * r + kb * R)
        qry = lax.broadcasted_iota(jnp.int32, (R, R), 1) + q0
        return key <= (qry | (bs - 1))

    def att_fwd_tile(l, r, q0):
        KB = 2 * (r + 1)

        def head(h, cy):
            qm = jnp.where(hmask(h), qkvT[l, 0:HP, pl.ds(q0, R)].astype(F32), 0.0).astype(BF)
            top = None
            for kb in range(KB):
                s = mm(kv_b[l, 0, kb * R : kb * R + R, :], qm)
                if kb >= 2 * r:
                    s = jnp.where(visible(r, kb - 2 * r, q0), s, NEGATIVE)
                s_b[kb * R : kb * R + R, :] = s
                mx = jnp.max(s, axis=0, keepdims=True)
                top = mx if top is None else jnp.maximum(top, mx)
            tot = None
            for kb in range(KB):
                e = jnp.exp(s_b[kb * R : kb * R + R, :] - top)
                p_b[kb * R : kb * R + R, :] = e.astype(BF)
                sm = jnp.sum(e, axis=0, keepdims=True)
                tot = sm if tot is None else tot + sm
            hr = pl.multiple_of(h * HEAD_DIM, HEAD_DIM)
            o = mm(qkvT[l, pl.ds(pl.multiple_of(2 * HP + hr, HEAD_DIM), HEAD_DIM), 0 : KB * R], p_b[0 : KB * R, :])
            oT_b[l, pl.ds(hr, HEAD_DIM), pl.ds(q0, R)] = (o * (1.0 / tot)).astype(BF)
            lse_b[l, pl.ds(h, 1), pl.ds(q0, R)] = top + jnp.log(tot)
            return cy

        lax.fori_loop(0, NH, head, 0)

    def nblocks(fn, n):
        for i in range(n):
            fn(i * 256)

    def out_tile(l, q0, dst):
        o = oT_b[l, :, pl.ds(q0, R)].astype(F32).T.astype(BF)

        def one(n):
            dst[:, n : n + 256] = mm(o, wout[l, :, n : n + 256]).astype(dst.dtype)

        nblocks(one, NB)

    def up_tile(l, q0):
        def one(n, cy):
            n = pl.multiple_of(n * 256, 256)
            u = mm(a2_b[l, pl.ds(q0, R), :], wup[l, :, pl.ds(n, 256)]) + bup_in[l : l + 1, pl.ds(n, 256)].astype(F32)
            phi = 0.5 * (1.0 + lax.erf(u * INV_SQRT2))
            g_b[l, pl.ds(q0, R), pl.ds(n, 256)] = (u * phi).astype(BF)
            gp = phi + u * (jnp.exp(u * u * -0.5) * INV_SQRT2PI)
            gp_b[l, pl.ds(q0, R), pl.ds(n, 256)] = gp.astype(BF)
            return cy

        lax.fori_loop(0, FB, one, 0)

    def down_tile(l, q0, dst):
        def one(n):
            dst[:, n : n + 256] = mm(g_b[l, pl.ds(q0, R), :], wdown[l, :, n : n + 256]).astype(dst.dtype)

        nblocks(one, NB)

    def att_fwd(l, r, tile_cp):
        qkv_tile(l, own(r))
        tile_cp.wait_recv()
        qkv_tile(l, oth(r))
        att_fwd_tile(l, r, oth(r))
        cp = send_partner(r, lambda ref: out_tile(l, oth(r), ref))
        att_fwd_tile(l, r, own(r))
        out_tile(l, own(r), part)
        tile_cp.wait_send()
        combine(0, r, cp)

    def ffn_fwd(l, r, tile_cp):
        up_tile(l, own(r))
        tile_cp.wait_recv()
        up_tile(l, oth(r))
        cp = send_partner(r, lambda ref: down_tile(l, oth(r), ref))
        down_tile(l, own(r), part)
        tile_cp.wait_send()
        combine(1, r, cp)

    for l in range(L):
        for r in range(2):
            if l == 0:
                if r == 0:
                    for cp in (loc[0], wcopies[0][0]):
                        cp.wait()
                    tcp[0].wait()
                src = lambda i, r=r: tokf[r, pl.ds(i, BLK), :].astype(F32) + emb_b[0:1, :]
            else:
                wait_y(1, r)
                bd = vrow(5, l - 1)
                src = lambda i, r=r, l=l, bd=bd: m_b[l - 1, r, pl.ds(i, BLK), :] + (ysum(1, r, i) + bd)
            if r == 0 and l > 0:
                wcopies[l][0].wait()
            cp = enter_fwd(l, r, src, 0, h_b, a_b)
            if r == 0:
                wcopies[l][1].wait()
            att_fwd(l, r, cp)
        for r in range(2):
            wait_y(0, r)
            bo = vrow(2, l)
            src = lambda i, r=r, l=l, bo=bo: h_b[l, r, pl.ds(i, BLK), :] + (ysum(0, r, i) + bo)
            if r == 0:
                wcopies[l][2].wait()
                wcopies[l][3].wait()
            cp = enter_fwd(l, r, src, 3, m_b, a2_b)
            ffn_fwd(l, r, cp)

    def finish_output(r):
        wait_y(1, r)
        bd = vrow(5, L - 1)

        def blk(i, cy):
            v = m_b[L - 1, r, pl.ds(i, BLK), :] + (ysum(1, r, i) + bd)
            tokf[r, pl.ds(i, BLK), :] = v.astype(BF)
            return cy

        rowloop(blk)

    def ln_bwd(l, r, par, gi, xbuf, emit):
        gain = vrow(gi, l)

        def blk(i, cy):
            dg, db = cy
            x = xbuf[l, r, pl.ds(i, BLK), :]
            dy = ysum(par, r, i)
            xc, rstd = ln_stats(x)
            xh = xc * rstd
            t1 = dy * gain
            m1 = jnp.sum(t1, axis=-1, keepdims=True) * (1.0 / D)
            m2 = jnp.sum(t1 * xh, axis=-1, keepdims=True) * (1.0 / D)
            dx = rstd * (t1 - m1 - xh * m2)
            emit(i, dx)
            dg = dg + jnp.sum(dy * xh, axis=0, keepdims=True)
            db = db + jnp.sum(dy, axis=0, keepdims=True)
            return (dg, db)

        z = jnp.zeros((1, D), F32)
        dg, db = rowloop(blk, (z, z))
        small[l, gi : gi + 1, :] = small[l, gi : gi + 1, :] + dg
        small[l, gi + 1 : gi + 2, :] = small[l, gi + 1 : gi + 2, :] + db

    def colsum_own(buf, r, l, row):
        def blk(i, cy):
            return cy + jnp.sum(buf[pl.ds(pl.multiple_of(own(r) + i, BLK), BLK), :].astype(F32), axis=0, keepdims=True)

        v = rowloop(blk, jnp.zeros((1, D), F32))
        small[l, row : row + 1, :] = small[l, row : row + 1, :] + v

    def enter_b1(l, r):
        if l == L - 1:
            def blk(i, cy):
                v = cotf[r, pl.ds(i, BLK), :]
                dh_b[r, pl.ds(i, BLK), :] = v.astype(F32)
                df_b[pl.ds(pl.multiple_of(own(r) + i, BLK), BLK), :] = v
                return cy

            rowloop(blk)
        else:
            wait_y(1, r)

            def emit(i, dx):
                v = dh_b[r, pl.ds(i, BLK), :] + dx
                dh_b[r, pl.ds(i, BLK), :] = v
                df_b[pl.ds(pl.multiple_of(own(r) + i, BLK), BLK), :] = v.astype(BF)

            ln_bwd(l + 1, r, 1, 0, h_b, emit)
        cp = tile_copy(df_b, r)
        cp.start()
        colsum_own(df_b, r, l, 5)
        return cp

    def du_tile(l, q0):
        def one(n, cy):
            n = pl.multiple_of(n * 256, 256)
            dg = mm(df_b[pl.ds(q0, R), :], wdown[l, pl.ds(n, 256), :], NT)
            du = (dg * gp_b[l, pl.ds(q0, R), pl.ds(n, 256)].astype(F32)).astype(BF)
            gp_b[l, pl.ds(q0, R), pl.ds(n, 256)] = du
            small[l, 7:8, pl.ds(n, 256)] = small[l, 7:8, pl.ds(n, 256)] + jnp.sum(du.astype(F32), axis=0, keepdims=True)
            return cy

        lax.fori_loop(0, FB, one, 0)

    def da2_tile(l, q0, dst):
        def one(n):
            dst[:, n : n + 256] = mm(gp_b[l, pl.ds(q0, R), :], wup[l, n : n + 256, :], NT).astype(dst.dtype)

        nblocks(one, NB)

    def ffn_bwd(l, r, tile_cp):
        du_tile(l, own(r))
        tile_cp.wait_recv()
        du_tile(l, oth(r))
        cp = send_partner(r, lambda ref: da2_tile(l, oth(r), ref))
        da2_tile(l, own(r), part)
        tile_cp.wait_send()
        combine(0, r, cp)

    def enter_b2(l, r):
        wait_y(0, r)

        def emit(i, dx):
            v = dh_b[r, pl.ds(i, BLK), :] + dx
            dh_b[r, pl.ds(i, BLK), :] = v
            dz_b[pl.ds(pl.multiple_of(own(r) + i, BLK), BLK), :] = v.astype(BF)

        ln_bwd(l, r, 0, 3, m_b, emit)
        cp = tile_copy(dz_b, r)
        cp.start()
        colsum_own(dz_b, r, l, 2)
        return cp

    def do_tile(l, q0):
        doT_b[:, pl.ds(q0, R)] = mm(wout[l], dz_b[pl.ds(q0, R), :], NT).astype(BF)

    def att_bwd_tile(l, r, q0):
        KB = 2 * (r + 1)
        KN = KB * R

        def head(h, cy):
            hr = pl.multiple_of(h * HEAD_DIM, HEAD_DIM)
            hm = hmask(h)
            qm = jnp.where(hm, qkvT[l, 0:HP, pl.ds(q0, R)].astype(F32), 0.0).astype(BF)
            dom = jnp.where(hm, doT_b[:, pl.ds(q0, R)].astype(F32), 0.0).astype(BF)
            do_h = doT_b[pl.ds(hr, HEAD_DIM), pl.ds(q0, R)]
            q_h = qkvT[l, pl.ds(hr, HEAD_DIM), pl.ds(q0, R)]
            o_h = oT_b[l, pl.ds(hr, HEAD_DIM), pl.ds(q0, R)]
            dsum = jnp.sum(do_h.astype(F32) * o_h.astype(F32), axis=0, keepdims=True)
            lse = lse_b[l, pl.ds(h, 1), pl.ds(q0, R)]
            for kb in range(KB):
                ks = slice(kb * R, kb * R + R)
                s = mm(kv_b[l, 0, ks, :], qm)
                p = jnp.exp(s - lse)
                if kb >= 2 * r:
                    p = jnp.where(visible(r, kb - 2 * r, q0), p, 0.0)
                p_b[ks, :] = p.astype(BF)
                dp = mm(kv_b[l, 1, ks, :], dom)
                ds_b[ks, :] = (p * (dp - dsum)).astype(BF)
            dkv_acc[1, pl.ds(hr, HEAD_DIM), 0:KN] = dkv_acc[1, pl.ds(hr, HEAD_DIM), 0:KN] + mm(do_h, p_b[0:KN, :], NT)
            dkv_acc[0, pl.ds(hr, HEAD_DIM), 0:KN] = dkv_acc[0, pl.ds(hr, HEAD_DIM), 0:KN] + mm(q_h, ds_b[0:KN, :], NT)
            k_h = qkvT[l, pl.ds(pl.multiple_of(HP + hr, HEAD_DIM), HEAD_DIM), 0:KN]
            dq = mm(k_h, ds_b[0:KN, :]) * (HEAD_DIM ** -0.5)
            dqT_b[pl.ds(hr, HEAD_DIM), pl.ds(q0, R)] = dq.astype(BF)
            return cy

        lax.fori_loop(0, NH, head, 0)

    def da_tile(l, q0, dst):
        dqkv = dqT_b[:, pl.ds(q0, R)].astype(F32).T.astype(BF)

        def one(n):
            dst[:, n : n + 256] = mm(dqkv, wqkv[l, :, n : n + 256]).astype(dst.dtype)

        nblocks(one, NB)

    def att_bwd(l, r, tile_cp):
        do_tile(l, own(r))
        att_bwd_tile(l, r, own(r))
        tile_cp.wait_recv()
        do_tile(l, oth(r))
        att_bwd_tile(l, r, oth(r))
        cs = slice(CH * r, CH * r + CH)
        for j in range(2):
            dqT_b[HP * (j + 1) : HP * (j + 1) + HL, cs] = dkv_acc[j, 0:HL, cs].astype(BF)
        cp = send_partner(r, lambda ref: da_tile(l, oth(r), ref))
        da_tile(l, own(r), part)
        tile_cp.wait_send()
        combine(1, r, cp)

    def r1_copy(j, k):
        peer = do_ * NI + lax.rem(di + k, NI)
        return dp_remote(send1.at[j, k - 1], recv1.at[j, k - 1], r1s.at[j, k - 1], r1r.at[j, k - 1], peer)

    def r2_copy(j, k):
        peer = lax.rem(do_ + k, NO) * NI + di
        return dp_remote(send2.at[j, k - 1], recv2.at[j, k - 1], r2s.at[j, k - 1], r2r.at[j, k - 1], peer)

    def piece(q):
        return pl.ds(pl.multiple_of(q * PER, PER), PER)

    def rs_start(l, j):
        if not FUSED:
            cp = pltpu.make_async_copy(gstage, g_o.at[l, j], gsem.at[0])
            cp.start()
            cp.wait()
            return
        for k in range(1, NI):
            for oo in range(NO):
                send1[j, k - 1, oo * PER : oo * PER + PER, :] = gstage[piece(oo * NI + lax.rem(di + k, NI)), :].astype(BF)
            r1_copy(j, k).start()
        for oo in range(NO):
            own1[j, oo * PER : oo * PER + PER, :] = gstage[piece(oo * NI + di), :]

    def rs_mid(l, j):
        if not FUSED:
            return
        for k in range(1, NI):
            cp = r1_copy(j, k)
            cp.wait_send()
            cp.wait_recv()
        for kk in range(NO - 1, -1, -1):
            rows = piece(lax.rem(do_ + kk, NO))
            v = own1[j, rows, :]
            for k in range(1, NI):
                v = v + recv1[j, k - 1, rows, :].astype(F32)
            if kk == 0:
                own1[j, rows, :] = v
            else:
                send2[j, kk - 1] = v.astype(BF)
                r2_copy(j, kk).start()

    def rs_fin(l, j):
        if not FUSED:
            return
        v = own1[j, piece(do_), :]
        for kk in range(1, NO):
            cp = r2_copy(j, kk)
            cp.wait_send()
            cp.wait_recv()
            v = v + recv2[j, kk - 1].astype(F32)
        fstage[l, j] = v
        pltpu.make_async_copy(fstage.at[l, j], g_o.at[l, j], gsem.at[l * 3 + j]).start()

    def wgrad_ffn(l):
        for j, (lhs, rhs) in ((1, (a2_b.at[l], gp_b.at[l])), (2, (df_b, g_b.at[l]))):
            for n in range(NB):
                lt = lhs[:, n * 256 : n * 256 + 256].astype(F32).T.astype(BF)
                for f in range(FB):
                    gstage[n * 256 : n * 256 + 256, f * 256 : f * 256 + 256] = mm(lt, rhs[:, f * 256 : f * 256 + 256])
            rs_start(l, j)

    def wgrad_att(l):
        for n in range(NB):
            ns = slice(n * 256, n * 256 + 256)
            gtmp[0 : 3 * HL, :] = mm(dqT_b[...], a_b[l, :, ns])
            gtmp[3 * HL : 4 * HL, :] = mm(oT_b[l], dz_b[:, ns])
            gstage[ns, 0 : 4 * HL] = gtmp[...].T
        rs_start(l, 0)

    loc[1].wait()
    tcp[1].wait()
    for l in range(L - 1, -1, -1):
        for r in (1, 0):
            cp = enter_b1(l, r)
            if l == L - 1:
                finish_output(r)
            elif r == 0:
                rs_mid(l + 1, 0)
            ffn_bwd(l, r, cp)
        wgrad_ffn(l)
        if l < L - 1:
            rs_fin(l + 1, 0)
        dkv_acc[...] = jnp.zeros_like(dkv_acc)
        for r in (1, 0):
            cp = enter_b2(l, r)
            if r == 0:
                rs_mid(l, 1)
                rs_mid(l, 2)
            att_bwd(l, r, cp)
        wgrad_att(l)
        rs_fin(l, 1)
        rs_fin(l, 2)
    ocp = pltpu.make_async_copy(tokf.at[y], out_o, osem.at[0])
    ocp.start()
    for r in (1, 0):
        wait_y(1, r)

        def emit(i, dx, r=r):
            dh_b[r, pl.ds(i, BLK), :] = dh_b[r, pl.ds(i, BLK), :] + dx

        ln_bwd(0, r, 1, 0, h_b, emit)

        def blk(i, cy, r=r):
            return cy + jnp.sum(dh_b[r, pl.ds(i, BLK), :], axis=0, keepdims=True)

        v = rowloop(blk, jnp.zeros((1, D), F32))
        small[0, 6:7, :] = small[0, 6:7, :] + v
    gcp = pltpu.make_async_copy(dh_b.at[y], gtok_o, osem.at[1])
    gcp.start()
    scp = remote(small, smallr, ssem.at[0], ssem.at[1], cpeer)
    scp.start()
    rs_mid(0, 0)
    scp.wait()
    shared = lax.broadcasted_iota(jnp.int32, (8, D), 0) < 7
    for l in range(L):
        small[l] = small[l] + jnp.where(shared, smallr[l], 0.0)
    for k in range(D // 128):
        seqt[k : k + 1, :] = small[0, 6:7, k * 128 : k * 128 + 128]
    seqt[D // 128 : 8, :] = jnp.full((8 - D // 128, 128), ts_ref[0].astype(F32), F32)

    def seq_copy(k):
        return dp_remote(seqt, seqall.at[d], qsem_s.at[k], qsem_r.at[k], lax.rem(d + k, N))

    def seq_go(k, cy):
        seq_copy(k).start()
        return cy

    def seq_wait(k, cy):
        cp = seq_copy(k)
        cp.wait_send()
        cp.wait_recv()
        return cy

    lax.fori_loop(1, N, seq_go, 0)
    seqall[d] = seqt[...]

    def x1_copy(k):
        return dp_remote(small, smallx.at[k - 1], x1s.at[k - 1], x1r.at[k - 1], do_ * NI + lax.rem(di + k, NI))

    def x2_copy(k):
        return dp_remote(smallr, smallz.at[k - 1], x2s.at[k - 1], x2r.at[k - 1], lax.rem(do_ + k, NO) * NI + di)

    for k in range(1, NI):
        x1_copy(k).start()
    for k in range(1, NI):
        x1_copy(k).wait()
    for l in range(L):
        v = small[l]
        for k in range(1, NI):
            v = v + smallx[k - 1, l]
        smallr[l] = v
    for k in range(1, NO):
        x2_copy(k).start()
    rs_fin(0, 0)
    for k in range(1, NO):
        x2_copy(k).wait()
    for l in range(L):
        v = smallr[l]
        for k in range(1, NO):
            v = v + smallz[k - 1, l]
        small_o[l] = v
    lax.fori_loop(1, N, seq_wait, 0)
    seq_o[...] = seqall[...]
    ocp.wait()
    gcp.wait()
    if FUSED:
        for l in range(L):
            for j in range(3):
                pltpu.make_async_copy(fstage.at[l, j], g_o.at[l, j], gsem.at[l * 3 + j]).wait()


def finish_kernel(dim, out_i, gtok_i, small_i, seq_i, g_i, out_o, gtok_o, table_o, dg1, db1, gq, go, dbo, dg2, db2, gup, dbup, gdown, dbd):
    D, FL, HL, L, PER, N = dim["D"], dim["FL"], dim["HL"], dim["L"], dim["PER"], dim["N"]
    d = lax.axis_index("dp")
    out_o[...] = out_i[...]
    gtok_o[...] = gtok_i[...]
    turn = lax.rem(D - PER * d, D)
    for l in range(L):
        row = pltpu.roll(small_i[l], turn, 1)[:, 0:PER]
        for i, ref in enumerate((dg1, db1, dbo, dg2, db2, dbd)):
            ref[l : l + 1, :] = row[i : i + 1, :]
        dbup[l : l + 1, :] = row[7:8, :]
        ga = g_i[l, 0]
        for cc in range(3):
            gq[l, :, cc, :] = ga[:, cc * HL : cc * HL + HL]
        up = -PER % 128
        gt = jnp.concatenate([ga, jnp.zeros((up, 4 * HL), F32)], axis=0).T
        go[l] = gt[3 * HL : 4 * HL, 0:PER]
        gup[l] = g_i[l, 1]
        gt = jnp.concatenate([g_i[l, 2], jnp.zeros((up, FL), F32)], axis=0).T
        gdown[l] = gt[:, 0:PER]
    table_o[...] = jnp.zeros_like(table_o)
    rows = lax.broadcasted_iota(jnp.int32, (dim["TS"], PER), 0).astype(F32)

    def add(q, cy):
        seq = jnp.concatenate([seq_i[q, k : k + 1, :] for k in range(D // 128)], axis=1)
        cols = pltpu.roll(jnp.broadcast_to(seq, (8, D)), turn, 1)[0:1, 0:PER]
        step = seq_i[q, D // 128 : D // 128 + 1, 0:1]
        table_o[...] = table_o[...] + jnp.where(rows == step, cols, 0.0)
        return cy

    lax.fori_loop(0, N, add, 0)


def split_of(n):
    inner = 2 ** ((n.bit_length() - 1) // 2)
    return inner, n // inner


def run_step(ts, bs, vecs, bup, tok, cot, table, wqkv, wout, wup, wdown):
    R, D = tok.shape
    L, _, FL = wup.shape
    HL = wout.shape[1]
    N = lax.axis_size("dp")
    NI, NO = split_of(N)
    PER = D // N
    FUSED = PER % 16 == 0
    assert lax.axis_size("tensor") == 4 and ts.shape[0] == 1 and FL == D == 4 * HL and D // 128 < 8
    T = 4 * R
    dim = dict(D=D, FL=FL, HL=HL, R=R, L=L, N=N, NI=NI, NO=NO, PER=PER, FUSED=FUSED, TS=table.shape[0])
    vm = pl.BlockSpec(memory_space=pltpu.VMEM)
    sm = pl.BlockSpec(memory_space=pltpu.SMEM)
    any_ = pl.BlockSpec(memory_space=pl.ANY)
    dma = pltpu.SemaphoreType.DMA
    V = pltpu.VMEM
    J = 3 if FUSED else 1
    PR = PER if FUSED else 16
    ones = max(NI - 1, 1)
    outs = max(NO - 1, 1)
    kept = (L, 3, PER, FL) if FUSED else (L, 3, D, FL)
    return dim, pl.pallas_call(
        functools.partial(step_kernel, dim),
        out_shape=(
            jax.ShapeDtypeStruct((R, D), BF),
            jax.ShapeDtypeStruct((R, D), F32),
            jax.ShapeDtypeStruct((L, 8, D), F32),
            jax.ShapeDtypeStruct((N, 8, 128), F32),
            jax.ShapeDtypeStruct(kept, F32),
        ),
        in_specs=[sm, sm] + [vm] * 7 + [any_] * 7,
        out_specs=(any_, any_, vm, vm, any_),
        scratch_shapes=[
            V((L, 3 * HL, D), BF), V((L, HL, D), BF), V((L, D, FL), BF), V((L, FL, D), BF),
            V((2, R, D), BF), V((2, R, D), BF),
            V((L, T, D), BF), V((L, T, D), BF), V((L, T, FL), BF), V((L, T, FL), BF),
            V((L, 3 * HL, T), BF), V((L, 2, T, HL), BF), V((L, HL, T), BF), V((L, 8, T), F32),
            V((L, 2, R, D), F32), V((L, 2, R, D), F32),
            V((T, D), BF), V((T, D), BF), V((2, R, D), F32),
            V((HL, T), BF), V((3 * HL, T), BF), V((2, HL, T), F32),
            V((2, 2, R, D), BF), V((2, 2, R, D), BF), V((2, R, D), BF), V((2, R, D), BF),
            V((R, D), F32), V((T, R), F32), V((T, R), BF), V((T, R), BF), V((4 * HL, 256), F32), V((D, FL), F32),
            V((L, 8, D), F32), V((L, 8, D), F32), V((ones, L, 8, D), F32), V((outs, L, 8, D), F32),
            V((8, 128), F32), V((N, 8, 128), F32), V((8, D), F32),
            V((J, ones, NO * PR, FL), BF), V((J, ones, NO * PR, FL), BF), V((J, NO * PR, FL), F32),
            V((J, outs, PR, FL), BF), V((J, outs, PR, FL), BF), V((L, J, PR, FL), F32),
            dma((L, 4)), dma((2,)), dma((2,)), dma((2, 2)), dma((2, 2)),
            dma((2,)), dma((2,)), dma((2,)), dma((2,)),
            dma((3,)), dma((2,)), dma((3 * L,)), dma((2,)), dma((N,)), dma((N,)),
            dma((ones,)), dma((ones,)), dma((outs,)), dma((outs,)),
            dma((3, ones)), dma((3, ones)), dma((3, outs)), dma((3, outs)),
        ],
        compiler_params=pltpu.CompilerParams(
            collective_id=0, has_side_effects=True, vmem_limit_bytes=67043328),
        name="layers",
    )(ts, bs, *vecs, bup, tok, cot, table, wqkv, wout, wup, wdown)


def local(tokens, timestep, block_size, table, ln1_gain, ln1_bias, w_qkv, w_out, b_out,
          ln2_gain, ln2_bias, w_up, b_up, w_down, b_down, cotangent):
    L, D, _, HL = w_qkv.shape
    wq = jnp.transpose(w_qkv, (0, 2, 3, 1)).reshape(L, 3 * HL, D)
    vecs = (ln1_gain, ln1_bias, b_out, ln2_gain, ln2_bias, b_down)
    dim, (out, gtok, small, seq, g) = run_step(
        timestep, block_size, vecs, b_up, tokens, cotangent, table, wq, w_out, w_up, w_down)
    PER, FL, TS = dim["PER"], dim["FL"], dim["TS"]
    if not dim["FUSED"]:
        g = lax.psum_scatter(g, "dp", scatter_dimension=2, tiled=True)
    vec = jax.ShapeDtypeStruct((L, PER), F32)
    vm = pl.BlockSpec(memory_space=pltpu.VMEM)
    return pl.pallas_call(
        functools.partial(finish_kernel, dim),
        out_shape=(
            jax.ShapeDtypeStruct(out.shape, BF), jax.ShapeDtypeStruct(gtok.shape, F32),
            jax.ShapeDtypeStruct((TS, PER), F32), vec, vec,
            jax.ShapeDtypeStruct((L, PER, 3, HL), F32), jax.ShapeDtypeStruct((L, HL, PER), F32),
            vec, vec, vec, jax.ShapeDtypeStruct((L, PER, FL), F32), vec,
            jax.ShapeDtypeStruct((L, FL, PER), F32), vec),
        in_specs=[vm] * 5,
        out_specs=(vm,) * 14,
        name="finish",
    )(out, gtok, small, seq, g)


def solution(mesh):
    placed = (
        P(("dp", "tensor"), None), P("dp"), P("dp"), P(), P(), P(),
        P(None, None, None, "tensor"), P(None, "tensor", None), P(), P(), P(),
        P(None, None, "tensor"), P(None, "tensor"), P(None, "tensor", None), P(),
        P(("dp", "tensor"), None),
    )
    return jax.shard_map(
        local,
        mesh=mesh,
        in_specs=placed,
        out_specs=(
            P(("dp", "tensor"), None), P(("dp", "tensor"), None), P(None, "dp"), P(None, "dp"), P(None, "dp"),
            P(None, "dp", None, "tensor"), P(None, "tensor", "dp"), P(None, "dp"), P(None, "dp"), P(None, "dp"),
            P(None, "dp", "tensor"), P(None, ("tensor", "dp")), P(None, "tensor", "dp"), P(None, "dp"),
        ),
        check_vma=False,
    )
```

```python
import functools

import jax
import jax.numpy as jnp
from jax import lax
from jax.experimental import pallas as pl
from jax.experimental.pallas import tpu as pltpu
from jax.sharding import PartitionSpec as P

HEAD_DIM = 64
EPSILON = 1e-05
NEGATIVE = -1e30
MESH = pl.DeviceIdType.MESH
BF = jnp.bfloat16
F32 = jnp.float32
INV_SQRT2 = 0.7071067811865476
INV_SQRT2PI = 0.3989422804014327

NN = (((1,), (0,)), ((), ()))
NT = (((1,), (1,)), ((), ()))
TN = (((0,), (0,)), ((), ()))


def mm(a, b, dims=NN):
    return lax.dot_general(a, b, dims, preferred_element_type=F32)


def step_kernel(dim, *refs):
    (
        ts_ref, bs_ref, g1_in, b1_in, bo_in, g2_in, b2_in, bd_in, bup_in,
        tok_in, cot_in, table_h, wqkv_h, wout_h, wup_h, wdown_h,
        out_o, gtok_o, smallx_o, g_o,
        wqkv, wout, wup, wdown, tokf, cotf,
        a_b, a2_b, g_b, gp_b, qkvT, kv_b, oT_b, lse_b, h_b, m_b,
        df_b, dz_b, dh_b, doT_b, dqT_b, dkv_acc,
        ysend, yrecv, csend, crecv, part, s_b, p_b, ds_b, gstage,
        small, smallr, smallx, smallp, emb_b,
        send1, recv1, own1, send2, recv2, fstage,
        wsem, tsem_s, tsem_r, ysem_s, ysem_r, casem_s, casem_r, cpsem_s, cpsem_r,
        lsem, osem, gsem, ssem, x1s, x1r,
        r1s, r1r, r2s, r2r,
    ) = refs
    D, FL, HL, R, L = dim["D"], dim["FL"], dim["HL"], dim["R"], dim["L"]
    N, NI, NO, PER, FUSED = dim["N"], dim["NI"], dim["NO"], dim["PER"], dim["FUSED"]
    HP = HL
    vecs = (g1_in, b1_in, bo_in, g2_in, b2_in, bd_in)

    def vrow(i, l):
        return vecs[i][l : l + 1, :].astype(F32)

    T = 4 * R
    NH = HL // HEAD_DIM
    CH = 2 * R
    NB = D // 256
    FB = FL // 256
    t = lax.axis_index("tensor")
    d = lax.axis_index("dp")
    di = lax.rem(d, NI)
    do_ = lax.div(d, NI)
    y = lax.div(t, 2)
    c = lax.rem(t, 2)
    ypeer = lax.rem(t + 2, 4)
    cpeer = t + 1 - 2 * c

    def own(r):
        return pl.multiple_of(R * (2 * r + c), R)

    def oth(r):
        return pl.multiple_of(R * (2 * r + 1 - c), R)

    def remote(src, dst, ss, rs, peer):
        return pltpu.make_async_remote_copy(
            src_ref=src, dst_ref=dst, send_sem=ss, recv_sem=rs,
            device_id={"tensor": peer}, device_id_type=MESH)

    def dp_remote(src, dst, ss, rs, peer):
        return pltpu.make_async_remote_copy(
            src_ref=src, dst_ref=dst, send_sem=ss, recv_sem=rs,
            device_id={"dp": peer}, device_id_type=MESH)

    bar = pltpu.get_barrier_semaphore()

    def greet(k, cy):
        pl.semaphore_signal(bar, inc=1, device_id={"dp": lax.rem(d + k, N)}, device_id_type=MESH)
        return cy

    lax.fori_loop(1, N, greet, 0)
    pl.semaphore_signal(bar, inc=1, device_id={"tensor": ypeer}, device_id_type=MESH)
    pl.semaphore_signal(bar, inc=1, device_id={"tensor": cpeer}, device_id_type=MESH)

    loc = [pltpu.make_async_copy(tok_in, tokf.at[y], lsem.at[0]),
           pltpu.make_async_copy(cot_in, cotf.at[y], lsem.at[1]),
           pltpu.make_async_copy(table_h, df_b.at[pl.ds(0, dim["TS"]), :], lsem.at[2])]
    for cp in loc:
        cp.start()
    wcopies = []
    for l in range(L):
        row = []
        for i, (src, dst) in enumerate(((wqkv_h, wqkv), (wout_h, wout), (wup_h, wup), (wdown_h, wdown))):
            cp = pltpu.make_async_copy(src.at[l], dst.at[l], wsem.at[l, i])
            cp.start()
            row.append(cp)
        wcopies.append(row)
    pl.semaphore_wait(bar, N + 1)
    tcp = [remote(tok_in, tokf.at[y], tsem_s.at[0], tsem_r.at[0], ypeer),
           remote(cot_in, cotf.at[y], tsem_s.at[1], tsem_r.at[1], ypeer)]
    tcp[0].start()

    small[...] = jnp.zeros_like(small)
    bs = bs_ref[0]
    loc[2].wait()
    pick = (lax.broadcasted_iota(jnp.int32, (8, dim["TS"]), 1) == ts_ref[0]).astype(BF)
    emb_b[...] = mm(pick, df_b[0 : dim["TS"], :])

    def y_copy(par, r):
        return remote(ysend.at[par, r], yrecv.at[par, r], ysem_s.at[par, r], ysem_r.at[par, r], ypeer)

    def tile_copy(buf, r):
        return remote(buf.at[pl.ds(own(r), R), :], buf.at[pl.ds(own(r), R), :],
                      casem_s.at[r], casem_r.at[r], cpeer)

    def part_copy(r):
        return remote(csend.at[r], crecv.at[r], cpsem_s.at[r], cpsem_r.at[r], cpeer)

    BLK = dim["BLK"]

    def rowloop(fn, init=0):
        return lax.fori_loop(0, R // BLK, lambda i, cy: fn(pl.multiple_of(i * BLK, BLK), cy), init)

    def ln_stats(x):
        mean = jnp.sum(x, axis=-1, keepdims=True) * (1.0 / D)
        xc = x - mean
        var = jnp.sum(xc * xc, axis=-1, keepdims=True) * (1.0 / D)
        return xc, lax.rsqrt(var + EPSILON)

    def enter_fwd(l, r, src, gi, dst_h, dst_a):
        gain = vrow(gi, l)
        bias = vrow(gi + 1, l)

        def blk(i, cy):
            x = src(i)
            dst_h[l, r, pl.ds(i, BLK), :] = x
            xc, rstd = ln_stats(x)
            dst_a[l, pl.ds(pl.multiple_of(own(r) + i, BLK), BLK), :] = (xc * rstd * gain + bias).astype(BF)
            return cy

        rowloop(blk)
        cp = tile_copy(dst_a.at[l], r)
        cp.start()
        return cp

    def ysum(par, r, i):
        return ysend[par, r, pl.ds(i, BLK), :].astype(F32) + yrecv[par, r, pl.ds(i, BLK), :].astype(F32)

    def wait_y(par, r):
        cp = y_copy(par, r)
        cp.wait_send()
        cp.wait_recv()

    def send_partner(r, fill):
        fill(csend.at[r])
        cp = part_copy(r)
        cp.start()
        return cp

    def combine(par, r, cp):
        cp.wait_recv()

        def blk(i, cy):
            v = part[pl.ds(i, BLK), :] + crecv[r, pl.ds(i, BLK), :].astype(F32)
            ysend[par, r, pl.ds(i, BLK), :] = v.astype(BF)
            return cy

        rowloop(blk)
        cp.wait_send()
        y_copy(par, r).start()

    def qkv_tile(l, q0):
        q = mm(wqkv[l, 0:HP, :], a_b[l, pl.ds(q0, R), :], NT).astype(BF)
        qkvT[l, 0:HP, pl.ds(q0, R)] = q * jnp.asarray(HEAD_DIM ** -0.5, BF)
        for cc in (1, 2):
            v = mm(wqkv[l, cc * HP : cc * HP + HP, :], a_b[l, pl.ds(q0, R), :], NT)
            qkvT[l, cc * HP : cc * HP + HP, pl.ds(q0, R)] = v.astype(BF)
            kv_b[l, cc - 1, pl.ds(q0, R), :] = v.T.astype(BF)

    def hmask(h):
        rows = lax.broadcasted_iota(jnp.int32, (HP, R), 0)
        return (rows >= h * HEAD_DIM) & (rows < (h + 1) * HEAD_DIM)

    def visible(r, kb, q0):
        key = lax.broadcasted_iota(jnp.int32, (R, R), 0) + (CH * r + kb * R)
        qry = lax.broadcasted_iota(jnp.int32, (R, R), 1) + q0
        return key <= (qry | (bs - 1))

    def att_fwd_tile(l, r, q0):
        KB = 2 * (r + 1)

        def head(h, cy):
            qm = jnp.where(hmask(h), qkvT[l, 0:HP, pl.ds(q0, R)].astype(F32), 0.0).astype(BF)
            top = None
            for kb in range(KB):
                s = mm(kv_b[l, 0, kb * R : kb * R + R, :], qm)
                if kb >= 2 * r:
                    s = jnp.where(visible(r, kb - 2 * r, q0), s, NEGATIVE)
                s_b[kb * R : kb * R + R, :] = s
                mx = jnp.max(s, axis=0, keepdims=True)
                top = mx if top is None else jnp.maximum(top, mx)
            tot = None
            for kb in range(KB):
                e = jnp.exp(s_b[kb * R : kb * R + R, :] - top)
                p_b[kb * R : kb * R + R, :] = e.astype(BF)
                sm = jnp.sum(e, axis=0, keepdims=True)
                tot = sm if tot is None else tot + sm
            hr = pl.multiple_of(h * HEAD_DIM, HEAD_DIM)
            o = mm(qkvT[l, pl.ds(pl.multiple_of(2 * HP + hr, HEAD_DIM), HEAD_DIM), 0 : KB * R], p_b[0 : KB * R, :])
            oT_b[l, pl.ds(hr, HEAD_DIM), pl.ds(q0, R)] = (o * (1.0 / tot)).astype(BF)
            lse_b[l, pl.ds(h, 1), pl.ds(q0, R)] = top + jnp.log(tot)
            return cy

        lax.fori_loop(0, NH, head, 0)

    def nblocks(fn, n):
        for i in range(n):
            fn(i * 256)

    def out_tile(l, q0, dst):
        o = oT_b[l, :, pl.ds(q0, R)].astype(F32).T.astype(BF)

        def one(n):
            dst[:, n : n + 256] = mm(o, wout[l, :, n : n + 256]).astype(dst.dtype)

        nblocks(one, NB)

    def up_tile(l, q0):
        def one(n, cy):
            n = pl.multiple_of(n * 256, 256)
            u = mm(a2_b[l, pl.ds(q0, R), :], wup[l, :, pl.ds(n, 256)]) + bup_in[l : l + 1, pl.ds(n, 256)].astype(F32)
            phi = 0.5 * (1.0 + lax.erf(u * INV_SQRT2))
            g_b[l, pl.ds(q0, R), pl.ds(n, 256)] = (u * phi).astype(BF)
            gp = phi + u * (jnp.exp(u * u * -0.5) * INV_SQRT2PI)
            gp_b[l, pl.ds(q0, R), pl.ds(n, 256)] = gp.astype(BF)
            return cy

        lax.fori_loop(0, FB, one, 0)

    def down_tile(l, q0, dst):
        def one(n):
            dst[:, n : n + 256] = mm(g_b[l, pl.ds(q0, R), :], wdown[l, :, n : n + 256]).astype(dst.dtype)

        nblocks(one, NB)

    def own_first(r, tile_cp, fn):
        def tile(i, cy):
            @pl.when(i == 1)
            def _():
                tile_cp.wait_recv()

            fn(pl.multiple_of(R * (2 * r + c + i * (1 - 2 * c)), R))
            return cy

        lax.fori_loop(0, 2, tile, 0)

    def att_fwd(l, r, tile_cp):
        own_first(r, tile_cp, lambda q0: qkv_tile(l, q0))
        cp = part_copy(r)

        def tile(i, cy):
            att_fwd_tile(l, r, pl.multiple_of(R * (2 * r + 1 - c + i * (2 * c - 1)), R))

            @pl.when(i == 0)
            def _():
                out_tile(l, oth(r), csend.at[r])
                cp.start()

            return cy

        lax.fori_loop(0, 2, tile, 0)
        out_tile(l, own(r), part)
        tile_cp.wait_send()
        combine(0, r, cp)

    def ffn_fwd(l, r, tile_cp):
        own_first(r, tile_cp, lambda q0: up_tile(l, q0))
        cp = send_partner(r, lambda ref: down_tile(l, oth(r), ref))
        down_tile(l, own(r), part)
        tile_cp.wait_send()
        combine(1, r, cp)

    for l in range(L):
        for r in range(2):
            if l == 0:
                if r == 0:
                    for cp in (loc[0], wcopies[0][0]):
                        cp.wait()
                    tcp[0].wait()
                    tcp[1].start()
                src = lambda i, r=r: tokf[r, pl.ds(i, BLK), :].astype(F32) + emb_b[0:1, :]
            else:
                wait_y(1, r)
                bd = vrow(5, l - 1)
                src = lambda i, r=r, l=l, bd=bd: m_b[l - 1, r, pl.ds(i, BLK), :] + (ysum(1, r, i) + bd)
            if r == 0 and l > 0:
                wcopies[l][0].wait()
            cp = enter_fwd(l, r, src, 0, h_b, a_b)
            if r == 0:
                wcopies[l][1].wait()
            att_fwd(l, r, cp)
        for r in range(2):
            wait_y(0, r)
            bo = vrow(2, l)
            src = lambda i, r=r, l=l, bo=bo: h_b[l, r, pl.ds(i, BLK), :] + (ysum(0, r, i) + bo)
            if r == 0:
                wcopies[l][2].wait()
                wcopies[l][3].wait()
            cp = enter_fwd(l, r, src, 3, m_b, a2_b)
            ffn_fwd(l, r, cp)

    def finish_output(r):
        wait_y(1, r)
        bd = vrow(5, L - 1)

        def blk(i, cy):
            v = m_b[L - 1, r, pl.ds(i, BLK), :] + (ysum(1, r, i) + bd)
            tokf[r, pl.ds(i, BLK), :] = v.astype(BF)
            return cy

        rowloop(blk)

    def ln_bwd(l, r, par, gi, xbuf, emit):
        gain = vrow(gi, l)

        def blk(i, cy):
            dg, db = cy
            x = xbuf[l, r, pl.ds(i, BLK), :]
            dy = ysum(par, r, i)
            xc, rstd = ln_stats(x)
            xh = xc * rstd
            t1 = dy * gain
            m1 = jnp.sum(t1, axis=-1, keepdims=True) * (1.0 / D)
            m2 = jnp.sum(t1 * xh, axis=-1, keepdims=True) * (1.0 / D)
            dx = rstd * (t1 - m1 - xh * m2)
            emit(i, dx)
            dg = dg + jnp.sum(dy * xh, axis=0, keepdims=True)
            db = db + jnp.sum(dy, axis=0, keepdims=True)
            return (dg, db)

        z = jnp.zeros((1, D), F32)
        dg, db = rowloop(blk, (z, z))
        small[l, gi : gi + 1, :] = small[l, gi : gi + 1, :] + dg
        small[l, gi + 1 : gi + 2, :] = small[l, gi + 1 : gi + 2, :] + db

    def colsum_own(buf, r, l, row):
        def blk(i, cy):
            return cy + jnp.sum(buf[pl.ds(pl.multiple_of(own(r) + i, BLK), BLK), :].astype(F32), axis=0, keepdims=True)

        v = rowloop(blk, jnp.zeros((1, D), F32))
        small[l, row : row + 1, :] = small[l, row : row + 1, :] + v

    def enter_b1(l, r):
        if l == L - 1:
            def blk(i, cy):
                v = cotf[r, pl.ds(i, BLK), :]
                dh_b[r, pl.ds(i, BLK), :] = v.astype(F32)
                df_b[pl.ds(pl.multiple_of(own(r) + i, BLK), BLK), :] = v
                return cy

            rowloop(blk)
        else:
            wait_y(0, r)

            def emit(i, dx):
                v = dh_b[r, pl.ds(i, BLK), :] + dx
                dh_b[r, pl.ds(i, BLK), :] = v
                df_b[pl.ds(pl.multiple_of(own(r) + i, BLK), BLK), :] = v.astype(BF)

            ln_bwd(l + 1, r, 0, 0, h_b, emit)
        cp = tile_copy(df_b, r)
        cp.start()
        colsum_own(df_b, r, l, 5)
        return cp

    def du_tile(l, q0):
        def one(n, cy):
            n = pl.multiple_of(n * 256, 256)
            dg = mm(df_b[pl.ds(q0, R), :], wdown[l, pl.ds(n, 256), :], NT)
            du = (dg * gp_b[l, pl.ds(q0, R), pl.ds(n, 256)].astype(F32)).astype(BF)
            gp_b[l, pl.ds(q0, R), pl.ds(n, 256)] = du
            small[l, 7:8, pl.ds(n, 256)] = small[l, 7:8, pl.ds(n, 256)] + jnp.sum(du.astype(F32), axis=0, keepdims=True)
            return cy

        lax.fori_loop(0, FB, one, 0)

    def da2_tile(l, q0, dst):
        def one(n):
            dst[:, n : n + 256] = mm(gp_b[l, pl.ds(q0, R), :], wup[l, n : n + 256, :], NT).astype(dst.dtype)

        nblocks(one, NB)

    def ffn_bwd(l, r, tile_cp):
        own_first(r, tile_cp, lambda q0: du_tile(l, q0))
        cp = send_partner(r, lambda ref: da2_tile(l, oth(r), ref))
        da2_tile(l, own(r), part)
        tile_cp.wait_send()
        combine(2, r, cp)

    def enter_b2(l, r):
        wait_y(2, r)

        def emit(i, dx):
            v = dh_b[r, pl.ds(i, BLK), :] + dx
            dh_b[r, pl.ds(i, BLK), :] = v
            dz_b[pl.ds(pl.multiple_of(own(r) + i, BLK), BLK), :] = v.astype(BF)

        ln_bwd(l, r, 2, 3, m_b, emit)
        cp = tile_copy(dz_b, r)
        cp.start()
        colsum_own(dz_b, r, l, 2)
        return cp

    def do_tile(l, q0):
        doT_b[:, pl.ds(q0, R)] = mm(wout[l], dz_b[pl.ds(q0, R), :], NT).astype(BF)

    def att_bwd_tile(l, r, q0):
        KB = 2 * (r + 1)
        KN = KB * R

        def head(h, cy):
            hr = pl.multiple_of(h * HEAD_DIM, HEAD_DIM)
            hm = hmask(h)
            qm = jnp.where(hm, qkvT[l, 0:HP, pl.ds(q0, R)].astype(F32), 0.0).astype(BF)
            dom = jnp.where(hm, doT_b[:, pl.ds(q0, R)].astype(F32), 0.0).astype(BF)
            do_h = doT_b[pl.ds(hr, HEAD_DIM), pl.ds(q0, R)]
            q_h = qkvT[l, pl.ds(hr, HEAD_DIM), pl.ds(q0, R)]
            o_h = oT_b[l, pl.ds(hr, HEAD_DIM), pl.ds(q0, R)]
            dsum = jnp.sum(do_h.astype(F32) * o_h.astype(F32), axis=0, keepdims=True)
            lse = lse_b[l, pl.ds(h, 1), pl.ds(q0, R)]
            for kb in range(KB):
                ks = slice(kb * R, kb * R + R)
                s = mm(kv_b[l, 0, ks, :], qm)
                p = jnp.exp(s - lse)
                if kb >= 2 * r:
                    p = jnp.where(visible(r, kb - 2 * r, q0), p, 0.0)
                p_b[ks, :] = p.astype(BF)
                dp = mm(kv_b[l, 1, ks, :], dom)
                ds_b[ks, :] = (p * (dp - dsum)).astype(BF)
            dkv_acc[1, pl.ds(hr, HEAD_DIM), 0:KN] = dkv_acc[1, pl.ds(hr, HEAD_DIM), 0:KN] + mm(do_h, p_b[0:KN, :], NT)
            dkv_acc[0, pl.ds(hr, HEAD_DIM), 0:KN] = dkv_acc[0, pl.ds(hr, HEAD_DIM), 0:KN] + mm(q_h, ds_b[0:KN, :], NT)
            k_h = qkvT[l, pl.ds(pl.multiple_of(HP + hr, HEAD_DIM), HEAD_DIM), 0:KN]
            dq = mm(k_h, ds_b[0:KN, :]) * (HEAD_DIM ** -0.5)
            dqT_b[pl.ds(hr, HEAD_DIM), pl.ds(q0, R)] = dq.astype(BF)
            return cy

        lax.fori_loop(0, NH, head, 0)

    def da_tile(l, q0, dst):
        dqkv = dqT_b[:, pl.ds(q0, R)].astype(F32).T.astype(BF)

        def one(n):
            dst[:, n : n + 256] = mm(dqkv, wqkv[l, :, n : n + 256]).astype(dst.dtype)

        nblocks(one, NB)

    def att_bwd(l, r, tile_cp):
        def both(q0):
            do_tile(l, q0)
            att_bwd_tile(l, r, q0)

        own_first(r, tile_cp, both)
        cs = slice(CH * r, CH * r + CH)
        for j in range(2):
            dqT_b[HP * (j + 1) : HP * (j + 1) + HL, cs] = dkv_acc[j, 0:HL, cs].astype(BF)
        cp = send_partner(r, lambda ref: da_tile(l, oth(r), ref))
        da_tile(l, own(r), part)
        tile_cp.wait_send()
        combine(0, r, cp)

    WHOLE = (0, FL, None)
    HALF = ((0, FL // 2, None), (FL // 2, FL - FL // 2, 3))

    def r1_copy(j, k, span):
        c0, w, extra = span
        q = j if extra is None else extra
        peer = do_ * NI + lax.rem(di + k, NI)
        return dp_remote(send1.at[j, k - 1, :, c0 : c0 + w], recv1.at[j, k - 1, :, c0 : c0 + w],
                         r1s.at[q, k - 1], r1r.at[q, k - 1], peer)

    def r2_copy(j, k, span):
        c0, w, extra = span
        q = j if extra is None else extra
        peer = lax.rem(do_ + k, NO) * NI + di
        return dp_remote(send2.at[j, k - 1, :, c0 : c0 + w], recv2.at[j, k - 1, :, c0 : c0 + w],
                         r2s.at[q, k - 1], r2r.at[q, k - 1], peer)

    def g_copy(l, j, span):
        c0, w, extra = span
        q = l * 3 + j if extra is None else 3 * L
        return pltpu.make_async_copy(fstage.at[l, j, :, c0 : c0 + w], g_o.at[l, j, :, c0 : c0 + w], gsem.at[q])

    def piece(q):
        return pl.ds(pl.multiple_of(q * PER, PER), PER)

    def rs_start(l, j, span=WHOLE):
        c0, w, _ = span
        cols = slice(c0, c0 + w)
        if not FUSED:
            cp = pltpu.make_async_copy(gstage.at[:, cols], g_o.at[l, j, :, cols], gsem.at[0])
            cp.start()
            cp.wait()
            return
        for k in range(1, NI):
            for oo in range(NO):
                send1[j, k - 1, oo * PER : oo * PER + PER, cols] = gstage[piece(oo * NI + lax.rem(di + k, NI)), cols].astype(BF)
            r1_copy(j, k, span).start()
        for oo in range(NO):
            own1[j, oo * PER : oo * PER + PER, cols] = gstage[piece(oo * NI + di), cols]

    def rs_mid(l, j, span=WHOLE):
        c0, w, _ = span
        cols = slice(c0, c0 + w)
        if not FUSED:
            return
        for k in range(1, NI):
            cp = r1_copy(j, k, span)
            cp.wait_send()
            cp.wait_recv()
        for kk in range(NO - 1, -1, -1):
            rows = piece(lax.rem(do_ + kk, NO))
            v = own1[j, rows, cols]
            for k in range(1, NI):
                v = v + recv1[j, k - 1, rows, cols].astype(F32)
            if kk == 0:
                own1[j, rows, cols] = v
            else:
                send2[j, kk - 1, :, cols] = v.astype(BF)
                r2_copy(j, kk, span).start()

    def rs_fin(l, j, span=WHOLE):
        c0, w, _ = span
        cols = slice(c0, c0 + w)
        if not FUSED:
            return
        v = own1[j, piece(do_), cols]
        for kk in range(1, NO):
            cp = r2_copy(j, kk, span)
            cp.wait_send()
            cp.wait_recv()
            v = v + recv2[j, kk - 1, :, cols].astype(F32)
        fstage[l, j, :, cols] = v
        g_copy(l, j, span).start()

    def wgrad_ffn(l, j, lhs, rhs):
        def one(n, cy):
            ns = pl.ds(pl.multiple_of(n * 256, 256), 256)
            lt = lhs[:, ns].astype(F32).T.astype(BF)
            for f in range(FB):
                gstage[ns, f * 256 : f * 256 + 256] = mm(lt, rhs[:, f * 256 : f * 256 + 256])
            return cy

        lax.fori_loop(0, NB, one, 0)

    def wgrad_att(l, span):
        lo, hi = span[0], span[0] + span[1]
        q = min(hi, 3 * HL)

        def one(n, cy):
            ns = pl.ds(pl.multiple_of(n * 256, 256), 256)
            s_b[lo:q, :] = mm(dqT_b[lo:q, :], a_b[l, :, ns])
            if hi > q:
                s_b[q:hi, :] = mm(oT_b[l], dz_b[:, ns])
            gstage[ns, lo:hi] = s_b[lo:hi, :].T
            return cy

        lax.fori_loop(0, NB, one, 0)

    loc[1].wait()
    tcp[1].wait()
    for l in range(L - 1, -1, -1):
        last = l == L - 1
        if last:
            cps = {r: enter_b1(l, r) for r in (1, 0)}
        for r in (1, 0):
            cp = cps[r] if last else enter_b1(l, r)
            ffn_bwd(l, r, cp)
            if not last:
                rs_fin(l + 1, 1 + r)
        if last:
            for r in (1, 0):
                finish_output(r)
        else:
            rs_mid(l + 1, 0)
        wgrad_ffn(l, 2, df_b, g_b.at[l])
        rs_start(l, 2)
        wgrad_ffn(l, 1, a2_b.at[l], gp_b.at[l])
        rs_start(l, 1)
        dkv_acc[...] = jnp.zeros_like(dkv_acc)
        for r in (1, 0):
            cp = enter_b2(l, r)
            att_bwd(l, r, cp)
            if r == 1:
                if not last:
                    rs_fin(l + 1, 0)
                rs_mid(l, 2)
        if l > 0:
            wgrad_att(l, WHOLE)
            rs_mid(l, 1)
            rs_start(l, 0)
        else:
            wgrad_att(l, HALF[0])
            rs_mid(l, 1)
            rs_start(l, 0, HALF[0])
            wgrad_att(l, HALF[1])
            rs_start(l, 0, HALF[1])
    ocp = pltpu.make_async_copy(tokf.at[y], out_o, osem.at[0])
    ocp.start()
    rs_fin(0, 2)
    for r in (1, 0):
        wait_y(0, r)

        def emit(i, dx, r=r):
            v = dh_b[r, pl.ds(i, BLK), :] + dx
            dh_b[r, pl.ds(i, BLK), :] = v
            small[0, 6:7, :] = small[0, 6:7, :] + jnp.sum(v, axis=0, keepdims=True)

        ln_bwd(0, r, 0, 0, h_b, emit)
        if r == 1:
            rs_mid(0, 0, HALF[0])
    gcp = pltpu.make_async_copy(dh_b.at[y], gtok_o, osem.at[1])
    gcp.start()
    scp = remote(small, smallr, ssem.at[0], ssem.at[1], cpeer)
    scp.start()
    rs_fin(0, 1)
    scp.wait()
    shared = lax.broadcasted_iota(jnp.int32, (8, D), 0) < 7
    for l in range(L):
        small[l] = small[l] + jnp.where(shared, smallr[l], 0.0)
    small[1, 6:7, :] = jnp.full((1, D), ts_ref[0].astype(F32), F32)

    def x_copy(k):
        return dp_remote(smallp.at[k], smallx.at[d], x1s.at[k], x1r.at[k], lax.rem(d + k, N))

    def columns(k):
        turn = lax.rem(D - PER * lax.rem(d + k, N), D)
        return [pltpu.roll(small[l], turn, 1)[:, 0 : smallx.shape[3]] for l in range(L)]

    def x_go(k, cy):
        for l, v in enumerate(columns(k)):
            smallp[k, l] = v
        x_copy(k).start()
        return cy

    def x_wait(k, cy):
        cp = x_copy(k)
        cp.wait_send()
        cp.wait_recv()
        return cy

    lax.fori_loop(1, N, x_go, 0)
    for l, v in enumerate(columns(0)):
        smallx[d, l] = v
    rs_mid(0, 0, HALF[1])
    rs_fin(0, 0, HALF[0])
    lax.fori_loop(1, N, x_wait, 0)
    smallx_o[...] = smallx[...]
    rs_fin(0, 0, HALF[1])
    ocp.wait()
    gcp.wait()
    if FUSED:
        for l in range(L):
            for j in range(3):
                for span in HALF if l == 0 and j == 0 else (WHOLE,):
                    g_copy(l, j, span).wait()


def finish_kernel(dim, out_i, gtok_i, sx, g_i, out_o, gtok_o, table_o, dg1, db1, gq, go, dbo, dg2, db2, gup, dbup, gdown, dbd,
                  g_b, out_b, gtok_b, rows_b, sem_i, sem_o):
    FL, HL, L, PER, N, TS = dim["FL"], dim["HL"], dim["L"], dim["PER"], dim["N"], dim["TS"]
    ins = []
    for j in range(3):
        for l in range(L):
            ins.append(pltpu.make_async_copy(g_i.at[l, j], g_b.at[l, j], sem_i.at[l * 3 + j]))
    order = ((out_i, out_b, out_o), (gtok_i, gtok_b, gtok_o))
    for i, (src, buf, _) in enumerate(order):
        ins.append(pltpu.make_async_copy(src, buf, sem_i.at[3 * L + i]))
    for cp in ins:
        cp.start()
    for l in range(L):
        tot = sx[0, l]
        for q in range(1, N):
            tot = tot + sx[q, l]
        for i, ref in enumerate((dg1, db1, dbo, dg2, db2, dbd)):
            ref[l : l + 1, :] = tot[i : i + 1, 0:PER]
        dbup[l : l + 1, :] = tot[7:8, 0:PER]
    for q in range(N):
        rows_b[0, q : q + 1, :] = sx[q, 0, 6:7, :]
        rows_b[1, q : q + 1, :] = sx[q, 1, 6:7, :]
    step = rows_b[1, :, 0:1]
    pick = jnp.where(lax.broadcasted_iota(jnp.int32, (N, TS), 1).astype(F32) == step, 1.0, 0.0)
    table_o[...] = lax.dot_general(rows_b[0], pick, TN, precision=lax.Precision.HIGHEST, preferred_element_type=F32)[0:PER, :]
    for l in range(L):
        ins[l].wait()
        ga = g_b[l, 0]
        for cc in range(3):
            gq[l, cc] = ga[:, cc * HL : cc * HL + HL]
        gt = jnp.concatenate([ga, jnp.zeros((-PER % 128, 4 * HL), F32)], axis=0).T
        go[l] = gt[3 * HL : 4 * HL, 0:PER]
    outs = []
    for j, ref in ((1, gup), (2, gdown)):
        for l in range(L):
            ins[j * L + l].wait()
            cp = pltpu.make_async_copy(g_b.at[l, j], ref.at[l], sem_o.at[l * 2 + j - 1])
            cp.start()
            outs.append(cp)
    for i, (_, buf, dst) in enumerate(order):
        ins[3 * L + i].wait()
        cp = pltpu.make_async_copy(buf, dst, sem_o.at[2 * L + i])
        cp.start()
        outs.append(cp)
    for cp in outs:
        cp.wait()


def split_of(n):
    inner = 2 ** ((n.bit_length() - 1) // 2)
    return inner, n // inner


def run_step(ts, bs, vecs, bup, tok, cot, table, wqkv, wout, wup, wdown):
    R, D = tok.shape
    L, _, FL = wup.shape
    HL = wout.shape[1]
    N = lax.axis_size("dp")
    NI, NO = split_of(N)
    PER = D // N
    FUSED = PER % 16 == 0
    assert lax.axis_size("tensor") == 4 and ts.shape[0] == 1 and FL == D == 4 * HL and L > 1 and R == 256
    T = 4 * R
    W = -(-PER // 128) * 128
    dim = dict(D=D, FL=FL, HL=HL, R=R, L=L, BLK=min(R, 128), W=W, N=N, NI=NI, NO=NO, PER=PER, FUSED=FUSED, TS=table.shape[0])
    vm = pl.BlockSpec(memory_space=pltpu.VMEM)
    sm = pl.BlockSpec(memory_space=pltpu.SMEM)
    any_ = pl.BlockSpec(memory_space=pl.ANY)
    dma = pltpu.SemaphoreType.DMA
    V = pltpu.VMEM
    J = 3 if FUSED else 1
    PR = PER if FUSED else 16
    ones = max(NI - 1, 1)
    outs = max(NO - 1, 1)
    kept = (L, 3, PER, FL) if FUSED else (L, 3, D, FL)
    return dim, pl.pallas_call(
        functools.partial(step_kernel, dim),
        out_shape=(
            jax.ShapeDtypeStruct((R, D), BF),
            jax.ShapeDtypeStruct((R, D), F32),
            jax.ShapeDtypeStruct((N, L, 8, W), F32),
            jax.ShapeDtypeStruct(kept, F32),
        ),
        in_specs=[sm, sm] + [vm] * 7 + [any_] * 7,
        out_specs=(any_, any_, vm, any_),
        scratch_shapes=[
            V((L, 3 * HL, D), BF), V((L, HL, D), BF), V((L, D, FL), BF), V((L, FL, D), BF),
            V((2, R, D), BF), V((2, R, D), BF),
            V((L, T, D), BF), V((L, T, D), BF), V((L, T, FL), BF), V((L, T, FL), BF),
            V((L, 3 * HL, T), BF), V((L, 2, T, HL), BF), V((L, HL, T), BF), V((L, 8, T), F32),
            V((L, 2, R, D), F32), V((L, 2, R, D), F32),
            V((T, D), BF), V((T, D), BF), V((2, R, D), F32),
            V((HL, T), BF), V((3 * HL, T), BF), V((2, HL, T), F32),
            V((3, 2, R, D), BF), V((3, 2, R, D), BF), V((2, R, D), BF), V((2, R, D), BF),
            V((R, D), F32), V((T, R), F32), V((T, R), BF), V((T, R), BF), V((D, FL), F32),
            V((L, 8, D), F32), V((L, 8, D), F32), V((N, L, 8, W), F32), V((N, L, 8, W), F32), V((8, D), F32),
            V((J, ones, NO * PR, FL), BF), V((J, ones, NO * PR, FL), BF), V((J, NO * PR, FL), F32),
            V((J, outs, PR, FL), BF), V((J, outs, PR, FL), BF), V((L, J, PR, FL), F32),
            dma((L, 4)), dma((2,)), dma((2,)), dma((3, 2)), dma((3, 2)),
            dma((2,)), dma((2,)), dma((2,)), dma((2,)),
            dma((3,)), dma((2,)), dma((3 * L + 1,)), dma((2,)), dma((N,)), dma((N,)),
            dma((4, ones)), dma((4, ones)), dma((4, outs)), dma((4, outs)),
        ],
        compiler_params=pltpu.CompilerParams(
            collective_id=0, has_side_effects=True, vmem_limit_bytes=67043328),
        name="layers",
    )(ts, bs, *vecs, bup, tok, cot, table, wqkv, wout, wup, wdown)


def local(tokens, timestep, block_size, table, ln1_gain, ln1_bias, w_qkv, w_out, b_out,
          ln2_gain, ln2_bias, w_up, b_up, w_down, b_down, cotangent):
    L, D, _, HL = w_qkv.shape
    wq = jnp.transpose(w_qkv, (0, 2, 3, 1)).reshape(L, 3 * HL, D)
    vecs = (ln1_gain, ln1_bias, b_out, ln2_gain, ln2_bias, b_down)
    dim, (out, gtok, sx, g) = run_step(
        timestep, block_size, vecs, b_up, tokens, cotangent, table, wq, w_out, w_up, w_down)
    PER, FL, TS = dim["PER"], dim["FL"], dim["TS"]
    if not dim["FUSED"]:
        g = lax.psum_scatter(g, "dp", scatter_dimension=2, tiled=True)
    vec = jax.ShapeDtypeStruct((L, PER), F32)
    big = jax.ShapeDtypeStruct((L, PER, FL), F32)
    vm = pl.BlockSpec(memory_space=pltpu.VMEM)
    any_ = pl.BlockSpec(memory_space=pl.ANY)
    N, W = dim["N"], dim["W"]
    got = pl.pallas_call(
        functools.partial(finish_kernel, dim),
        out_shape=(
            jax.ShapeDtypeStruct(out.shape, BF), jax.ShapeDtypeStruct(gtok.shape, F32),
            jax.ShapeDtypeStruct((PER, TS), F32), vec, vec,
            jax.ShapeDtypeStruct((L, 3, PER, HL), F32), jax.ShapeDtypeStruct((L, HL, PER), F32),
            vec, vec, vec, big, vec, big, vec),
        in_specs=[any_, any_, vm, any_],
        out_specs=(any_, any_) + (vm,) * 8 + (any_, vm, any_, vm),
        scratch_shapes=[
            pltpu.VMEM((L, 3, PER, FL), F32), pltpu.VMEM(out.shape, BF), pltpu.VMEM(gtok.shape, F32),
            pltpu.VMEM((2, N, W), F32), pltpu.SemaphoreType.DMA((3 * L + 2,)), pltpu.SemaphoreType.DMA((2 * L + 2,))],
        name="finish",
    )(out, gtok, sx, g)
    got = list(got)
    got[2] = jnp.transpose(got[2])
    got[5] = jnp.transpose(got[5], (0, 2, 1, 3))
    got[12] = jnp.transpose(got[12], (0, 2, 1))
    return tuple(got)


def solution(mesh):
    placed = (
        P(("dp", "tensor"), None), P("dp"), P("dp"), P(), P(), P(),
        P(None, None, None, "tensor"), P(None, "tensor", None), P(), P(), P(),
        P(None, None, "tensor"), P(None, "tensor"), P(None, "tensor", None), P(),
        P(("dp", "tensor"), None),
    )
    return jax.shard_map(
        local,
        mesh=mesh,
        in_specs=placed,
        out_specs=(
            P(("dp", "tensor"), None), P(("dp", "tensor"), None), P(None, "dp"), P(None, "dp"), P(None, "dp"),
            P(None, "dp", None, "tensor"), P(None, "tensor", "dp"), P(None, "dp"), P(None, "dp"), P(None, "dp"),
            P(None, "dp", "tensor"), P(None, ("tensor", "dp")), P(None, "tensor", "dp"), P(None, "dp"),
        ),
        check_vma=False,
    )
```

```python
import functools

import jax
import jax.numpy as jnp
from jax import lax
from jax.experimental import pallas as pl
from jax.experimental.pallas import tpu as pltpu
from jax.sharding import PartitionSpec as P

HEAD_DIM = 64
EPSILON = 1e-05
NEGATIVE = -1e30
MESH = pl.DeviceIdType.MESH
BF = jnp.bfloat16
F32 = jnp.float32
INV_SQRT2 = 0.7071067811865476
INV_SQRT2PI = 0.3989422804014327

NN = (((1,), (0,)), ((), ()))
NT = (((1,), (1,)), ((), ()))
TN = (((0,), (0,)), ((), ()))


def mm(a, b, dims=NN):
    return lax.dot_general(a, b, dims, preferred_element_type=F32)


def step_kernel(dim, *refs):
    (
        ts_ref, bs_ref, g1_in, b1_in, bo_in, g2_in, b2_in, bd_in, bup_in,
        tok_in, cot_in, table_h, wqkv_h, wout_h, wup_h, wdown_h,
        out_o, gtok_o, smallx_o, g_o,
        wqkv, wout, wup, wdown, tokf, cotf,
        a_b, a2_b, g_b, gp_b, qkvT, kv_b, oT_b, lse_b, h_b, m_b,
        df_b, dz_b, dh_b, doT_b, dqT_b, dkv_acc,
        ysend, yrecv, csend, crecv, part, s_b, p_b, ds_b, gstage,
        small, smallr, smallx, smallp, emb_b,
        send1, recv1, own1, send2, recv2, fstage,
        wsem, tsem_s, tsem_r, ysem_s, ysem_r, casem_s, casem_r, cpsem_s, cpsem_r,
        lsem, osem, gsem, ssem, x1s, x1r,
        r1s, r1r, r2s, r2r, turned,
    ) = refs
    D, FL, HL, R, L = dim["D"], dim["FL"], dim["HL"], dim["R"], dim["L"]
    N, NI, NO, PER, FUSED = dim["N"], dim["NI"], dim["NO"], dim["PER"], dim["FUSED"]
    HP = HL
    vecs = (g1_in, b1_in, bo_in, g2_in, b2_in, bd_in)

    def vrow(i, l):
        return vecs[i][l : l + 1, :].astype(F32)

    T = 4 * R
    NH = HL // HEAD_DIM
    CH = 2 * R
    NB = D // 256
    FB = FL // 256
    t = lax.axis_index("tensor")
    d = lax.axis_index("dp")
    di = lax.rem(d, NI)
    do_ = lax.div(d, NI)
    y = lax.div(t, 2)
    c = lax.rem(t, 2)
    ypeer = lax.rem(t + 2, 4)
    cpeer = t + 1 - 2 * c

    def own(r):
        return pl.multiple_of(R * (2 * r + c), R)

    def oth(r):
        return pl.multiple_of(R * (2 * r + 1 - c), R)

    def remote(src, dst, ss, rs, peer):
        return pltpu.make_async_remote_copy(
            src_ref=src, dst_ref=dst, send_sem=ss, recv_sem=rs,
            device_id={"tensor": peer}, device_id_type=MESH)

    def dp_remote(src, dst, ss, rs, peer):
        return pltpu.make_async_remote_copy(
            src_ref=src, dst_ref=dst, send_sem=ss, recv_sem=rs,
            device_id={"dp": peer}, device_id_type=MESH)

    bar = pltpu.get_barrier_semaphore()

    def greet(k, cy):
        pl.semaphore_signal(bar, inc=1, device_id={"dp": lax.rem(d + k, N)}, device_id_type=MESH)
        return cy

    lax.fori_loop(1, N, greet, 0)
    pl.semaphore_signal(bar, inc=1, device_id={"tensor": ypeer}, device_id_type=MESH)
    pl.semaphore_signal(bar, inc=1, device_id={"tensor": cpeer}, device_id_type=MESH)

    loc = [pltpu.make_async_copy(tok_in, tokf.at[y], lsem.at[0]),
           pltpu.make_async_copy(cot_in, cotf.at[y], lsem.at[1]),
           pltpu.make_async_copy(table_h, df_b.at[pl.ds(0, dim["TS"]), :], lsem.at[2])]
    for cp in loc:
        cp.start()
    wcopies = []
    for l in range(L):
        row = []
        for i, (src, dst) in enumerate(((wqkv_h, wqkv), (wout_h, wout), (wup_h, wup), (wdown_h, wdown))):
            cp = pltpu.make_async_copy(src.at[l], dst.at[l], wsem.at[l, i])
            cp.start()
            row.append(cp)
        wcopies.append(row)
    pl.semaphore_wait(bar, N + 1)
    tcp = [remote(tok_in, tokf.at[y], tsem_s.at[0], tsem_r.at[0], ypeer),
           remote(cot_in, cotf.at[y], tsem_s.at[1], tsem_r.at[1], ypeer)]
    tcp[0].start()

    small[...] = jnp.zeros_like(small)
    bs = bs_ref[0]
    loc[2].wait()
    pick = (lax.broadcasted_iota(jnp.int32, (8, dim["TS"]), 1) == ts_ref[0]).astype(BF)
    emb_b[...] = mm(pick, df_b[0 : dim["TS"], :])

    def y_copy(par, r, i):
        rows = pl.ds(i, BLK)
        b = i // BLK
        return remote(ysend.at[par, r, rows, :], yrecv.at[par, r, rows, :],
                      ysem_s.at[par, r, b], ysem_r.at[par, r, b], ypeer)

    def tile_copy(buf, r, i, q):
        rows = pl.ds(pl.multiple_of(own(r) + i, BLK), BLK)
        b = i // BLK
        return remote(buf.at[rows, :], buf.at[rows, :], casem_s.at[q, b], casem_r.at[q, b], cpeer)

    class Tile:
        def __init__(self, buf, r, q=None):
            self.copy = lambda i: tile_copy(buf, r, i, r if q is None else q)

        def wait_recv(self):
            for i in range(0, R, BLK):
                self.copy(i).wait_recv()

        def wait_send(self):
            for i in range(0, R, BLK):
                self.copy(i).wait_send()

    def part_copy(r):
        return remote(csend.at[r], crecv.at[r], cpsem_s.at[r], cpsem_r.at[r], cpeer)

    BLK = dim["BLK"]

    def rowloop(fn, init=0):
        return lax.fori_loop(0, R // BLK, lambda i, cy: fn(pl.multiple_of(i * BLK, BLK), cy), init)

    def ln_stats(x):
        mean = jnp.sum(x, axis=-1, keepdims=True) * (1.0 / D)
        xc = x - mean
        var = jnp.sum(xc * xc, axis=-1, keepdims=True) * (1.0 / D)
        return xc, lax.rsqrt(var + EPSILON)

    def enter_fwd(l, r, src, gi, dst_h, dst_a, par=None):
        gain = vrow(gi, l)
        bias = vrow(gi + 1, l)
        cp = Tile(dst_a.at[l], r)

        def blk(i, cy):
            if par is not None:
                wait_y(par, r, i)
            x = src(i)
            dst_h[l, r, pl.ds(i, BLK), :] = x
            xc, rstd = ln_stats(x)
            dst_a[l, pl.ds(pl.multiple_of(own(r) + i, BLK), BLK), :] = (xc * rstd * gain + bias).astype(BF)
            cp.copy(i).start()
            return cy

        rowloop(blk)
        return cp

    def ysum(par, r, i):
        return ysend[par, r, pl.ds(i, BLK), :].astype(F32) + yrecv[par, r, pl.ds(i, BLK), :].astype(F32)

    def wait_y(par, r, i):
        cp = y_copy(par, r, i)
        cp.wait_send()
        cp.wait_recv()

    def send_partner(r, fill):
        fill(csend.at[r])
        cp = part_copy(r)
        cp.start()
        return cp

    def combine(par, r, cp):
        cp.wait_recv()

        def blk(i, cy):
            v = part[pl.ds(i, BLK), :] + crecv[r, pl.ds(i, BLK), :].astype(F32)
            ysend[par, r, pl.ds(i, BLK), :] = v.astype(BF)
            y_copy(par, r, i).start()
            return cy

        rowloop(blk)
        cp.wait_send()

    def qkv_tile(l, q0):
        q = mm(wqkv[l, 0:HP, :], a_b[l, pl.ds(q0, R), :], NT).astype(BF)
        qkvT[l, 0:HP, pl.ds(q0, R)] = q * jnp.asarray(HEAD_DIM ** -0.5, BF)
        for cc in (1, 2):
            v = mm(wqkv[l, cc * HP : cc * HP + HP, :], a_b[l, pl.ds(q0, R), :], NT)
            qkvT[l, cc * HP : cc * HP + HP, pl.ds(q0, R)] = v.astype(BF)
            kv_b[l, cc - 1, pl.ds(q0, R), :] = v.T.astype(BF)

    def hmask(h):
        rows = lax.broadcasted_iota(jnp.int32, (HP, R), 0)
        return (rows >= h * HEAD_DIM) & (rows < (h + 1) * HEAD_DIM)

    def visible(r, kb, q0):
        key = lax.broadcasted_iota(jnp.int32, (R, R), 0) + (CH * r + kb * R)
        qry = lax.broadcasted_iota(jnp.int32, (R, R), 1) + q0
        return key <= (qry | (bs - 1))

    def att_fwd_tile(l, r, q0):
        KB = 2 * (r + 1)

        def head(h, cy):
            qm = jnp.where(hmask(h), qkvT[l, 0:HP, pl.ds(q0, R)].astype(F32), 0.0).astype(BF)
            top = None
            for kb in range(KB):
                s = mm(kv_b[l, 0, kb * R : kb * R + R, :], qm)
                if kb >= 2 * r:
                    s = jnp.where(visible(r, kb - 2 * r, q0), s, NEGATIVE)
                s_b[kb * R : kb * R + R, :] = s
                mx = jnp.max(s, axis=0, keepdims=True)
                top = mx if top is None else jnp.maximum(top, mx)
            tot = None
            for kb in range(KB):
                e = jnp.exp(s_b[kb * R : kb * R + R, :] - top)
                p_b[kb * R : kb * R + R, :] = e.astype(BF)
                sm = jnp.sum(e, axis=0, keepdims=True)
                tot = sm if tot is None else tot + sm
            hr = pl.multiple_of(h * HEAD_DIM, HEAD_DIM)
            o = mm(qkvT[l, pl.ds(pl.multiple_of(2 * HP + hr, HEAD_DIM), HEAD_DIM), 0 : KB * R], p_b[0 : KB * R, :])
            oT_b[l, pl.ds(hr, HEAD_DIM), pl.ds(q0, R)] = (o * (1.0 / tot)).astype(BF)
            lse_b[l, pl.ds(h, 1), pl.ds(q0, R)] = top + jnp.log(tot)
            return cy

        lax.fori_loop(0, NH, head, 0)

    def nblocks(fn, n):
        for i in range(n):
            fn(i * 256)

    def out_tile(l, q0, dst):
        o = oT_b[l, :, pl.ds(q0, R)].astype(F32).T.astype(BF)

        def one(n):
            dst[:, n : n + 256] = mm(o, wout[l, :, n : n + 256]).astype(dst.dtype)

        nblocks(one, NB)

    def up_tile(l, q0):
        def one(n, cy):
            n = pl.multiple_of(n * 256, 256)
            u = mm(a2_b[l, pl.ds(q0, R), :], wup[l, :, pl.ds(n, 256)]) + bup_in[l : l + 1, pl.ds(n, 256)].astype(F32)
            phi = 0.5 * (1.0 + lax.erf(u * INV_SQRT2))
            g_b[l, pl.ds(q0, R), pl.ds(n, 256)] = (u * phi).astype(BF)
            gp = phi + u * (jnp.exp(u * u * -0.5) * INV_SQRT2PI)
            gp_b[l, pl.ds(q0, R), pl.ds(n, 256)] = gp.astype(BF)
            return cy

        lax.fori_loop(0, FB, one, 0)

    def down_tile(l, q0, dst):
        def one(n):
            dst[:, n : n + 256] = mm(g_b[l, pl.ds(q0, R), :], wdown[l, :, n : n + 256]).astype(dst.dtype)

        nblocks(one, NB)

    def own_first(r, tile_cp, fn):
        def tile(i, cy):
            if tile_cp is not None:
                @pl.when(i == 1)
                def _():
                    tile_cp.wait_recv()

            fn(pl.multiple_of(R * (2 * r + c + i * (1 - 2 * c)), R))
            return cy

        lax.fori_loop(0, 2, tile, 0)

    def att_fwd(l, r, tile_cp):
        own_first(r, tile_cp, lambda q0: qkv_tile(l, q0))
        cp = part_copy(r)

        def tile(i, cy):
            att_fwd_tile(l, r, pl.multiple_of(R * (2 * r + 1 - c + i * (2 * c - 1)), R))

            @pl.when(i == 0)
            def _():
                out_tile(l, oth(r), csend.at[r])
                cp.start()

            return cy

        lax.fori_loop(0, 2, tile, 0)
        out_tile(l, own(r), part)
        tile_cp.wait_send()
        combine(0, r, cp)

    def ffn_fwd(l, r, tile_cp):
        own_first(r, tile_cp, lambda q0: up_tile(l, q0))
        cp = send_partner(r, lambda ref: down_tile(l, oth(r), ref))
        down_tile(l, own(r), part)
        tile_cp.wait_send()
        combine(1, r, cp)

    def finish_output(r):
        bd = vrow(5, L - 1)

        def blk(i, cy):
            wait_y(1, r, i)
            v = m_b[L - 1, r, pl.ds(i, BLK), :] + (ysum(1, r, i) + bd)
            tokf[r, pl.ds(i, BLK), :] = v.astype(BF)
            return cy

        rowloop(blk)

    def ln_bwd(l, r, par, gi, xbuf, emit):
        gain = vrow(gi, l)

        def blk(i, cy):
            dg, db = cy
            wait_y(par, r, i)
            x = xbuf[l, r, pl.ds(i, BLK), :]
            dy = ysum(par, r, i)
            xc, rstd = ln_stats(x)
            xh = xc * rstd
            t1 = dy * gain
            m1 = jnp.sum(t1, axis=-1, keepdims=True) * (1.0 / D)
            m2 = jnp.sum(t1 * xh, axis=-1, keepdims=True) * (1.0 / D)
            dx = rstd * (t1 - m1 - xh * m2)
            emit(i, dx)
            dg = dg + jnp.sum(dy * xh, axis=0, keepdims=True)
            db = db + jnp.sum(dy, axis=0, keepdims=True)
            return (dg, db)

        z = jnp.zeros((1, D), F32)
        dg, db = rowloop(blk, (z, z))
        small[l, gi : gi + 1, :] = small[l, gi : gi + 1, :] + dg
        small[l, gi + 1 : gi + 2, :] = small[l, gi + 1 : gi + 2, :] + db

    def colsum_own(buf, r, l, row):
        def blk(i, cy):
            return cy + jnp.sum(buf[pl.ds(pl.multiple_of(own(r) + i, BLK), BLK), :].astype(F32), axis=0, keepdims=True)

        v = rowloop(blk, jnp.zeros((1, D), F32))
        small[l, row : row + 1, :] = small[l, row : row + 1, :] + v

    def enter_b1(l, r):
        cp = Tile(df_b, r, 2 + r if l == L - 1 else r)
        if l == L - 1:
            def blk(i, cy):
                v = cotf[r, pl.ds(i, BLK), :]
                dh_b[r, pl.ds(i, BLK), :] = v.astype(F32)
                df_b[pl.ds(pl.multiple_of(own(r) + i, BLK), BLK), :] = v
                cp.copy(i).start()
                return cy

            rowloop(blk)
        else:
            def emit(i, dx):
                v = dh_b[r, pl.ds(i, BLK), :] + dx
                dh_b[r, pl.ds(i, BLK), :] = v
                df_b[pl.ds(pl.multiple_of(own(r) + i, BLK), BLK), :] = v.astype(BF)
                cp.copy(i).start()

            ln_bwd(l + 1, r, 0, 0, h_b, emit)
        colsum_own(df_b, r, l, 5)
        return cp

    def du_tile(l, q0):
        def one(n, cy):
            n = pl.multiple_of(n * 256, 256)
            dg = mm(df_b[pl.ds(q0, R), :], wdown[l, pl.ds(n, 256), :], NT)
            du = (dg * gp_b[l, pl.ds(q0, R), pl.ds(n, 256)].astype(F32)).astype(BF)
            gp_b[l, pl.ds(q0, R), pl.ds(n, 256)] = du
            small[l, 7:8, pl.ds(n, 256)] = small[l, 7:8, pl.ds(n, 256)] + jnp.sum(du.astype(F32), axis=0, keepdims=True)
            return cy

        lax.fori_loop(0, FB, one, 0)

    def da2_tile(l, q0, dst):
        def one(n):
            dst[:, n : n + 256] = mm(gp_b[l, pl.ds(q0, R), :], wup[l, n : n + 256, :], NT).astype(dst.dtype)

        nblocks(one, NB)

    def ffn_bwd(l, r, tile_cp):
        own_first(r, tile_cp, lambda q0: du_tile(l, q0))
        if l == L - 1 and r == 1:
            pl.semaphore_wait(turned, 1)
        cp = send_partner(r, lambda ref: da2_tile(l, oth(r), ref))
        da2_tile(l, own(r), part)
        if tile_cp is not None:
            tile_cp.wait_send()
        combine(2, r, cp)

    def enter_b2(l, r):
        cp = Tile(dz_b, r)

        def emit(i, dx):
            v = dh_b[r, pl.ds(i, BLK), :] + dx
            dh_b[r, pl.ds(i, BLK), :] = v
            dz_b[pl.ds(pl.multiple_of(own(r) + i, BLK), BLK), :] = v.astype(BF)
            cp.copy(i).start()

        ln_bwd(l, r, 2, 3, m_b, emit)
        colsum_own(dz_b, r, l, 2)
        return cp

    def do_tile(l, q0):
        doT_b[:, pl.ds(q0, R)] = mm(wout[l], dz_b[pl.ds(q0, R), :], NT).astype(BF)

    def att_bwd_tile(l, r, q0):
        KB = 2 * (r + 1)
        KN = KB * R

        def head(h, cy):
            hr = pl.multiple_of(h * HEAD_DIM, HEAD_DIM)
            hm = hmask(h)
            qm = jnp.where(hm, qkvT[l, 0:HP, pl.ds(q0, R)].astype(F32), 0.0).astype(BF)
            dom = jnp.where(hm, doT_b[:, pl.ds(q0, R)].astype(F32), 0.0).astype(BF)
            do_h = doT_b[pl.ds(hr, HEAD_DIM), pl.ds(q0, R)]
            q_h = qkvT[l, pl.ds(hr, HEAD_DIM), pl.ds(q0, R)]
            o_h = oT_b[l, pl.ds(hr, HEAD_DIM), pl.ds(q0, R)]
            dsum = jnp.sum(do_h.astype(F32) * o_h.astype(F32), axis=0, keepdims=True)
            lse = lse_b[l, pl.ds(h, 1), pl.ds(q0, R)]
            for kb in range(KB):
                ks = slice(kb * R, kb * R + R)
                s = mm(kv_b[l, 0, ks, :], qm)
                p = jnp.exp(s - lse)
                if kb >= 2 * r:
                    p = jnp.where(visible(r, kb - 2 * r, q0), p, 0.0)
                p_b[ks, :] = p.astype(BF)
                dp = mm(kv_b[l, 1, ks, :], dom)
                ds_b[ks, :] = (p * (dp - dsum)).astype(BF)
            dkv_acc[1, pl.ds(hr, HEAD_DIM), 0:KN] = dkv_acc[1, pl.ds(hr, HEAD_DIM), 0:KN] + mm(do_h, p_b[0:KN, :], NT)
            dkv_acc[0, pl.ds(hr, HEAD_DIM), 0:KN] = dkv_acc[0, pl.ds(hr, HEAD_DIM), 0:KN] + mm(q_h, ds_b[0:KN, :], NT)
            k_h = qkvT[l, pl.ds(pl.multiple_of(HP + hr, HEAD_DIM), HEAD_DIM), 0:KN]
            dq = mm(k_h, ds_b[0:KN, :]) * (HEAD_DIM ** -0.5)
            dqT_b[pl.ds(hr, HEAD_DIM), pl.ds(q0, R)] = dq.astype(BF)
            return cy

        lax.fori_loop(0, NH, head, 0)

    def da_tile(l, q0, dst):
        dqkv = dqT_b[:, pl.ds(q0, R)].astype(F32).T.astype(BF)

        def one(n):
            dst[:, n : n + 256] = mm(dqkv, wqkv[l, :, n : n + 256]).astype(dst.dtype)

        nblocks(one, NB)

    def att_bwd(l, r, tile_cp):
        def both(q0):
            do_tile(l, q0)
            att_bwd_tile(l, r, q0)

        own_first(r, tile_cp, both)
        cs = slice(CH * r, CH * r + CH)
        for j in range(2):
            dqT_b[HP * (j + 1) : HP * (j + 1) + HL, cs] = dkv_acc[j, 0:HL, cs].astype(BF)
        cp = send_partner(r, lambda ref: da_tile(l, oth(r), ref))
        da_tile(l, own(r), part)
        tile_cp.wait_send()
        combine(0, r, cp)

    WHOLE = (0, FL, 0)
    HALF = ((0, FL // 2, 0), (FL // 2, FL - FL // 2, 3))

    def r1_copy(j, k, span):
        c0, w, extra = span
        q = j + extra
        peer = do_ * NI + lax.rem(di + k, NI)
        return dp_remote(send1.at[j, k - 1, :, c0 : c0 + w], recv1.at[j, k - 1, :, c0 : c0 + w],
                         r1s.at[q, k - 1], r1r.at[q, k - 1], peer)

    def r2_copy(j, k, span):
        c0, w, extra = span
        q = j + extra
        peer = lax.rem(do_ + k, NO) * NI + di
        return dp_remote(send2.at[j, k - 1, :, c0 : c0 + w], recv2.at[j, k - 1, :, c0 : c0 + w],
                         r2s.at[q, k - 1], r2r.at[q, k - 1], peer)

    def g_copy(l, j, span):
        c0, w, extra = span
        q = l * 6 + j + extra
        return pltpu.make_async_copy(fstage.at[l, j, :, c0 : c0 + w], g_o.at[l, j, :, c0 : c0 + w], gsem.at[q])

    def piece(q):
        return pl.ds(pl.multiple_of(q * PER, PER), PER)

    def rs_start(l, j, span=WHOLE):
        c0, w, _ = span
        cols = slice(c0, c0 + w)
        if not FUSED:
            cp = pltpu.make_async_copy(gstage.at[:, cols], g_o.at[l, j, :, cols], gsem.at[0])
            cp.start()
            cp.wait()
            return
        for k in range(1, NI):
            for oo in range(NO):
                send1[j, k - 1, oo * PER : oo * PER + PER, cols] = gstage[piece(oo * NI + lax.rem(di + k, NI)), cols].astype(BF)
            r1_copy(j, k, span).start()
        for oo in range(NO):
            own1[j, oo * PER : oo * PER + PER, cols] = gstage[piece(oo * NI + di), cols]

    def rs_mid(l, j, span=WHOLE):
        c0, w, _ = span
        cols = slice(c0, c0 + w)
        if not FUSED:
            return
        for k in range(1, NI):
            cp = r1_copy(j, k, span)
            cp.wait_send()
            cp.wait_recv()
        for kk in range(NO - 1, -1, -1):
            rows = piece(lax.rem(do_ + kk, NO))
            v = own1[j, rows, cols]
            for k in range(1, NI):
                v = v + recv1[j, k - 1, rows, cols].astype(F32)
            if kk == 0:
                own1[j, rows, cols] = v
            else:
                send2[j, kk - 1, :, cols] = v.astype(BF)
                r2_copy(j, kk, span).start()

    def rs_fin(l, j, span=WHOLE):
        c0, w, _ = span
        cols = slice(c0, c0 + w)
        if not FUSED:
            return
        v = own1[j, piece(do_), cols]
        for kk in range(1, NO):
            cp = r2_copy(j, kk, span)
            cp.wait_send()
            cp.wait_recv()
            v = v + recv2[j, kk - 1, :, cols].astype(F32)
        fstage[l, j, :, cols] = v
        g_copy(l, j, span).start()

    def wgrad_ffn(l, lhs, rhs, rows=slice(None), add=False):
        def one(n, cy):
            ns = pl.ds(pl.multiple_of(n * 256, 256), 256)
            lt = lhs[rows, ns].astype(F32).T.astype(BF)
            for f in range(FB):
                fs = slice(f * 256, f * 256 + 256)
                v = mm(lt, rhs[rows, fs])
                gstage[ns, fs] = gstage[ns, fs] + v if add else v
            return cy

        lax.fori_loop(0, NB, one, 0)

    def wgrad_att(l, span):
        lo, hi = span[0], span[0] + span[1]
        q = min(hi, 3 * HL)

        def one(n, cy):
            ns = pl.ds(pl.multiple_of(n * 256, 256), 256)
            s_b[lo:q, :] = mm(dqT_b[lo:q, :], a_b[l, :, ns])
            if hi > q:
                s_b[q:hi, :] = mm(oT_b[l], dz_b[:, ns])
            gstage[ns, lo:hi] = s_b[lo:hi, :].T
            return cy

        lax.fori_loop(0, NB, one, 0)

    for l in range(L):
        for r in range(2):
            if l == 0:
                if r == 0:
                    for cp in (loc[0], wcopies[0][0]):
                        cp.wait()
                    tcp[0].wait()
                    tcp[1].start()
                src = lambda i, r=r: tokf[r, pl.ds(i, BLK), :].astype(F32) + emb_b[0:1, :]
            else:
                bd = vrow(5, l - 1)
                src = lambda i, r=r, l=l, bd=bd: m_b[l - 1, r, pl.ds(i, BLK), :] + (ysum(1, r, i) + bd)
            if r == 0 and l > 0:
                wcopies[l][0].wait()
            cp = enter_fwd(l, r, src, 0, h_b, a_b, 1 if l > 0 else None)
            if r == 0:
                wcopies[l][1].wait()
            att_fwd(l, r, cp)
        for r in range(2):
            if l == L - 1 and r == 0:
                loc[1].wait()
                tcp[1].wait()
                b1 = [enter_b1(l, 0), enter_b1(l, 1)]
            elif l == L - 1:
                b1[0].wait_recv()
                wgrad_ffn(l, df_b, g_b.at[l], slice(0, CH))
            bo = vrow(2, l)
            src = lambda i, r=r, l=l, bo=bo: h_b[l, r, pl.ds(i, BLK), :] + (ysum(0, r, i) + bo)
            if r == 0:
                wcopies[l][2].wait()
                wcopies[l][3].wait()
            cp = enter_fwd(l, r, src, 3, m_b, a2_b, 0)
            ffn_fwd(l, r, cp)

    pl.semaphore_signal(turned, inc=1, device_id={"tensor": cpeer}, device_id_type=MESH)
    b1[1].wait_recv()
    wgrad_ffn(L - 1, df_b, g_b.at[L - 1], slice(CH, T), True)
    rs_start(L - 1, 2)
    for cp in b1:
        cp.wait_send()
    for l in range(L - 1, -1, -1):
        last = l == L - 1
        spans = (WHOLE,) if l > 0 else HALF
        for r in (1, 0):
            ffn_bwd(l, r, None if last else enter_b1(l, r))
            if not last:
                rs_fin(l + 1, 1 + r)
        if last:
            for r in (1, 0):
                finish_output(r)
        else:
            rs_mid(l + 1, 0)
            wgrad_ffn(l, df_b, g_b.at[l])
            for span in spans:
                rs_start(l, 2, span)
        wgrad_ffn(l, a2_b.at[l], gp_b.at[l])
        for span in spans:
            rs_start(l, 1, span)
        dkv_acc[...] = jnp.zeros_like(dkv_acc)
        for r in (1, 0):
            cp = enter_b2(l, r)
            if last and r == 1:
                rs_mid(l, 2)
            att_bwd(l, r, cp)
            if not last and r == 1:
                rs_fin(l + 1, 0)
                for span in spans:
                    rs_mid(l, 2, span)
        if last:
            rs_mid(l, 1)
            wgrad_att(l, WHOLE)
            rs_start(l, 0)
        else:
            wgrad_att(l, HALF[0])
            rs_mid(l, 1, HALF[0])
            rs_start(l, 0, HALF[0])
            wgrad_att(l, HALF[1])
            rs_start(l, 0, HALF[1])
            rs_mid(l, 1, HALF[1])
    ocp = pltpu.make_async_copy(tokf.at[y], out_o, osem.at[0])
    ocp.start()
    for span in HALF:
        rs_fin(0, 2, span)
    for r in (1, 0):
        def emit(i, dx, r=r):
            v = dh_b[r, pl.ds(i, BLK), :] + dx
            dh_b[r, pl.ds(i, BLK), :] = v
            small[0, 6:7, :] = small[0, 6:7, :] + jnp.sum(v, axis=0, keepdims=True)

        ln_bwd(0, r, 0, 0, h_b, emit)
        if r == 1:
            rs_mid(0, 0, HALF[0])
    gcp = pltpu.make_async_copy(dh_b.at[y], gtok_o, osem.at[1])
    gcp.start()
    scp = remote(small, smallr, ssem.at[0], ssem.at[1], cpeer)
    scp.start()
    scp.wait()
    shared = lax.broadcasted_iota(jnp.int32, (8, D), 0) < 7
    for l in range(L):
        small[l] = small[l] + jnp.where(shared, smallr[l], 0.0)
    small[1, 6:7, :] = jnp.full((1, D), ts_ref[0].astype(F32), F32)

    def x_copy(k):
        return dp_remote(smallp.at[k], smallx.at[d], x1s.at[k], x1r.at[k], lax.rem(d + k, N))

    def columns(k):
        turn = lax.rem(D - PER * lax.rem(d + k, N), D)
        return [pltpu.roll(small[l], turn, 1)[:, 0 : smallx.shape[3]] for l in range(L)]

    def x_go(k, cy):
        for l, v in enumerate(columns(k)):
            smallp[k, l] = v
        x_copy(k).start()
        return cy

    def x_wait(k, cy):
        cp = x_copy(k)
        cp.wait_send()
        cp.wait_recv()
        return cy

    lax.fori_loop(1, N, x_go, 0)
    for l, v in enumerate(columns(0)):
        smallx[d, l] = v
    rs_mid(0, 0, HALF[1])
    for span in HALF:
        rs_fin(0, 1, span)
    rs_fin(0, 0, HALF[0])
    lax.fori_loop(1, N, x_wait, 0)
    smallx_o[...] = smallx[...]
    rs_fin(0, 0, HALF[1])
    ocp.wait()
    gcp.wait()
    if FUSED:
        for l in range(L):
            for j in range(3):
                for span in HALF if l == 0 else (WHOLE,):
                    g_copy(l, j, span).wait()


def finish_kernel(dim, out_i, gtok_i, sx, g_i, out_o, gtok_o, table_o, dg1, db1, gq, go, dbo, dg2, db2, gup, dbup, gdown, dbd,
                  g_b, out_b, gtok_b, rows_b, sem_i, sem_o):
    FL, HL, L, PER, N, TS = dim["FL"], dim["HL"], dim["L"], dim["PER"], dim["N"], dim["TS"]
    ins = []
    for j in range(3):
        for l in range(L):
            ins.append(pltpu.make_async_copy(g_i.at[l, j], g_b.at[l, j], sem_i.at[l * 3 + j]))
    order = ((out_i, out_b, out_o), (gtok_i, gtok_b, gtok_o))
    for i, (src, buf, _) in enumerate(order):
        ins.append(pltpu.make_async_copy(src, buf, sem_i.at[3 * L + i]))
    for cp in ins:
        cp.start()
    for l in range(L):
        tot = sx[0, l]
        for q in range(1, N):
            tot = tot + sx[q, l]
        for i, ref in enumerate((dg1, db1, dbo, dg2, db2, dbd)):
            ref[l : l + 1, :] = tot[i : i + 1, 0:PER]
        dbup[l : l + 1, :] = tot[7:8, 0:PER]
    for q in range(N):
        rows_b[0, q : q + 1, :] = sx[q, 0, 6:7, :]
        rows_b[1, q : q + 1, :] = sx[q, 1, 6:7, :]
    step = rows_b[1, :, 0:1]
    pick = jnp.where(lax.broadcasted_iota(jnp.int32, (N, TS), 1).astype(F32) == step, 1.0, 0.0)
    table_o[...] = lax.dot_general(rows_b[0], pick, TN, precision=lax.Precision.HIGHEST, preferred_element_type=F32)[0:PER, :]
    for l in range(L):
        ins[l].wait()
        ga = g_b[l, 0]
        for cc in range(3):
            gq[l, cc] = ga[:, cc * HL : cc * HL + HL]
        gt = jnp.concatenate([ga, jnp.zeros((-PER % 128, 4 * HL), F32)], axis=0).T
        go[l] = gt[3 * HL : 4 * HL, 0:PER]
    outs = []
    for j, ref in ((1, gup), (2, gdown)):
        for l in range(L):
            ins[j * L + l].wait()
            cp = pltpu.make_async_copy(g_b.at[l, j], ref.at[l], sem_o.at[l * 2 + j - 1])
            cp.start()
            outs.append(cp)
    for i, (_, buf, dst) in enumerate(order):
        ins[3 * L + i].wait()
        cp = pltpu.make_async_copy(buf, dst, sem_o.at[2 * L + i])
        cp.start()
        outs.append(cp)
    for cp in outs:
        cp.wait()


def split_of(n):
    inner = 2 ** ((n.bit_length() - 1) // 2)
    return inner, n // inner


def run_step(ts, bs, vecs, bup, tok, cot, table, wqkv, wout, wup, wdown):
    R, D = tok.shape
    L, _, FL = wup.shape
    HL = wout.shape[1]
    N = lax.axis_size("dp")
    NI, NO = split_of(N)
    PER = D // N
    FUSED = PER % 16 == 0
    assert lax.axis_size("tensor") == 4 and ts.shape[0] == 1 and FL == D == 4 * HL and L > 1 and R == 256
    T = 4 * R
    W = -(-PER // 128) * 128
    BLK = min(R, 128)
    HB = R // BLK
    dim = dict(D=D, FL=FL, HL=HL, R=R, L=L, BLK=BLK, W=W, N=N, NI=NI, NO=NO, PER=PER, FUSED=FUSED, TS=table.shape[0])
    vm = pl.BlockSpec(memory_space=pltpu.VMEM)
    sm = pl.BlockSpec(memory_space=pltpu.SMEM)
    any_ = pl.BlockSpec(memory_space=pl.ANY)
    dma = pltpu.SemaphoreType.DMA
    V = pltpu.VMEM
    J = 3 if FUSED else 1
    PR = PER if FUSED else 16
    ones = max(NI - 1, 1)
    outs = max(NO - 1, 1)
    kept = (L, 3, PER, FL) if FUSED else (L, 3, D, FL)
    return dim, pl.pallas_call(
        functools.partial(step_kernel, dim),
        out_shape=(
            jax.ShapeDtypeStruct((R, D), BF),
            jax.ShapeDtypeStruct((R, D), F32),
            jax.ShapeDtypeStruct((N, L, 8, W), F32),
            jax.ShapeDtypeStruct(kept, F32),
        ),
        in_specs=[sm, sm] + [vm] * 7 + [any_] * 7,
        out_specs=(any_, any_, vm, any_),
        scratch_shapes=[
            V((L, 3 * HL, D), BF), V((L, HL, D), BF), V((L, D, FL), BF), V((L, FL, D), BF),
            V((2, R, D), BF), V((2, R, D), BF),
            V((L, T, D), BF), V((L, T, D), BF), V((L, T, FL), BF), V((L, T, FL), BF),
            V((L, 3 * HL, T), BF), V((L, 2, T, HL), BF), V((L, HL, T), BF), V((L, 8, T), F32),
            V((L, 2, R, D), F32), V((L, 2, R, D), F32),
            V((T, D), BF), V((T, D), BF), V((2, R, D), F32),
            V((HL, T), BF), V((3 * HL, T), BF), V((2, HL, T), F32),
            V((3, 2, R, D), BF), V((3, 2, R, D), BF), V((2, R, D), BF), V((2, R, D), BF),
            V((R, D), F32), V((T, R), F32), V((T, R), BF), V((T, R), BF), V((D, FL), F32),
            V((L, 8, D), F32), V((L, 8, D), F32), V((N, L, 8, W), F32), V((N, L, 8, W), F32), V((8, D), F32),
            V((J, ones, NO * PR, FL), BF), V((J, ones, NO * PR, FL), BF), V((J, NO * PR, FL), F32),
            V((J, outs, PR, FL), BF), V((J, outs, PR, FL), BF), V((L, J, PR, FL), F32),
            dma((L, 4)), dma((2,)), dma((2,)), dma((3, 2, HB)), dma((3, 2, HB)),
            dma((4, HB)), dma((4, HB)), dma((2,)), dma((2,)),
            dma((3,)), dma((2,)), dma((6 * L,)), dma((2,)), dma((N,)), dma((N,)),
            dma((6, ones)), dma((6, ones)), dma((6, outs)), dma((6, outs)), pltpu.SemaphoreType.REGULAR,
        ],
        compiler_params=pltpu.CompilerParams(
            collective_id=0, has_side_effects=True, vmem_limit_bytes=67043328),
        name="layers",
    )(ts, bs, *vecs, bup, tok, cot, table, wqkv, wout, wup, wdown)


def local(tokens, timestep, block_size, table, ln1_gain, ln1_bias, w_qkv, w_out, b_out,
          ln2_gain, ln2_bias, w_up, b_up, w_down, b_down, cotangent):
    L, D, _, HL = w_qkv.shape
    wq = jnp.transpose(w_qkv, (0, 2, 3, 1)).reshape(L, 3 * HL, D)
    vecs = (ln1_gain, ln1_bias, b_out, ln2_gain, ln2_bias, b_down)
    dim, (out, gtok, sx, g) = run_step(
        timestep, block_size, vecs, b_up, tokens, cotangent, table, wq, w_out, w_up, w_down)
    PER, FL, TS = dim["PER"], dim["FL"], dim["TS"]
    if not dim["FUSED"]:
        g = lax.psum_scatter(g, "dp", scatter_dimension=2, tiled=True)
    vec = jax.ShapeDtypeStruct((L, PER), F32)
    big = jax.ShapeDtypeStruct((L, PER, FL), F32)
    vm = pl.BlockSpec(memory_space=pltpu.VMEM)
    any_ = pl.BlockSpec(memory_space=pl.ANY)
    N, W = dim["N"], dim["W"]
    got = pl.pallas_call(
        functools.partial(finish_kernel, dim),
        out_shape=(
            jax.ShapeDtypeStruct(out.shape, BF), jax.ShapeDtypeStruct(gtok.shape, F32),
            jax.ShapeDtypeStruct((PER, TS), F32), vec, vec,
            jax.ShapeDtypeStruct((L, 3, PER, HL), F32), jax.ShapeDtypeStruct((L, HL, PER), F32),
            vec, vec, vec, big, vec, big, vec),
        in_specs=[any_, any_, vm, any_],
        out_specs=(any_, any_) + (vm,) * 8 + (any_, vm, any_, vm),
        scratch_shapes=[
            pltpu.VMEM((L, 3, PER, FL), F32), pltpu.VMEM(out.shape, BF), pltpu.VMEM(gtok.shape, F32),
            pltpu.VMEM((2, N, W), F32), pltpu.SemaphoreType.DMA((3 * L + 2,)), pltpu.SemaphoreType.DMA((2 * L + 2,))],
        name="finish",
    )(out, gtok, sx, g)
    got = list(got)
    got[2] = jnp.transpose(got[2])
    got[5] = jnp.transpose(got[5], (0, 2, 1, 3))
    got[12] = jnp.transpose(got[12], (0, 2, 1))
    return tuple(got)


def solution(mesh):
    placed = (
        P(("dp", "tensor"), None), P("dp"), P("dp"), P(), P(), P(),
        P(None, None, None, "tensor"), P(None, "tensor", None), P(), P(), P(),
        P(None, None, "tensor"), P(None, "tensor"), P(None, "tensor", None), P(),
        P(("dp", "tensor"), None),
    )
    return jax.shard_map(
        local,
        mesh=mesh,
        in_specs=placed,
        out_specs=(
            P(("dp", "tensor"), None), P(("dp", "tensor"), None), P(None, "dp"), P(None, "dp"), P(None, "dp"),
            P(None, "dp", None, "tensor"), P(None, "tensor", "dp"), P(None, "dp"), P(None, "dp"), P(None, "dp"),
            P(None, "dp", "tensor"), P(None, ("tensor", "dp")), P(None, "tensor", "dp"), P(None, "dp"),
        ),
        check_vma=False,
    )
```

```python
import functools

import jax
import jax.numpy as jnp
from jax import lax
from jax.experimental import pallas as pl
from jax.experimental.pallas import tpu as pltpu
from jax.sharding import PartitionSpec as P

HEAD_DIM = 64
EPSILON = 1e-05
NEGATIVE = -1e30
MESH = pl.DeviceIdType.MESH
BF = jnp.bfloat16
F32 = jnp.float32
INV_SQRT2 = 0.7071067811865476
INV_SQRT2PI = 0.3989422804014327

NN = (((1,), (0,)), ((), ()))
NT = (((1,), (1,)), ((), ()))
TN = (((0,), (0,)), ((), ()))


def mm(a, b, dims=NN):
    return lax.dot_general(a, b, dims, preferred_element_type=F32)


def step_kernel(dim, *refs):
    (
        ts_ref, bs_ref, g1_in, b1_in, bo_in, g2_in, b2_in, bd_in, bup_in,
        tok_in, cot_in, table_h, wqkv_h, wout_h, wup_h, wdown_h,
        out_o, gtok_o, smallx_o, g_o,
        wqkv, wout, wup, wdown, tokf, cotf,
        a_b, a2_b, g_b, gp_b, qkvT, kv_b, oT_b, lse_b, h_b, m_b,
        df_b, dz_b, dh_b, doT_b, dqT_b, dkv_acc,
        ysend, yrecv, csend, crecv, part, s_b, p_b, ds_b, gstage,
        small, smallr, smallx, smallp, emb_b,
        send1, recv1, own1, send2, recv2, fstage,
        wsem, tsem_s, tsem_r, ysem_s, ysem_r, casem_s, casem_r, cpsem_s, cpsem_r,
        lsem, osem, gsem, ssem, x1s, x1r,
        r1s, r1r, r2s, r2r, turned,
    ) = refs
    D, FL, HL, R, L = dim["D"], dim["FL"], dim["HL"], dim["R"], dim["L"]
    N, NI, NO, PER, FUSED = dim["N"], dim["NI"], dim["NO"], dim["PER"], dim["FUSED"]
    HP = HL
    vecs = (g1_in, b1_in, bo_in, g2_in, b2_in, bd_in)

    def vrow(i, l):
        return vecs[i][l : l + 1, :].astype(F32)

    T = 4 * R
    NH = HL // HEAD_DIM
    CH = 2 * R
    NB = D // 256
    FB = FL // 256
    t = lax.axis_index("tensor")
    d = lax.axis_index("dp")
    di = lax.rem(d, NI)
    do_ = lax.div(d, NI)
    y = lax.div(t, 2)
    c = lax.rem(t, 2)
    ypeer = lax.rem(t + 2, 4)
    cpeer = t + 1 - 2 * c
    dpeer = lax.rem(cpeer + 2, 4)

    def own(r):
        return pl.multiple_of(R * (2 * r + c), R)

    def oth(r):
        return pl.multiple_of(R * (2 * r + 1 - c), R)

    def remote(src, dst, ss, rs, peer):
        return pltpu.make_async_remote_copy(
            src_ref=src, dst_ref=dst, send_sem=ss, recv_sem=rs,
            device_id={"tensor": peer}, device_id_type=MESH)

    def dp_remote(src, dst, ss, rs, peer):
        return pltpu.make_async_remote_copy(
            src_ref=src, dst_ref=dst, send_sem=ss, recv_sem=rs,
            device_id={"dp": peer}, device_id_type=MESH)

    bar = pltpu.get_barrier_semaphore()

    def greet(k, cy):
        pl.semaphore_signal(bar, inc=1, device_id={"dp": lax.rem(d + k, N)}, device_id_type=MESH)
        return cy

    lax.fori_loop(1, N, greet, 0)
    pl.semaphore_signal(bar, inc=1, device_id={"tensor": ypeer}, device_id_type=MESH)
    pl.semaphore_signal(bar, inc=1, device_id={"tensor": cpeer}, device_id_type=MESH)
    pl.semaphore_signal(bar, inc=1, device_id={"tensor": dpeer}, device_id_type=MESH)

    loc = [pltpu.make_async_copy(tok_in, tokf.at[y], lsem.at[0]),
           pltpu.make_async_copy(cot_in, cotf.at[y], lsem.at[1]),
           pltpu.make_async_copy(table_h, df_b.at[pl.ds(0, dim["TS"]), :], lsem.at[2])]
    for cp in loc:
        cp.start()
    wcopies = []
    for l in range(L):
        row = []
        for i, (src, dst) in enumerate(((wqkv_h, wqkv), (wout_h, wout), (wup_h, wup), (wdown_h, wdown))):
            cp = pltpu.make_async_copy(src.at[l], dst.at[l], wsem.at[l, i])
            cp.start()
            row.append(cp)
        wcopies.append(row)
    pl.semaphore_wait(bar, N + 2)
    tcp = [remote(tok_in, tokf.at[y], tsem_s.at[0], tsem_r.at[0], ypeer),
           remote(cot_in, cotf.at[y], tsem_s.at[1], tsem_r.at[1], ypeer)]
    tcp[0].start()

    small[...] = jnp.zeros_like(small)
    bs = bs_ref[0]
    loc[2].wait()
    pick = (lax.broadcasted_iota(jnp.int32, (8, dim["TS"]), 1) == ts_ref[0]).astype(BF)
    emb_b[...] = mm(pick, df_b[0 : dim["TS"], :])

    def y_copy(par, r, i):
        rows = pl.ds(i, BLK)
        b = i // BLK
        return remote(ysend.at[par, r, rows, :], yrecv.at[par, r, rows, :],
                      ysem_s.at[par, r, b], ysem_r.at[par, r, b], ypeer)

    def tile_copy(buf, r, i, q):
        rows = pl.ds(pl.multiple_of(own(r) + i, BLK), BLK)
        b = i // BLK
        return remote(buf.at[rows, :], buf.at[rows, :], casem_s.at[q, b], casem_r.at[q, b], cpeer)

    class Tile:
        def __init__(self, buf, r, q=None):
            self.copy = lambda i: tile_copy(buf, r, i, r if q is None else q)

        def wait_recv(self):
            for i in range(0, R, BLK):
                self.copy(i).wait_recv()

        def wait_send(self):
            for i in range(0, R, BLK):
                self.copy(i).wait_send()

    def part_copy(r):
        return remote(csend.at[r], crecv.at[r], cpsem_s.at[r], cpsem_r.at[r], cpeer)

    BLK = dim["BLK"]

    def rowloop(fn, init=0):
        return lax.fori_loop(0, R // BLK, lambda i, cy: fn(pl.multiple_of(i * BLK, BLK), cy), init)

    def ln_stats(x):
        mean = jnp.sum(x, axis=-1, keepdims=True) * (1.0 / D)
        xc = x - mean
        var = jnp.sum(xc * xc, axis=-1, keepdims=True) * (1.0 / D)
        return xc, lax.rsqrt(var + EPSILON)

    def enter_fwd(l, r, src, gi, dst_h, dst_a, par=None):
        gain = vrow(gi, l)
        bias = vrow(gi + 1, l)
        cp = Tile(dst_a.at[l], r)

        def blk(i, cy):
            if par is not None:
                wait_y(par, r, i)
            x = src(i)
            dst_h[l, r, pl.ds(i, BLK), :] = x
            xc, rstd = ln_stats(x)
            dst_a[l, pl.ds(pl.multiple_of(own(r) + i, BLK), BLK), :] = (xc * rstd * gain + bias).astype(BF)
            cp.copy(i).start()
            return cy

        rowloop(blk)
        return cp

    def ysum(par, r, i):
        return ysend[par, r, pl.ds(i, BLK), :].astype(F32) + yrecv[par, r, pl.ds(i, BLK), :].astype(F32)

    def wait_y(par, r, i):
        cp = y_copy(par, r, i)
        cp.wait_send()
        cp.wait_recv()

    def wait_mine(par, i):
        y_copy(par, 1 - y, i).wait_send()
        y_copy(par, y, i).wait_recv()

    def send_partner(r, fill):
        fill(csend.at[r])
        cp = part_copy(r)
        cp.start()
        return cp

    def combine(par, r, cp, last=False):
        cp.wait_recv()

        def blk(i, cy):
            v = part[pl.ds(i, BLK), :] + crecv[r, pl.ds(i, BLK), :].astype(F32)
            ysend[par, r, pl.ds(i, BLK), :] = v.astype(BF)
            if last:
                @pl.when(y == 1 - r)
                def _():
                    y_copy(par, r, i).start()
            else:
                y_copy(par, r, i).start()
            return cy

        rowloop(blk)
        cp.wait_send()

    def qkv_tile(l, q0):
        q = mm(wqkv[l, 0:HP, :], a_b[l, pl.ds(q0, R), :], NT).astype(BF)
        qkvT[l, 0:HP, pl.ds(q0, R)] = q * jnp.asarray(HEAD_DIM ** -0.5, BF)
        for cc in (1, 2):
            v = mm(wqkv[l, cc * HP : cc * HP + HP, :], a_b[l, pl.ds(q0, R), :], NT)
            qkvT[l, cc * HP : cc * HP + HP, pl.ds(q0, R)] = v.astype(BF)
            kv_b[l, cc - 1, pl.ds(q0, R), :] = v.T.astype(BF)

    def hmask(h):
        rows = lax.broadcasted_iota(jnp.int32, (HP, R), 0)
        return (rows >= h * HEAD_DIM) & (rows < (h + 1) * HEAD_DIM)

    def visible(r, kb, q0):
        key = lax.broadcasted_iota(jnp.int32, (R, R), 0) + (CH * r + kb * R)
        qry = lax.broadcasted_iota(jnp.int32, (R, R), 1) + q0
        return key <= (qry | (bs - 1))

    def att_fwd_tile(l, r, q0):
        KB = 2 * (r + 1)

        def head(h, cy):
            qm = jnp.where(hmask(h), qkvT[l, 0:HP, pl.ds(q0, R)].astype(F32), 0.0).astype(BF)
            top = None
            for kb in range(KB):
                s = mm(kv_b[l, 0, kb * R : kb * R + R, :], qm)
                if kb >= 2 * r:
                    s = jnp.where(visible(r, kb - 2 * r, q0), s, NEGATIVE)
                s_b[kb * R : kb * R + R, :] = s
                mx = jnp.max(s, axis=0, keepdims=True)
                top = mx if top is None else jnp.maximum(top, mx)
            tot = None
            for kb in range(KB):
                e = jnp.exp(s_b[kb * R : kb * R + R, :] - top)
                p_b[kb * R : kb * R + R, :] = e.astype(BF)
                sm = jnp.sum(e, axis=0, keepdims=True)
                tot = sm if tot is None else tot + sm
            hr = pl.multiple_of(h * HEAD_DIM, HEAD_DIM)
            o = mm(qkvT[l, pl.ds(pl.multiple_of(2 * HP + hr, HEAD_DIM), HEAD_DIM), 0 : KB * R], p_b[0 : KB * R, :])
            oT_b[l, pl.ds(hr, HEAD_DIM), pl.ds(q0, R)] = (o * (1.0 / tot)).astype(BF)
            lse_b[l, pl.ds(h, 1), pl.ds(q0, R)] = top + jnp.log(tot)
            return cy

        lax.fori_loop(0, NH, head, 0)

    def nblocks(fn, n):
        for i in range(n):
            fn(i * 256)

    def out_tile(l, q0, dst):
        o = oT_b[l, :, pl.ds(q0, R)].astype(F32).T.astype(BF)

        def one(n):
            dst[:, n : n + 256] = mm(o, wout[l, :, n : n + 256]).astype(dst.dtype)

        nblocks(one, NB)

    def up_tile(l, q0):
        def one(n, cy):
            n = pl.multiple_of(n * 256, 256)
            u = mm(a2_b[l, pl.ds(q0, R), :], wup[l, :, pl.ds(n, 256)]) + bup_in[l : l + 1, pl.ds(n, 256)].astype(F32)
            phi = 0.5 * (1.0 + lax.erf(u * INV_SQRT2))
            g_b[l, pl.ds(q0, R), pl.ds(n, 256)] = (u * phi).astype(BF)
            gp = phi + u * (jnp.exp(u * u * -0.5) * INV_SQRT2PI)
            gp_b[l, pl.ds(q0, R), pl.ds(n, 256)] = gp.astype(BF)
            return cy

        lax.fori_loop(0, FB, one, 0)

    def down_tile(l, q0, dst):
        def one(n):
            dst[:, n : n + 256] = mm(g_b[l, pl.ds(q0, R), :], wdown[l, :, n : n + 256]).astype(dst.dtype)

        nblocks(one, NB)

    def own_first(r, tile_cp, fn):
        def tile(i, cy):
            if tile_cp is not None:
                @pl.when(i == 1)
                def _():
                    tile_cp.wait_recv()

            fn(pl.multiple_of(R * (2 * r + c + i * (1 - 2 * c)), R))
            return cy

        lax.fori_loop(0, 2, tile, 0)

    def att_fwd(l, r, tile_cp):
        own_first(r, tile_cp, lambda q0: qkv_tile(l, q0))
        cp = part_copy(r)

        def tile(i, cy):
            att_fwd_tile(l, r, pl.multiple_of(R * (2 * r + 1 - c + i * (2 * c - 1)), R))

            @pl.when(i == 0)
            def _():
                out_tile(l, oth(r), csend.at[r])
                cp.start()

            return cy

        lax.fori_loop(0, 2, tile, 0)
        out_tile(l, own(r), part)
        tile_cp.wait_send()
        combine(0, r, cp)

    def ffn_fwd(l, r, tile_cp):
        own_first(r, tile_cp, lambda q0: up_tile(l, q0))
        cp = send_partner(r, lambda ref: down_tile(l, oth(r), ref))
        down_tile(l, own(r), part)
        tile_cp.wait_send()
        combine(1, r, cp, l == L - 1)

    def finish_output():
        bd = vrow(5, L - 1)

        def blk(i, cy):
            wait_mine(1, i)
            v = m_b[L - 1, y, pl.ds(i, BLK), :] + (ysum(1, y, i) + bd)
            tokf[y, pl.ds(i, BLK), :] = v.astype(BF)
            return cy

        rowloop(blk)

    def ln_bwd(l, r, par, gi, xbuf, emit, mine=False):
        gain = vrow(gi, l)

        def blk(i, cy):
            dg, db = cy
            if mine:
                wait_mine(par, i)
            else:
                wait_y(par, r, i)
            x = xbuf[l, r, pl.ds(i, BLK), :]
            dy = ysum(par, r, i)
            xc, rstd = ln_stats(x)
            xh = xc * rstd
            t1 = dy * gain
            m1 = jnp.sum(t1, axis=-1, keepdims=True) * (1.0 / D)
            m2 = jnp.sum(t1 * xh, axis=-1, keepdims=True) * (1.0 / D)
            dx = rstd * (t1 - m1 - xh * m2)
            emit(i, dx)
            dg = dg + jnp.sum(dy * xh, axis=0, keepdims=True)
            db = db + jnp.sum(dy, axis=0, keepdims=True)
            return (dg, db)

        z = jnp.zeros((1, D), F32)
        dg, db = rowloop(blk, (z, z))
        small[l, gi : gi + 1, :] = small[l, gi : gi + 1, :] + dg
        small[l, gi + 1 : gi + 2, :] = small[l, gi + 1 : gi + 2, :] + db

    def colsum_own(buf, r, l, row):
        def blk(i, cy):
            return cy + jnp.sum(buf[pl.ds(pl.multiple_of(own(r) + i, BLK), BLK), :].astype(F32), axis=0, keepdims=True)

        v = rowloop(blk, jnp.zeros((1, D), F32))
        small[l, row : row + 1, :] = small[l, row : row + 1, :] + v

    def enter_b1(l, r):
        cp = Tile(df_b, r, 2 + r if l == L - 1 else r)
        if l == L - 1:
            def blk(i, cy):
                v = cotf[r, pl.ds(i, BLK), :]
                dh_b[r, pl.ds(i, BLK), :] = v.astype(F32)
                df_b[pl.ds(pl.multiple_of(own(r) + i, BLK), BLK), :] = v
                cp.copy(i).start()
                return cy

            rowloop(blk)
        else:
            def emit(i, dx):
                v = dh_b[r, pl.ds(i, BLK), :] + dx
                dh_b[r, pl.ds(i, BLK), :] = v
                df_b[pl.ds(pl.multiple_of(own(r) + i, BLK), BLK), :] = v.astype(BF)
                cp.copy(i).start()

            ln_bwd(l + 1, r, 0, 0, h_b, emit)
        colsum_own(df_b, r, l, 5)
        return cp

    def du_tile(l, q0):
        def one(n, cy):
            n = pl.multiple_of(n * 256, 256)
            dg = mm(df_b[pl.ds(q0, R), :], wdown[l, pl.ds(n, 256), :], NT)
            du = (dg * gp_b[l, pl.ds(q0, R), pl.ds(n, 256)].astype(F32)).astype(BF)
            gp_b[l, pl.ds(q0, R), pl.ds(n, 256)] = du
            small[l, 7:8, pl.ds(n, 256)] = small[l, 7:8, pl.ds(n, 256)] + jnp.sum(du.astype(F32), axis=0, keepdims=True)
            return cy

        lax.fori_loop(0, FB, one, 0)

    def da2_tile(l, q0, dst):
        def one(n):
            dst[:, n : n + 256] = mm(gp_b[l, pl.ds(q0, R), :], wup[l, n : n + 256, :], NT).astype(dst.dtype)

        nblocks(one, NB)

    def ffn_bwd(l, r, tile_cp):
        own_first(r, tile_cp, lambda q0: du_tile(l, q0))
        if l == L - 1 and r == 1:
            pl.semaphore_wait(turned, 1)
        cp = send_partner(r, lambda ref: da2_tile(l, oth(r), ref))
        da2_tile(l, own(r), part)
        if tile_cp is not None:
            tile_cp.wait_send()
        combine(2, r, cp)

    def enter_b2(l, r):
        cp = Tile(dz_b, r)

        def emit(i, dx):
            v = dh_b[r, pl.ds(i, BLK), :] + dx
            dh_b[r, pl.ds(i, BLK), :] = v
            dz_b[pl.ds(pl.multiple_of(own(r) + i, BLK), BLK), :] = v.astype(BF)
            cp.copy(i).start()

        ln_bwd(l, r, 2, 3, m_b, emit)
        colsum_own(dz_b, r, l, 2)
        return cp

    def do_tile(l, q0):
        doT_b[:, pl.ds(q0, R)] = mm(wout[l], dz_b[pl.ds(q0, R), :], NT).astype(BF)

    def att_bwd_tile(l, r, q0):
        KB = 2 * (r + 1)
        KN = KB * R

        def head(h, cy):
            hr = pl.multiple_of(h * HEAD_DIM, HEAD_DIM)
            hm = hmask(h)
            qm = jnp.where(hm, qkvT[l, 0:HP, pl.ds(q0, R)].astype(F32), 0.0).astype(BF)
            dom = jnp.where(hm, doT_b[:, pl.ds(q0, R)].astype(F32), 0.0).astype(BF)
            do_h = doT_b[pl.ds(hr, HEAD_DIM), pl.ds(q0, R)]
            q_h = qkvT[l, pl.ds(hr, HEAD_DIM), pl.ds(q0, R)]
            o_h = oT_b[l, pl.ds(hr, HEAD_DIM), pl.ds(q0, R)]
            dsum = jnp.sum(do_h.astype(F32) * o_h.astype(F32), axis=0, keepdims=True)
            lse = lse_b[l, pl.ds(h, 1), pl.ds(q0, R)]
            for kb in range(KB):
                ks = slice(kb * R, kb * R + R)
                s = mm(kv_b[l, 0, ks, :], qm)
                p = jnp.exp(s - lse)
                if kb >= 2 * r:
                    p = jnp.where(visible(r, kb - 2 * r, q0), p, 0.0)
                p_b[ks, :] = p.astype(BF)
                dp = mm(kv_b[l, 1, ks, :], dom)
                ds_b[ks, :] = (p * (dp - dsum)).astype(BF)
            dkv_acc[1, pl.ds(hr, HEAD_DIM), 0:KN] = dkv_acc[1, pl.ds(hr, HEAD_DIM), 0:KN] + mm(do_h, p_b[0:KN, :], NT)
            dkv_acc[0, pl.ds(hr, HEAD_DIM), 0:KN] = dkv_acc[0, pl.ds(hr, HEAD_DIM), 0:KN] + mm(q_h, ds_b[0:KN, :], NT)
            k_h = qkvT[l, pl.ds(pl.multiple_of(HP + hr, HEAD_DIM), HEAD_DIM), 0:KN]
            dq = mm(k_h, ds_b[0:KN, :]) * (HEAD_DIM ** -0.5)
            dqT_b[pl.ds(hr, HEAD_DIM), pl.ds(q0, R)] = dq.astype(BF)
            return cy

        lax.fori_loop(0, NH, head, 0)

    def da_tile(l, q0, dst):
        dqkv = dqT_b[:, pl.ds(q0, R)].astype(F32).T.astype(BF)

        def one(n):
            dst[:, n : n + 256] = mm(dqkv, wqkv[l, :, n : n + 256]).astype(dst.dtype)

        nblocks(one, NB)

    def att_bwd(l, r, tile_cp):
        def both(q0):
            do_tile(l, q0)
            att_bwd_tile(l, r, q0)

        own_first(r, tile_cp, both)
        cs = slice(CH * r, CH * r + CH)
        for j in range(2):
            dqT_b[HP * (j + 1) : HP * (j + 1) + HL, cs] = dkv_acc[j, 0:HL, cs].astype(BF)
        cp = send_partner(r, lambda ref: da_tile(l, oth(r), ref))
        da_tile(l, own(r), part)
        tile_cp.wait_send()
        combine(0, r, cp, l == 0)

    WHOLE = (0, FL, 0)
    HALF = ((0, FL // 2, 0), (FL // 2, FL - FL // 2, 3))

    def r1_copy(j, k, span):
        c0, w, extra = span
        q = j + extra
        peer = do_ * NI + lax.rem(di + k, NI)
        return dp_remote(send1.at[j, k - 1, :, c0 : c0 + w], recv1.at[j, k - 1, :, c0 : c0 + w],
                         r1s.at[q, k - 1], r1r.at[q, k - 1], peer)

    def r2_copy(j, k, span):
        c0, w, extra = span
        q = j + extra
        peer = lax.rem(do_ + k, NO) * NI + di
        return dp_remote(send2.at[j, k - 1, :, c0 : c0 + w], recv2.at[j, k - 1, :, c0 : c0 + w],
                         r2s.at[q, k - 1], r2r.at[q, k - 1], peer)

    def g_copy(l, j, span):
        c0, w, extra = span
        q = l * 6 + j + extra
        return pltpu.make_async_copy(fstage.at[l, j, :, c0 : c0 + w], g_o.at[l, j, :, c0 : c0 + w], gsem.at[q])

    def piece(q):
        return pl.ds(pl.multiple_of(q * PER, PER), PER)

    def rs_start(l, j, span=WHOLE):
        c0, w, _ = span
        cols = slice(c0, c0 + w)
        if not FUSED:
            cp = pltpu.make_async_copy(gstage.at[:, cols], g_o.at[l, j, :, cols], gsem.at[0])
            cp.start()
            cp.wait()
            return
        for k in range(1, NI):
            for oo in range(NO):
                send1[j, k - 1, oo * PER : oo * PER + PER, cols] = gstage[piece(oo * NI + lax.rem(di + k, NI)), cols].astype(BF)
            r1_copy(j, k, span).start()
        for oo in range(NO):
            own1[j, oo * PER : oo * PER + PER, cols] = gstage[piece(oo * NI + di), cols]

    def rs_mid(l, j, span=WHOLE):
        c0, w, _ = span
        cols = slice(c0, c0 + w)
        if not FUSED:
            return
        for k in range(1, NI):
            cp = r1_copy(j, k, span)
            cp.wait_send()
            cp.wait_recv()
        for kk in range(NO - 1, -1, -1):
            rows = piece(lax.rem(do_ + kk, NO))
            v = own1[j, rows, cols]
            for k in range(1, NI):
                v = v + recv1[j, k - 1, rows, cols].astype(F32)
            if kk == 0:
                own1[j, rows, cols] = v
            else:
                send2[j, kk - 1, :, cols] = v.astype(BF)
                r2_copy(j, kk, span).start()

    def rs_fin(l, j, span=WHOLE):
        c0, w, _ = span
        cols = slice(c0, c0 + w)
        if not FUSED:
            return
        v = own1[j, piece(do_), cols]
        for kk in range(1, NO):
            cp = r2_copy(j, kk, span)
            cp.wait_send()
            cp.wait_recv()
            v = v + recv2[j, kk - 1, :, cols].astype(F32)
        fstage[l, j, :, cols] = v
        g_copy(l, j, span).start()

    def wgrad_ffn(l, lhs, rhs, rows=slice(None), add=False):
        def one(n, cy):
            ns = pl.ds(pl.multiple_of(n * 256, 256), 256)
            lt = lhs[rows, ns].astype(F32).T.astype(BF)
            for f in range(FB):
                fs = slice(f * 256, f * 256 + 256)
                v = mm(lt, rhs[rows, fs])
                gstage[ns, fs] = gstage[ns, fs] + v if add else v
            return cy

        lax.fori_loop(0, NB, one, 0)

    def wgrad_att(l, span):
        lo, hi = span[0], span[0] + span[1]
        q = min(hi, 3 * HL)

        def one(n, cy):
            ns = pl.ds(pl.multiple_of(n * 256, 256), 256)
            s_b[lo:q, :] = mm(dqT_b[lo:q, :], a_b[l, :, ns])
            if hi > q:
                s_b[q:hi, :] = mm(oT_b[l], dz_b[:, ns])
            gstage[ns, lo:hi] = s_b[lo:hi, :].T
            return cy

        lax.fori_loop(0, NB, one, 0)

    for l in range(L):
        for r in range(2):
            if l == 0:
                if r == 0:
                    for cp in (loc[0], wcopies[0][0]):
                        cp.wait()
                    tcp[0].wait()
                    tcp[1].start()
                src = lambda i, r=r: tokf[r, pl.ds(i, BLK), :].astype(F32) + emb_b[0:1, :]
            else:
                bd = vrow(5, l - 1)
                src = lambda i, r=r, l=l, bd=bd: m_b[l - 1, r, pl.ds(i, BLK), :] + (ysum(1, r, i) + bd)
            if r == 0 and l > 0:
                wcopies[l][0].wait()
            cp = enter_fwd(l, r, src, 0, h_b, a_b, 1 if l > 0 else None)
            if r == 0:
                wcopies[l][1].wait()
            att_fwd(l, r, cp)
        for r in range(2):
            if l == L - 1 and r == 0:
                loc[1].wait()
                tcp[1].wait()
                b1 = [enter_b1(l, 0), enter_b1(l, 1)]
            elif l == L - 1:
                b1[0].wait_recv()
                wgrad_ffn(l, df_b, g_b.at[l], slice(0, CH))
            bo = vrow(2, l)
            src = lambda i, r=r, l=l, bo=bo: h_b[l, r, pl.ds(i, BLK), :] + (ysum(0, r, i) + bo)
            if r == 0:
                wcopies[l][2].wait()
                wcopies[l][3].wait()
            cp = enter_fwd(l, r, src, 3, m_b, a2_b, 0)
            ffn_fwd(l, r, cp)

    pl.semaphore_signal(turned, inc=1, device_id={"tensor": cpeer}, device_id_type=MESH)
    b1[1].wait_recv()
    wgrad_ffn(L - 1, df_b, g_b.at[L - 1], slice(CH, T), True)
    rs_start(L - 1, 2)
    for cp in b1:
        cp.wait_send()
    for l in range(L - 1, -1, -1):
        last = l == L - 1
        spans = (WHOLE,) if l > 0 else HALF
        for r in (1, 0):
            ffn_bwd(l, r, None if last else enter_b1(l, r))
            if not last:
                rs_fin(l + 1, 1 + r)
        if last:
            finish_output()
        else:
            rs_mid(l + 1, 0)
            wgrad_ffn(l, df_b, g_b.at[l])
            for span in spans:
                rs_start(l, 2, span)
        wgrad_ffn(l, a2_b.at[l], gp_b.at[l])
        for span in spans:
            rs_start(l, 1, span)
        dkv_acc[...] = jnp.zeros_like(dkv_acc)
        for r in (1, 0):
            cp = enter_b2(l, r)
            if last and r == 1:
                rs_mid(l, 2)
            att_bwd(l, r, cp)
            if not last and r == 1:
                rs_fin(l + 1, 0)
                for span in spans:
                    rs_mid(l, 2, span)
        if last:
            rs_mid(l, 1)
            wgrad_att(l, WHOLE)
            rs_start(l, 0)
        else:
            wgrad_att(l, HALF[0])
            rs_mid(l, 1, HALF[0])
            rs_start(l, 0, HALF[0])
            wgrad_att(l, HALF[1])
            rs_start(l, 0, HALF[1])
            rs_mid(l, 1, HALF[1])
    ocp = pltpu.make_async_copy(tokf.at[y], out_o, osem.at[0])
    ocp.start()
    for span in HALF:
        rs_fin(0, 2, span)
    rs_mid(0, 0, HALF[0])

    def emit(i, dx):
        v = dh_b[y, pl.ds(i, BLK), :] + dx
        dh_b[y, pl.ds(i, BLK), :] = v
        small[0, 6:7, :] = small[0, 6:7, :] + jnp.sum(v, axis=0, keepdims=True)

    ln_bwd(0, y, 0, 0, h_b, emit, True)
    gcp = pltpu.make_async_copy(dh_b.at[y], gtok_o, osem.at[1])
    gcp.start()
    scps = [remote(small, smallr.at[0:L], ssem.at[0], ssem.at[3], cpeer),
            remote(small.at[0], smallr.at[L], ssem.at[1], ssem.at[4], ypeer),
            remote(small.at[0], smallr.at[L + 1], ssem.at[2], ssem.at[5], dpeer)]
    for scp in scps:
        scp.start()
    for scp in scps:
        scp.wait()
    which = lax.broadcasted_iota(jnp.int32, (8, D), 0)
    small[0] = small[0] + jnp.where((which < 2) | (which == 6), smallr[L] + smallr[L + 1], 0.0)
    for l in range(L):
        small[l] = small[l] + jnp.where(which < 7, smallr[l], 0.0)
    small[1, 6:7, :] = jnp.full((1, D), ts_ref[0].astype(F32), F32)

    def x_copy(k):
        return dp_remote(smallp.at[k], smallx.at[d], x1s.at[k], x1r.at[k], lax.rem(d + k, N))

    def columns(k):
        turn = lax.rem(D - PER * lax.rem(d + k, N), D)
        return [pltpu.roll(small[l], turn, 1)[:, 0 : smallx.shape[3]] for l in range(L)]

    def x_go(k, cy):
        for l, v in enumerate(columns(k)):
            smallp[k, l] = v
        x_copy(k).start()
        return cy

    def x_wait(k, cy):
        cp = x_copy(k)
        cp.wait_send()
        cp.wait_recv()
        return cy

    lax.fori_loop(1, N, x_go, 0)
    for l, v in enumerate(columns(0)):
        smallx[d, l] = v
    rs_mid(0, 0, HALF[1])
    for span in HALF:
        rs_fin(0, 1, span)
    rs_fin(0, 0, HALF[0])
    lax.fori_loop(1, N, x_wait, 0)
    smallx_o[...] = smallx[...]
    rs_fin(0, 0, HALF[1])
    ocp.wait()
    gcp.wait()
    if FUSED:
        for l in range(L):
            for j in range(3):
                for span in HALF if l == 0 else (WHOLE,):
                    g_copy(l, j, span).wait()


def finish_kernel(dim, out_i, gtok_i, sx, g_i, out_o, gtok_o, table_o, dg1, db1, gq, go, dbo, dg2, db2, gup, dbup, gdown, dbd,
                  g_b, out_b, gtok_b, rows_b, sem_i, sem_o):
    FL, HL, L, PER, N, TS = dim["FL"], dim["HL"], dim["L"], dim["PER"], dim["N"], dim["TS"]
    ins = []
    for j in range(3):
        for l in range(L):
            ins.append(pltpu.make_async_copy(g_i.at[l, j], g_b.at[l, j], sem_i.at[l * 3 + j]))
    order = ((out_i, out_b, out_o), (gtok_i, gtok_b, gtok_o))
    for i, (src, buf, _) in enumerate(order):
        ins.append(pltpu.make_async_copy(src, buf, sem_i.at[3 * L + i]))
    for cp in ins:
        cp.start()
    for l in range(L):
        tot = sx[0, l]
        for q in range(1, N):
            tot = tot + sx[q, l]
        for i, ref in enumerate((dg1, db1, dbo, dg2, db2, dbd)):
            ref[l : l + 1, :] = tot[i : i + 1, 0:PER]
        dbup[l : l + 1, :] = tot[7:8, 0:PER]
    for q in range(N):
        rows_b[0, q : q + 1, :] = sx[q, 0, 6:7, :]
        rows_b[1, q : q + 1, :] = sx[q, 1, 6:7, :]
    step = rows_b[1, :, 0:1]
    pick = jnp.where(lax.broadcasted_iota(jnp.int32, (N, TS), 1).astype(F32) == step, 1.0, 0.0)
    table_o[...] = lax.dot_general(rows_b[0], pick, TN, precision=lax.Precision.HIGHEST, preferred_element_type=F32)[0:PER, :]
    for l in range(L):
        ins[l].wait()
        ga = g_b[l, 0]
        for cc in range(3):
            gq[l, cc] = ga[:, cc * HL : cc * HL + HL]
        gt = jnp.concatenate([ga, jnp.zeros((-PER % 128, 4 * HL), F32)], axis=0).T
        go[l] = gt[3 * HL : 4 * HL, 0:PER]
    outs = []
    for j, ref in ((1, gup), (2, gdown)):
        for l in range(L):
            ins[j * L + l].wait()
            cp = pltpu.make_async_copy(g_b.at[l, j], ref.at[l], sem_o.at[l * 2 + j - 1])
            cp.start()
            outs.append(cp)
    for i, (_, buf, dst) in enumerate(order):
        ins[3 * L + i].wait()
        cp = pltpu.make_async_copy(buf, dst, sem_o.at[2 * L + i])
        cp.start()
        outs.append(cp)
    for cp in outs:
        cp.wait()


def split_of(n):
    inner = 2 ** ((n.bit_length() - 1) // 2)
    return inner, n // inner


def run_step(ts, bs, vecs, bup, tok, cot, table, wqkv, wout, wup, wdown):
    R, D = tok.shape
    L, _, FL = wup.shape
    HL = wout.shape[1]
    N = lax.axis_size("dp")
    NI, NO = split_of(N)
    PER = D // N
    FUSED = PER % 16 == 0
    assert lax.axis_size("tensor") == 4 and ts.shape[0] == 1 and FL == D == 4 * HL and L > 1 and R == 256
    T = 4 * R
    W = -(-PER // 128) * 128
    BLK = min(R, 128)
    HB = R // BLK
    dim = dict(D=D, FL=FL, HL=HL, R=R, L=L, BLK=BLK, W=W, N=N, NI=NI, NO=NO, PER=PER, FUSED=FUSED, TS=table.shape[0])
    vm = pl.BlockSpec(memory_space=pltpu.VMEM)
    sm = pl.BlockSpec(memory_space=pltpu.SMEM)
    any_ = pl.BlockSpec(memory_space=pl.ANY)
    dma = pltpu.SemaphoreType.DMA
    V = pltpu.VMEM
    J = 3 if FUSED else 1
    PR = PER if FUSED else 16
    ones = max(NI - 1, 1)
    outs = max(NO - 1, 1)
    kept = (L, 3, PER, FL) if FUSED else (L, 3, D, FL)
    return dim, pl.pallas_call(
        functools.partial(step_kernel, dim),
        out_shape=(
            jax.ShapeDtypeStruct((R, D), BF),
            jax.ShapeDtypeStruct((R, D), F32),
            jax.ShapeDtypeStruct((N, L, 8, W), F32),
            jax.ShapeDtypeStruct(kept, F32),
        ),
        in_specs=[sm, sm] + [vm] * 7 + [any_] * 7,
        out_specs=(any_, any_, vm, any_),
        scratch_shapes=[
            V((L, 3 * HL, D), BF), V((L, HL, D), BF), V((L, D, FL), BF), V((L, FL, D), BF),
            V((2, R, D), BF), V((2, R, D), BF),
            V((L, T, D), BF), V((L, T, D), BF), V((L, T, FL), BF), V((L, T, FL), BF),
            V((L, 3 * HL, T), BF), V((L, 2, T, HL), BF), V((L, HL, T), BF), V((L, 8, T), F32),
            V((L, 2, R, D), F32), V((L, 2, R, D), F32),
            V((T, D), BF), V((T, D), BF), V((2, R, D), F32),
            V((HL, T), BF), V((3 * HL, T), BF), V((2, HL, T), F32),
            V((3, 2, R, D), BF), V((3, 2, R, D), BF), V((2, R, D), BF), V((2, R, D), BF),
            V((R, D), F32), V((T, R), F32), V((T, R), BF), V((T, R), BF), V((D, FL), F32),
            V((L, 8, D), F32), V((L + 2, 8, D), F32), V((N, L, 8, W), F32), V((N, L, 8, W), F32), V((8, D), F32),
            V((J, ones, NO * PR, FL), BF), V((J, ones, NO * PR, FL), BF), V((J, NO * PR, FL), F32),
            V((J, outs, PR, FL), BF), V((J, outs, PR, FL), BF), V((L, J, PR, FL), F32),
            dma((L, 4)), dma((2,)), dma((2,)), dma((3, 2, HB)), dma((3, 2, HB)),
            dma((4, HB)), dma((4, HB)), dma((2,)), dma((2,)),
            dma((3,)), dma((2,)), dma((6 * L,)), dma((6,)), dma((N,)), dma((N,)),
            dma((6, ones)), dma((6, ones)), dma((6, outs)), dma((6, outs)), pltpu.SemaphoreType.REGULAR,
        ],
        compiler_params=pltpu.CompilerParams(
            collective_id=0, has_side_effects=True, vmem_limit_bytes=67043328),
        name="layers",
    )(ts, bs, *vecs, bup, tok, cot, table, wqkv, wout, wup, wdown)


def local(tokens, timestep, block_size, table, ln1_gain, ln1_bias, w_qkv, w_out, b_out,
          ln2_gain, ln2_bias, w_up, b_up, w_down, b_down, cotangent):
    L, D, _, HL = w_qkv.shape
    wq = jnp.transpose(w_qkv, (0, 2, 3, 1)).reshape(L, 3 * HL, D)
    vecs = (ln1_gain, ln1_bias, b_out, ln2_gain, ln2_bias, b_down)
    dim, (out, gtok, sx, g) = run_step(
        timestep, block_size, vecs, b_up, tokens, cotangent, table, wq, w_out, w_up, w_down)
    PER, FL, TS = dim["PER"], dim["FL"], dim["TS"]
    if not dim["FUSED"]:
        g = lax.psum_scatter(g, "dp", scatter_dimension=2, tiled=True)
    vec = jax.ShapeDtypeStruct((L, PER), F32)
    big = jax.ShapeDtypeStruct((L, PER, FL), F32)
    vm = pl.BlockSpec(memory_space=pltpu.VMEM)
    any_ = pl.BlockSpec(memory_space=pl.ANY)
    N, W = dim["N"], dim["W"]
    got = pl.pallas_call(
        functools.partial(finish_kernel, dim),
        out_shape=(
            jax.ShapeDtypeStruct(out.shape, BF), jax.ShapeDtypeStruct(gtok.shape, F32),
            jax.ShapeDtypeStruct((PER, TS), F32), vec, vec,
            jax.ShapeDtypeStruct((L, 3, PER, HL), F32), jax.ShapeDtypeStruct((L, HL, PER), F32),
            vec, vec, vec, big, vec, big, vec),
        in_specs=[any_, any_, vm, any_],
        out_specs=(any_, any_) + (vm,) * 8 + (any_, vm, any_, vm),
        scratch_shapes=[
            pltpu.VMEM((L, 3, PER, FL), F32), pltpu.VMEM(out.shape, BF), pltpu.VMEM(gtok.shape, F32),
            pltpu.VMEM((2, N, W), F32), pltpu.SemaphoreType.DMA((3 * L + 2,)), pltpu.SemaphoreType.DMA((2 * L + 2,))],
        name="finish",
    )(out, gtok, sx, g)
    got = list(got)
    got[2] = jnp.transpose(got[2])
    got[5] = jnp.transpose(got[5], (0, 2, 1, 3))
    got[12] = jnp.transpose(got[12], (0, 2, 1))
    return tuple(got)


def solution(mesh):
    placed = (
        P(("dp", "tensor"), None), P("dp"), P("dp"), P(), P(), P(),
        P(None, None, None, "tensor"), P(None, "tensor", None), P(), P(), P(),
        P(None, None, "tensor"), P(None, "tensor"), P(None, "tensor", None), P(),
        P(("dp", "tensor"), None),
    )
    return jax.shard_map(
        local,
        mesh=mesh,
        in_specs=placed,
        out_specs=(
            P(("dp", "tensor"), None), P(("dp", "tensor"), None), P(None, "dp"), P(None, "dp"), P(None, "dp"),
            P(None, "dp", None, "tensor"), P(None, "tensor", "dp"), P(None, "dp"), P(None, "dp"), P(None, "dp"),
            P(None, "dp", "tensor"), P(None, ("tensor", "dp")), P(None, "tensor", "dp"), P(None, "dp"),
        ),
        check_vma=False,
    )
```

```python
import functools

import jax
import jax.numpy as jnp
from jax import lax
from jax.experimental import pallas as pl
from jax.experimental.pallas import tpu as pltpu
from jax.sharding import PartitionSpec as P

HEAD_DIM = 64
EPSILON = 1e-05
NEGATIVE = -1e30
MESH = pl.DeviceIdType.MESH
BF = jnp.bfloat16
F32 = jnp.float32
INV_SQRT2 = 0.7071067811865476
INV_SQRT2PI = 0.3989422804014327

NN = (((1,), (0,)), ((), ()))
NT = (((1,), (1,)), ((), ()))
TN = (((0,), (0,)), ((), ()))


def mm(a, b, dims=NN):
    return lax.dot_general(a, b, dims, preferred_element_type=F32)


def step_kernel(dim, *refs):
    (
        ts_ref, bs_ref, g1_in, b1_in, bo_in, g2_in, b2_in, bd_in, bup_in,
        tok_in, cot_in, table_h, wqkv_h, wout_h, wup_h, wdown_h,
        out_o, gtok_o, smallx_o, g_o,
        wqkv, wout, wup, wdown, tokf, cotf,
        a_b, a2_b, g_b, gp_b, qkvT, kv_b, oT_b, lse_b, h_b, m_b,
        df_b, dz_b, dh_b, doT_b, dqT_b, dkv_acc,
        ysend, yrecv, csend, crecv, part, s_b, p_b, ds_b, gstage,
        small, smallr, smallx, smallp, emb_b,
        send1, recv1, own1, send2, recv2, fstage,
        wsem, tsem_s, tsem_r, ysem_s, ysem_r, casem_s, casem_r, cpsem_s, cpsem_r,
        lsem, osem, gsem, ssem, x1s, x1r,
        r1s, r1r, r2s, r2r, turned,
    ) = refs
    D, FL, HL, R, L = dim["D"], dim["FL"], dim["HL"], dim["R"], dim["L"]
    N, NI, NO, PER, FUSED = dim["N"], dim["NI"], dim["NO"], dim["PER"], dim["FUSED"]
    HP = HL
    vecs = (g1_in, b1_in, bo_in, g2_in, b2_in, bd_in)

    def vrow(i, l):
        return vecs[i][l : l + 1, :].astype(F32)

    T = 4 * R
    NH = HL // HEAD_DIM
    CH = 2 * R
    NB = D // 256
    FB = FL // 256
    t = lax.axis_index("tensor")
    d = lax.axis_index("dp")
    di = lax.rem(d, NI)
    do_ = lax.div(d, NI)
    y = lax.div(t, 2)
    c = lax.rem(t, 2)
    ypeer = lax.rem(t + 2, 4)
    cpeer = t + 1 - 2 * c
    dpeer = lax.rem(cpeer + 2, 4)

    def own(r):
        return pl.multiple_of(R * (2 * r + c), R)

    def oth(r):
        return pl.multiple_of(R * (2 * r + 1 - c), R)

    def remote(src, dst, ss, rs, peer):
        return pltpu.make_async_remote_copy(
            src_ref=src, dst_ref=dst, send_sem=ss, recv_sem=rs,
            device_id={"tensor": peer}, device_id_type=MESH)

    def dp_remote(src, dst, ss, rs, peer):
        return pltpu.make_async_remote_copy(
            src_ref=src, dst_ref=dst, send_sem=ss, recv_sem=rs,
            device_id={"dp": peer}, device_id_type=MESH)

    bar = pltpu.get_barrier_semaphore()

    def greet(k, cy):
        pl.semaphore_signal(bar, inc=1, device_id={"dp": lax.rem(d + k, N)}, device_id_type=MESH)
        return cy

    lax.fori_loop(1, N, greet, 0)
    pl.semaphore_signal(bar, inc=1, device_id={"tensor": ypeer}, device_id_type=MESH)
    pl.semaphore_signal(bar, inc=1, device_id={"tensor": cpeer}, device_id_type=MESH)
    pl.semaphore_signal(bar, inc=1, device_id={"tensor": dpeer}, device_id_type=MESH)

    loc = [pltpu.make_async_copy(tok_in, tokf.at[y], lsem.at[0]),
           pltpu.make_async_copy(cot_in, cotf.at[y], lsem.at[1]),
           pltpu.make_async_copy(table_h, df_b.at[pl.ds(0, dim["TS"]), :], lsem.at[2])]
    for cp in loc:
        cp.start()
    wcopies = []
    for l in range(L):
        row = []
        for i, (src, dst) in enumerate(((wqkv_h, wqkv), (wout_h, wout), (wup_h, wup), (wdown_h, wdown))):
            cp = pltpu.make_async_copy(src.at[l], dst.at[l], wsem.at[l, i])
            cp.start()
            row.append(cp)
        wcopies.append(row)
    pl.semaphore_wait(bar, N + 2)
    tcp = [remote(tok_in, tokf.at[y], tsem_s.at[0], tsem_r.at[0], ypeer),
           remote(cot_in, cotf.at[y], tsem_s.at[1], tsem_r.at[1], ypeer)]
    tcp[0].start()

    small[...] = jnp.zeros_like(small)
    bs = bs_ref[0]
    loc[2].wait()
    pick = (lax.broadcasted_iota(jnp.int32, (8, dim["TS"]), 1) == ts_ref[0]).astype(BF)
    emb_b[...] = mm(pick, df_b[0 : dim["TS"], :])

    def y_copy(par, r, i):
        rows = pl.ds(i, BLK)
        b = i // BLK
        return remote(ysend.at[par, r, rows, :], yrecv.at[par, r, rows, :],
                      ysem_s.at[par, r, b], ysem_r.at[par, r, b], ypeer)

    def tile_copy(buf, r, i, q):
        rows = pl.ds(pl.multiple_of(own(r) + i, BLK), BLK)
        b = i // BLK
        return remote(buf.at[rows, :], buf.at[rows, :], casem_s.at[q, b], casem_r.at[q, b], cpeer)

    class Tile:
        def __init__(self, buf, r, q=None):
            self.copy = lambda i: tile_copy(buf, r, i, r if q is None else q)

        def wait_recv(self):
            for i in range(0, R, BLK):
                self.copy(i).wait_recv()

        def wait_send(self):
            for i in range(0, R, BLK):
                self.copy(i).wait_send()

    def part_copy(r):
        return remote(csend.at[r], crecv.at[r], cpsem_s.at[r], cpsem_r.at[r], cpeer)

    BLK = dim["BLK"]

    def rowloop(fn, init=0):
        return lax.fori_loop(0, R // BLK, lambda i, cy: fn(pl.multiple_of(i * BLK, BLK), cy), init)

    def ln_stats(x):
        mean = jnp.sum(x, axis=-1, keepdims=True) * (1.0 / D)
        xc = x - mean
        var = jnp.sum(xc * xc, axis=-1, keepdims=True) * (1.0 / D)
        return xc, lax.rsqrt(var + EPSILON)

    def enter_fwd(l, r, src, gi, dst_h, dst_a, par=None):
        gain = vrow(gi, l)
        bias = vrow(gi + 1, l)
        cp = Tile(dst_a.at[l], r)

        def blk(i, cy):
            if par is not None:
                wait_y(par, r, i)
            x = src(i)
            dst_h[l, r, pl.ds(i, BLK), :] = x
            xc, rstd = ln_stats(x)
            dst_a[l, pl.ds(pl.multiple_of(own(r) + i, BLK), BLK), :] = (xc * rstd * gain + bias).astype(BF)
            cp.copy(i).start()
            return cy

        rowloop(blk)
        return cp

    def ysum(par, r, i):
        return ysend[par, r, pl.ds(i, BLK), :].astype(F32) + yrecv[par, r, pl.ds(i, BLK), :].astype(F32)

    def wait_y(par, r, i):
        cp = y_copy(par, r, i)
        cp.wait_send()
        cp.wait_recv()

    def wait_mine(par, i):
        y_copy(par, 1 - y, i).wait_send()
        y_copy(par, y, i).wait_recv()

    def send_partner(r, fill):
        fill(csend.at[r])
        cp = part_copy(r)
        cp.start()
        return cp

    def combine(par, r, cp, last=False):
        cp.wait_recv()

        def blk(i, cy):
            v = part[pl.ds(i, BLK), :] + crecv[r, pl.ds(i, BLK), :].astype(F32)
            ysend[par, r, pl.ds(i, BLK), :] = v.astype(BF)
            if last:
                @pl.when(y == 1 - r)
                def _():
                    y_copy(par, r, i).start()
            else:
                y_copy(par, r, i).start()
            return cy

        rowloop(blk)
        cp.wait_send()

    def qkv_tile(l, q0):
        q = mm(wqkv[l, 0:HP, :], a_b[l, pl.ds(q0, R), :], NT).astype(BF)
        qkvT[l, 0:HP, pl.ds(q0, R)] = q * jnp.asarray(HEAD_DIM ** -0.5, BF)
        for cc in (1, 2):
            v = mm(wqkv[l, cc * HP : cc * HP + HP, :], a_b[l, pl.ds(q0, R), :], NT)
            qkvT[l, cc * HP : cc * HP + HP, pl.ds(q0, R)] = v.astype(BF)
            kv_b[l, cc - 1, pl.ds(q0, R), :] = v.T.astype(BF)

    def hmask(h):
        rows = lax.broadcasted_iota(jnp.int32, (HP, R), 0)
        return (rows >= h * HEAD_DIM) & (rows < (h + 1) * HEAD_DIM)

    def visible(r, kb, q0):
        key = lax.broadcasted_iota(jnp.int32, (R, R), 0) + (CH * r + kb * R)
        qry = lax.broadcasted_iota(jnp.int32, (R, R), 1) + q0
        return key <= (qry | (bs - 1))

    def att_fwd_tile(l, r, q0):
        KB = 2 * (r + 1)

        def head(h, cy):
            qm = jnp.where(hmask(h), qkvT[l, 0:HP, pl.ds(q0, R)].astype(F32), 0.0).astype(BF)
            top = None
            for kb in range(KB):
                s = mm(kv_b[l, 0, kb * R : kb * R + R, :], qm)
                if kb >= 2 * r:
                    s = jnp.where(visible(r, kb - 2 * r, q0), s, NEGATIVE)
                s_b[kb * R : kb * R + R, :] = s
                mx = jnp.max(s, axis=0, keepdims=True)
                top = mx if top is None else jnp.maximum(top, mx)
            tot = None
            for kb in range(KB):
                e = jnp.exp(s_b[kb * R : kb * R + R, :] - top)
                p_b[kb * R : kb * R + R, :] = e.astype(BF)
                sm = jnp.sum(e, axis=0, keepdims=True)
                tot = sm if tot is None else tot + sm
            hr = pl.multiple_of(h * HEAD_DIM, HEAD_DIM)
            o = mm(qkvT[l, pl.ds(pl.multiple_of(2 * HP + hr, HEAD_DIM), HEAD_DIM), 0 : KB * R], p_b[0 : KB * R, :])
            oT_b[l, pl.ds(hr, HEAD_DIM), pl.ds(q0, R)] = (o * (1.0 / tot)).astype(BF)
            lse_b[l, pl.ds(h, 1), pl.ds(q0, R)] = top + jnp.log(tot)
            return cy

        lax.fori_loop(0, NH, head, 0)

    def nblocks(fn, n):
        for i in range(n):
            fn(i * 256)

    def out_tile(l, q0, dst):
        o = oT_b[l, :, pl.ds(q0, R)].astype(F32).T.astype(BF)

        def one(n):
            dst[:, n : n + 256] = mm(o, wout[l, :, n : n + 256]).astype(dst.dtype)

        nblocks(one, NB)

    def up_tile(l, q0):
        def one(n, cy):
            n = pl.multiple_of(n * 256, 256)
            u = mm(a2_b[l, pl.ds(q0, R), :], wup[l, :, pl.ds(n, 256)]) + bup_in[l : l + 1, pl.ds(n, 256)].astype(F32)
            phi = 0.5 * (1.0 + lax.erf(u * INV_SQRT2))
            g_b[l, pl.ds(q0, R), pl.ds(n, 256)] = (u * phi).astype(BF)
            gp = phi + u * (jnp.exp(u * u * -0.5) * INV_SQRT2PI)
            gp_b[l, pl.ds(q0, R), pl.ds(n, 256)] = gp.astype(BF)
            return cy

        lax.fori_loop(0, FB, one, 0)

    def down_tile(l, q0, dst):
        def one(n):
            dst[:, n : n + 256] = mm(g_b[l, pl.ds(q0, R), :], wdown[l, :, n : n + 256]).astype(dst.dtype)

        nblocks(one, NB)

    def own_first(r, tile_cp, fn, between=None):
        def tile(i, cy):
            if tile_cp is not None:
                @pl.when(i == 1)
                def _():
                    tile_cp.wait_recv()
                    if between is not None:
                        between()

            fn(pl.multiple_of(R * (2 * r + c + i * (1 - 2 * c)), R))
            return cy

        lax.fori_loop(0, 2, tile, 0)

    def att_fwd(l, r, tile_cp):
        own_first(r, tile_cp, lambda q0: qkv_tile(l, q0))
        cp = part_copy(r)

        def tile(i, cy):
            att_fwd_tile(l, r, pl.multiple_of(R * (2 * r + 1 - c + i * (2 * c - 1)), R))

            @pl.when(i == 0)
            def _():
                out_tile(l, oth(r), csend.at[r])
                cp.start()

            return cy

        lax.fori_loop(0, 2, tile, 0)
        out_tile(l, own(r), part)
        tile_cp.wait_send()
        combine(0, r, cp)

    def ffn_fwd(l, r, tile_cp):
        own_first(r, tile_cp, lambda q0: up_tile(l, q0))
        cp = send_partner(r, lambda ref: down_tile(l, oth(r), ref))
        down_tile(l, own(r), part)
        tile_cp.wait_send()
        combine(1, r, cp, l == L - 1)

    def finish_output():
        bd = vrow(5, L - 1)

        def blk(i, cy):
            wait_mine(1, i)
            v = m_b[L - 1, y, pl.ds(i, BLK), :] + (ysum(1, y, i) + bd)
            tokf[y, pl.ds(i, BLK), :] = v.astype(BF)
            return cy

        rowloop(blk)

    def ln_bwd(l, r, par, gi, xbuf, emit, mine=False):
        gain = vrow(gi, l)

        def blk(i, cy):
            dg, db = cy
            if mine:
                wait_mine(par, i)
            else:
                wait_y(par, r, i)
            x = xbuf[l, r, pl.ds(i, BLK), :]
            dy = ysum(par, r, i)
            xc, rstd = ln_stats(x)
            xh = xc * rstd
            t1 = dy * gain
            m1 = jnp.sum(t1, axis=-1, keepdims=True) * (1.0 / D)
            m2 = jnp.sum(t1 * xh, axis=-1, keepdims=True) * (1.0 / D)
            dx = rstd * (t1 - m1 - xh * m2)
            emit(i, dx)
            dg = dg + jnp.sum(dy * xh, axis=0, keepdims=True)
            db = db + jnp.sum(dy, axis=0, keepdims=True)
            return (dg, db)

        z = jnp.zeros((1, D), F32)
        dg, db = rowloop(blk, (z, z))
        small[l, gi : gi + 1, :] = small[l, gi : gi + 1, :] + dg
        small[l, gi + 1 : gi + 2, :] = small[l, gi + 1 : gi + 2, :] + db

    def colsum_own(buf, r, l, row):
        def blk(i, cy):
            return cy + jnp.sum(buf[pl.ds(pl.multiple_of(own(r) + i, BLK), BLK), :].astype(F32), axis=0, keepdims=True)

        v = rowloop(blk, jnp.zeros((1, D), F32))
        small[l, row : row + 1, :] = small[l, row : row + 1, :] + v

    def enter_b1(l, r):
        cp = Tile(df_b, r, 2 + r if l == L - 1 else r)
        if l == L - 1:
            def blk(i, cy):
                v = cotf[r, pl.ds(i, BLK), :]
                dh_b[r, pl.ds(i, BLK), :] = v.astype(F32)
                df_b[pl.ds(pl.multiple_of(own(r) + i, BLK), BLK), :] = v
                cp.copy(i).start()
                return cy

            rowloop(blk)
        else:
            def emit(i, dx):
                v = dh_b[r, pl.ds(i, BLK), :] + dx
                dh_b[r, pl.ds(i, BLK), :] = v
                df_b[pl.ds(pl.multiple_of(own(r) + i, BLK), BLK), :] = v.astype(BF)
                cp.copy(i).start()

            ln_bwd(l + 1, r, 0, 0, h_b, emit)
        colsum_own(df_b, r, l, 5)
        return cp

    def du_tile(l, q0):
        def one(n, cy):
            n = pl.multiple_of(n * 256, 256)
            dg = mm(df_b[pl.ds(q0, R), :], wdown[l, pl.ds(n, 256), :], NT)
            du = (dg * gp_b[l, pl.ds(q0, R), pl.ds(n, 256)].astype(F32)).astype(BF)
            gp_b[l, pl.ds(q0, R), pl.ds(n, 256)] = du
            small[l, 7:8, pl.ds(n, 256)] = small[l, 7:8, pl.ds(n, 256)] + jnp.sum(du.astype(F32), axis=0, keepdims=True)
            return cy

        lax.fori_loop(0, FB, one, 0)

    def da2_tile(l, q0, dst):
        def one(n):
            dst[:, n : n + 256] = mm(gp_b[l, pl.ds(q0, R), :], wup[l, n : n + 256, :], NT).astype(dst.dtype)

        nblocks(one, NB)

    def ffn_bwd(l, r, tile_cp):
        own_first(r, tile_cp, lambda q0: du_tile(l, q0))
        if l == L - 1 and r == 1:
            pl.semaphore_wait(turned, 1)
        cp = send_partner(r, lambda ref: da2_tile(l, oth(r), ref))
        da2_tile(l, own(r), part)
        if tile_cp is not None:
            tile_cp.wait_send()
        combine(2, r, cp)

    def enter_b2(l, r):
        cp = Tile(dz_b, r)

        def emit(i, dx):
            v = dh_b[r, pl.ds(i, BLK), :] + dx
            dh_b[r, pl.ds(i, BLK), :] = v
            dz_b[pl.ds(pl.multiple_of(own(r) + i, BLK), BLK), :] = v.astype(BF)
            cp.copy(i).start()

        ln_bwd(l, r, 2, 3, m_b, emit)
        colsum_own(dz_b, r, l, 2)
        return cp

    def do_tile(l, q0):
        doT_b[:, pl.ds(q0, R)] = mm(wout[l], dz_b[pl.ds(q0, R), :], NT).astype(BF)

    def att_bwd_tile(l, r, q0):
        KB = 2 * (r + 1)
        KN = KB * R

        def head(h, cy):
            hr = pl.multiple_of(h * HEAD_DIM, HEAD_DIM)
            hm = hmask(h)
            qm = jnp.where(hm, qkvT[l, 0:HP, pl.ds(q0, R)].astype(F32), 0.0).astype(BF)
            dom = jnp.where(hm, doT_b[:, pl.ds(q0, R)].astype(F32), 0.0).astype(BF)
            do_h = doT_b[pl.ds(hr, HEAD_DIM), pl.ds(q0, R)]
            q_h = qkvT[l, pl.ds(hr, HEAD_DIM), pl.ds(q0, R)]
            o_h = oT_b[l, pl.ds(hr, HEAD_DIM), pl.ds(q0, R)]
            dsum = jnp.sum(do_h.astype(F32) * o_h.astype(F32), axis=0, keepdims=True)
            lse = lse_b[l, pl.ds(h, 1), pl.ds(q0, R)]
            for kb in range(KB):
                ks = slice(kb * R, kb * R + R)
                s = mm(kv_b[l, 0, ks, :], qm)
                p = jnp.exp(s - lse)
                if kb >= 2 * r:
                    p = jnp.where(visible(r, kb - 2 * r, q0), p, 0.0)
                p_b[ks, :] = p.astype(BF)
                dp = mm(kv_b[l, 1, ks, :], dom)
                ds_b[ks, :] = (p * (dp - dsum)).astype(BF)
            dkv_acc[1, pl.ds(hr, HEAD_DIM), 0:KN] = dkv_acc[1, pl.ds(hr, HEAD_DIM), 0:KN] + mm(do_h, p_b[0:KN, :], NT)
            dkv_acc[0, pl.ds(hr, HEAD_DIM), 0:KN] = dkv_acc[0, pl.ds(hr, HEAD_DIM), 0:KN] + mm(q_h, ds_b[0:KN, :], NT)
            k_h = qkvT[l, pl.ds(pl.multiple_of(HP + hr, HEAD_DIM), HEAD_DIM), 0:KN]
            dq = mm(k_h, ds_b[0:KN, :]) * (HEAD_DIM ** -0.5)
            dqT_b[pl.ds(hr, HEAD_DIM), pl.ds(q0, R)] = dq.astype(BF)
            return cy

        lax.fori_loop(0, NH, head, 0)

    def da_tile(l, q0, dst):
        dqkv = dqT_b[:, pl.ds(q0, R)].astype(F32).T.astype(BF)

        def one(n):
            dst[:, n : n + 256] = mm(dqkv, wqkv[l, :, n : n + 256]).astype(dst.dtype)

        nblocks(one, NB)

    def att_bwd(l, r, tile_cp, between=None):
        def both(q0):
            do_tile(l, q0)
            att_bwd_tile(l, r, q0)

        own_first(r, tile_cp, both, between)
        cs = slice(CH * r, CH * r + CH)
        for j in range(2):
            dqT_b[HP * (j + 1) : HP * (j + 1) + HL, cs] = dkv_acc[j, 0:HL, cs].astype(BF)
        cp = send_partner(r, lambda ref: da_tile(l, oth(r), ref))
        da_tile(l, own(r), part)
        tile_cp.wait_send()
        combine(0, r, cp, l == 0)

    WHOLE = (0, FL, 0)
    HALF = ((0, FL // 2, 0), (FL // 2, FL - FL // 2, 3))
    THIRD = tuple((i * 256, 256, 3 * i) for i in range(FL // 256))

    def r1_copy(j, k, span):
        c0, w, extra = span
        q = j + extra
        peer = do_ * NI + lax.rem(di + k, NI)
        return dp_remote(send1.at[j, k - 1, :, c0 : c0 + w], recv1.at[j, k - 1, :, c0 : c0 + w],
                         r1s.at[q, k - 1], r1r.at[q, k - 1], peer)

    def r2_copy(j, k, span):
        c0, w, extra = span
        q = j + extra
        peer = lax.rem(do_ + k, NO) * NI + di
        return dp_remote(send2.at[j, k - 1, :, c0 : c0 + w], recv2.at[j, k - 1, :, c0 : c0 + w],
                         r2s.at[q, k - 1], r2r.at[q, k - 1], peer)

    def g_copy(l, j, span):
        c0, w, extra = span
        q = l * 9 + j + extra
        return pltpu.make_async_copy(fstage.at[l, j, :, c0 : c0 + w], g_o.at[l, j, :, c0 : c0 + w], gsem.at[q])

    def piece(q):
        return pl.ds(pl.multiple_of(q * PER, PER), PER)

    def rs_start(l, j, span=WHOLE):
        c0, w, _ = span
        cols = slice(c0, c0 + w)
        if not FUSED:
            cp = pltpu.make_async_copy(gstage.at[:, cols], g_o.at[l, j, :, cols], gsem.at[0])
            cp.start()
            cp.wait()
            return
        for k in range(1, NI):
            for oo in range(NO):
                send1[j, k - 1, oo * PER : oo * PER + PER, cols] = gstage[piece(oo * NI + lax.rem(di + k, NI)), cols].astype(BF)
            r1_copy(j, k, span).start()
        for oo in range(NO):
            own1[j, oo * PER : oo * PER + PER, cols] = gstage[piece(oo * NI + di), cols]

    def rs_mid(l, j, span=WHOLE):
        c0, w, _ = span
        cols = slice(c0, c0 + w)
        if not FUSED:
            return
        for k in range(1, NI):
            cp = r1_copy(j, k, span)
            cp.wait_send()
            cp.wait_recv()
        for kk in range(NO - 1, -1, -1):
            rows = piece(lax.rem(do_ + kk, NO))
            v = own1[j, rows, cols]
            for k in range(1, NI):
                v = v + recv1[j, k - 1, rows, cols].astype(F32)
            if kk == 0:
                own1[j, rows, cols] = v
            else:
                send2[j, kk - 1, :, cols] = v.astype(BF)
                r2_copy(j, kk, span).start()

    def rs_fin(l, j, span=WHOLE):
        c0, w, _ = span
        cols = slice(c0, c0 + w)
        if not FUSED:
            return
        v = own1[j, piece(do_), cols]
        for kk in range(1, NO):
            cp = r2_copy(j, kk, span)
            cp.wait_send()
            cp.wait_recv()
            v = v + recv2[j, kk - 1, :, cols].astype(F32)
        fstage[l, j, :, cols] = v
        g_copy(l, j, span).start()

    def wgrad_ffn(l, lhs, rhs, rows=slice(None), add=False):
        def one(n, cy):
            ns = pl.ds(pl.multiple_of(n * 256, 256), 256)
            lt = lhs[rows, ns].astype(F32).T.astype(BF)
            for f in range(FB):
                fs = slice(f * 256, f * 256 + 256)
                v = mm(lt, rhs[rows, fs])
                gstage[ns, fs] = gstage[ns, fs] + v if add else v
            return cy

        lax.fori_loop(0, NB, one, 0)

    def wgrad_att(l, span):
        lo, hi = span[0], span[0] + span[1]
        q = min(hi, 3 * HL)

        def one(n, cy):
            ns = pl.ds(pl.multiple_of(n * 256, 256), 256)
            s_b[lo:q, :] = mm(dqT_b[lo:q, :], a_b[l, :, ns])
            if hi > q:
                s_b[q:hi, :] = mm(oT_b[l], dz_b[:, ns])
            gstage[ns, lo:hi] = s_b[lo:hi, :].T
            return cy

        lax.fori_loop(0, NB, one, 0)

    for l in range(L):
        for r in range(2):
            if l == 0:
                if r == 0:
                    for cp in (loc[0], wcopies[0][0]):
                        cp.wait()
                    tcp[0].wait()
                    tcp[1].start()
                src = lambda i, r=r: tokf[r, pl.ds(i, BLK), :].astype(F32) + emb_b[0:1, :]
            else:
                bd = vrow(5, l - 1)
                src = lambda i, r=r, l=l, bd=bd: m_b[l - 1, r, pl.ds(i, BLK), :] + (ysum(1, r, i) + bd)
            if r == 0 and l > 0:
                wcopies[l][0].wait()
            cp = enter_fwd(l, r, src, 0, h_b, a_b, 1 if l > 0 else None)
            if r == 0:
                wcopies[l][1].wait()
            att_fwd(l, r, cp)
        for r in range(2):
            if l == L - 1 and r == 0:
                loc[1].wait()
                tcp[1].wait()
                b1 = [enter_b1(l, 0), enter_b1(l, 1)]
            elif l == L - 1:
                b1[0].wait_recv()
                wgrad_ffn(l, df_b, g_b.at[l], slice(0, CH))
            bo = vrow(2, l)
            src = lambda i, r=r, l=l, bo=bo: h_b[l, r, pl.ds(i, BLK), :] + (ysum(0, r, i) + bo)
            if r == 0:
                wcopies[l][2].wait()
                wcopies[l][3].wait()
            cp = enter_fwd(l, r, src, 3, m_b, a2_b, 0)
            ffn_fwd(l, r, cp)

    pl.semaphore_signal(turned, inc=1, device_id={"tensor": cpeer}, device_id_type=MESH)
    b1[1].wait_recv()
    wgrad_ffn(L - 1, df_b, g_b.at[L - 1], slice(CH, T), True)
    rs_start(L - 1, 2)
    for cp in b1:
        cp.wait_send()
    def many(fn, l, j, spans):
        for span in spans:
            fn(l, j, span)

    for l in range(L - 1, -1, -1):
        last = l == L - 1
        spans = (WHOLE,) if last else HALF
        ends = HALF if l > 0 else THIRD
        if last:
            for r in (1, 0):
                ffn_bwd(l, r, None)
            finish_output()
        else:
            ffn_bwd(l, 1, enter_b1(l, 1))
            many(rs_fin, l + 1, 2, (WHOLE,) if l + 1 == L - 1 else HALF)
            rs_mid(l + 1, 0, HALF[0])
            cp = enter_b1(l, 0)
            cp.wait_recv()
            wgrad_ffn(l, df_b, g_b.at[l])
            many(rs_start, l, 2, spans)
            cp.wait_send()
            many(rs_fin, l + 1, 1, (WHOLE,) if l + 1 == L - 1 else HALF)
            rs_mid(l + 1, 0, HALF[1])
            ffn_bwd(l, 0, None)
        wgrad_ffn(l, a2_b.at[l], gp_b.at[l])
        many(rs_start, l, 1, spans)
        dkv_acc[...] = jnp.zeros_like(dkv_acc)
        cp = enter_b2(l, 1)
        if not last:
            many(rs_fin, l + 1, 0, HALF)
        rs_mid(l, 2, spans[0])
        att_bwd(l, 1, cp, None if last else lambda l=l, span=HALF[1]: rs_mid(l, 2, span))
        cp = enter_b2(l, 0)
        att_bwd(l, 0, cp, lambda l=l, span=spans[0]: rs_mid(l, 1, span))
        for i, span in enumerate(ends):
            wgrad_att(l, span)
            if not last and i == 1:
                rs_mid(l, 1, HALF[1])
            rs_start(l, 0, span)
    ocp = pltpu.make_async_copy(tokf.at[y], out_o, osem.at[0])
    ocp.start()
    many(rs_fin, 0, 2, HALF)
    rs_mid(0, 0, THIRD[0])

    def emit(i, dx):
        v = dh_b[y, pl.ds(i, BLK), :] + dx
        dh_b[y, pl.ds(i, BLK), :] = v
        small[0, 6:7, :] = small[0, 6:7, :] + jnp.sum(v, axis=0, keepdims=True)

    ln_bwd(0, y, 0, 0, h_b, emit, True)
    gcp = pltpu.make_async_copy(dh_b.at[y], gtok_o, osem.at[1])
    gcp.start()
    scps = [remote(small, smallr.at[0:L], ssem.at[0], ssem.at[3], cpeer),
            remote(small.at[0], smallr.at[L], ssem.at[1], ssem.at[4], ypeer),
            remote(small.at[0], smallr.at[L + 1], ssem.at[2], ssem.at[5], dpeer)]
    for scp in scps:
        scp.start()
    many(rs_mid, 0, 0, THIRD[1:])
    for scp in scps:
        scp.wait()
    which = lax.broadcasted_iota(jnp.int32, (8, D), 0)
    small[0] = small[0] + jnp.where((which < 2) | (which == 6), smallr[L] + smallr[L + 1], 0.0)
    for l in range(L):
        small[l] = small[l] + jnp.where(which < 7, smallr[l], 0.0)
    small[1, 6:7, :] = jnp.full((1, D), ts_ref[0].astype(F32), F32)

    def x_copy(k):
        return dp_remote(smallp.at[k], smallx.at[d], x1s.at[k], x1r.at[k], lax.rem(d + k, N))

    def columns(k):
        turn = lax.rem(D - PER * lax.rem(d + k, N), D)
        return [pltpu.roll(small[l], turn, 1)[:, 0 : smallx.shape[3]] for l in range(L)]

    def x_go(k, cy):
        for l, v in enumerate(columns(k)):
            smallp[k, l] = v
        x_copy(k).start()
        return cy

    def x_wait(k, cy):
        cp = x_copy(k)
        cp.wait_send()
        cp.wait_recv()
        return cy

    lax.fori_loop(1, N, x_go, 0)
    for l, v in enumerate(columns(0)):
        smallx[d, l] = v
    many(rs_fin, 0, 1, HALF)
    many(rs_fin, 0, 0, THIRD[:-1])
    lax.fori_loop(1, N, x_wait, 0)
    smallx_o[...] = smallx[...]
    rs_fin(0, 0, THIRD[-1])
    ocp.wait()
    gcp.wait()
    if FUSED:
        for l in range(L):
            for j in range(3):
                for span in THIRD if l == 0 and j == 0 else HALF if l < L - 1 or j == 0 else (WHOLE,):
                    g_copy(l, j, span).wait()


def finish_kernel(dim, out_i, gtok_i, sx, g_i, out_o, gtok_o, table_o, dg1, db1, gq, go, dbo, dg2, db2, gup, dbup, gdown, dbd,
                  g_b, out_b, gtok_b, rows_b, sem_i, sem_o):
    FL, HL, L, PER, N, TS = dim["FL"], dim["HL"], dim["L"], dim["PER"], dim["N"], dim["TS"]
    ins = []
    for j in range(3):
        for l in range(L):
            ins.append(pltpu.make_async_copy(g_i.at[l, j], g_b.at[l, j], sem_i.at[l * 3 + j]))
    order = ((out_i, out_b, out_o), (gtok_i, gtok_b, gtok_o))
    for i, (src, buf, _) in enumerate(order):
        ins.append(pltpu.make_async_copy(src, buf, sem_i.at[3 * L + i]))
    for cp in ins:
        cp.start()
    for l in range(L):
        tot = sx[0, l]
        for q in range(1, N):
            tot = tot + sx[q, l]
        for i, ref in enumerate((dg1, db1, dbo, dg2, db2, dbd)):
            ref[l : l + 1, :] = tot[i : i + 1, 0:PER]
        dbup[l : l + 1, :] = tot[7:8, 0:PER]
    for q in range(N):
        rows_b[0, q : q + 1, :] = sx[q, 0, 6:7, :]
        rows_b[1, q : q + 1, :] = sx[q, 1, 6:7, :]
    step = rows_b[1, :, 0:1]
    pick = jnp.where(lax.broadcasted_iota(jnp.int32, (N, TS), 1).astype(F32) == step, 1.0, 0.0)
    table_o[...] = lax.dot_general(rows_b[0], pick, TN, precision=lax.Precision.HIGHEST, preferred_element_type=F32)[0:PER, :]
    for l in range(L):
        ins[l].wait()
        ga = g_b[l, 0]
        for cc in range(3):
            gq[l, cc] = ga[:, cc * HL : cc * HL + HL]
        gt = jnp.concatenate([ga, jnp.zeros((-PER % 128, 4 * HL), F32)], axis=0).T
        go[l] = gt[3 * HL : 4 * HL, 0:PER]
    outs = []
    for j, ref in ((1, gup), (2, gdown)):
        for l in range(L):
            ins[j * L + l].wait()
            cp = pltpu.make_async_copy(g_b.at[l, j], ref.at[l], sem_o.at[l * 2 + j - 1])
            cp.start()
            outs.append(cp)
    for i, (_, buf, dst) in enumerate(order):
        ins[3 * L + i].wait()
        cp = pltpu.make_async_copy(buf, dst, sem_o.at[2 * L + i])
        cp.start()
        outs.append(cp)
    for cp in outs:
        cp.wait()


def split_of(n):
    inner = 2 ** ((n.bit_length() - 1) // 2)
    return inner, n // inner


def run_step(ts, bs, vecs, bup, tok, cot, table, wqkv, wout, wup, wdown):
    R, D = tok.shape
    L, _, FL = wup.shape
    HL = wout.shape[1]
    N = lax.axis_size("dp")
    NI, NO = split_of(N)
    PER = D // N
    FUSED = PER % 16 == 0
    assert lax.axis_size("tensor") == 4 and ts.shape[0] == 1 and FL == D == 4 * HL and L > 1 and R == 256 and FL == 768
    T = 4 * R
    W = -(-PER // 128) * 128
    BLK = min(R, 128)
    HB = R // BLK
    dim = dict(D=D, FL=FL, HL=HL, R=R, L=L, BLK=BLK, W=W, N=N, NI=NI, NO=NO, PER=PER, FUSED=FUSED, TS=table.shape[0])
    vm = pl.BlockSpec(memory_space=pltpu.VMEM)
    sm = pl.BlockSpec(memory_space=pltpu.SMEM)
    any_ = pl.BlockSpec(memory_space=pl.ANY)
    dma = pltpu.SemaphoreType.DMA
    V = pltpu.VMEM
    J = 3 if FUSED else 1
    PR = PER if FUSED else 16
    ones = max(NI - 1, 1)
    outs = max(NO - 1, 1)
    kept = (L, 3, PER, FL) if FUSED else (L, 3, D, FL)
    return dim, pl.pallas_call(
        functools.partial(step_kernel, dim),
        out_shape=(
            jax.ShapeDtypeStruct((R, D), BF),
            jax.ShapeDtypeStruct((R, D), F32),
            jax.ShapeDtypeStruct((N, L, 8, W), F32),
            jax.ShapeDtypeStruct(kept, F32),
        ),
        in_specs=[sm, sm] + [vm] * 7 + [any_] * 7,
        out_specs=(any_, any_, vm, any_),
        scratch_shapes=[
            V((L, 3 * HL, D), BF), V((L, HL, D), BF), V((L, D, FL), BF), V((L, FL, D), BF),
            V((2, R, D), BF), V((2, R, D), BF),
            V((L, T, D), BF), V((L, T, D), BF), V((L, T, FL), BF), V((L, T, FL), BF),
            V((L, 3 * HL, T), BF), V((L, 2, T, HL), BF), V((L, HL, T), BF), V((L, 8, T), F32),
            V((L, 2, R, D), F32), V((L, 2, R, D), F32),
            V((T, D), BF), V((T, D), BF), V((2, R, D), F32),
            V((HL, T), BF), V((3 * HL, T), BF), V((2, HL, T), F32),
            V((3, 2, R, D), BF), V((3, 2, R, D), BF), V((2, R, D), BF), V((2, R, D), BF),
            V((R, D), F32), V((T, R), F32), V((T, R), BF), V((T, R), BF), V((D, FL), F32),
            V((L, 8, D), F32), V((L + 2, 8, D), F32), V((N, L, 8, W), F32), V((N, L, 8, W), F32), V((8, D), F32),
            V((J, ones, NO * PR, FL), BF), V((J, ones, NO * PR, FL), BF), V((J, NO * PR, FL), F32),
            V((J, outs, PR, FL), BF), V((J, outs, PR, FL), BF), V((L, J, PR, FL), F32),
            dma((L, 4)), dma((2,)), dma((2,)), dma((3, 2, HB)), dma((3, 2, HB)),
            dma((4, HB)), dma((4, HB)), dma((2,)), dma((2,)),
            dma((3,)), dma((2,)), dma((9 * L,)), dma((6,)), dma((N,)), dma((N,)),
            dma((9, ones)), dma((9, ones)), dma((9, outs)), dma((9, outs)), pltpu.SemaphoreType.REGULAR,
        ],
        compiler_params=pltpu.CompilerParams(
            collective_id=0, has_side_effects=True, vmem_limit_bytes=67043328),
        name="layers",
    )(ts, bs, *vecs, bup, tok, cot, table, wqkv, wout, wup, wdown)


def local(tokens, timestep, block_size, table, ln1_gain, ln1_bias, w_qkv, w_out, b_out,
          ln2_gain, ln2_bias, w_up, b_up, w_down, b_down, cotangent):
    L, D, _, HL = w_qkv.shape
    wq = jnp.transpose(w_qkv, (0, 2, 3, 1)).reshape(L, 3 * HL, D)
    vecs = (ln1_gain, ln1_bias, b_out, ln2_gain, ln2_bias, b_down)
    dim, (out, gtok, sx, g) = run_step(
        timestep, block_size, vecs, b_up, tokens, cotangent, table, wq, w_out, w_up, w_down)
    PER, FL, TS = dim["PER"], dim["FL"], dim["TS"]
    if not dim["FUSED"]:
        g = lax.psum_scatter(g, "dp", scatter_dimension=2, tiled=True)
    vec = jax.ShapeDtypeStruct((L, PER), F32)
    big = jax.ShapeDtypeStruct((L, PER, FL), F32)
    vm = pl.BlockSpec(memory_space=pltpu.VMEM)
    any_ = pl.BlockSpec(memory_space=pl.ANY)
    N, W = dim["N"], dim["W"]
    got = pl.pallas_call(
        functools.partial(finish_kernel, dim),
        out_shape=(
            jax.ShapeDtypeStruct(out.shape, BF), jax.ShapeDtypeStruct(gtok.shape, F32),
            jax.ShapeDtypeStruct((PER, TS), F32), vec, vec,
            jax.ShapeDtypeStruct((L, 3, PER, HL), F32), jax.ShapeDtypeStruct((L, HL, PER), F32),
            vec, vec, vec, big, vec, big, vec),
        in_specs=[any_, any_, vm, any_],
        out_specs=(any_, any_) + (vm,) * 8 + (any_, vm, any_, vm),
        scratch_shapes=[
            pltpu.VMEM((L, 3, PER, FL), F32), pltpu.VMEM(out.shape, BF), pltpu.VMEM(gtok.shape, F32),
            pltpu.VMEM((2, N, W), F32), pltpu.SemaphoreType.DMA((3 * L + 2,)), pltpu.SemaphoreType.DMA((2 * L + 2,))],
        name="finish",
    )(out, gtok, sx, g)
    got = list(got)
    got[2] = jnp.transpose(got[2])
    got[5] = jnp.transpose(got[5], (0, 2, 1, 3))
    got[12] = jnp.transpose(got[12], (0, 2, 1))
    return tuple(got)


def solution(mesh):
    placed = (
        P(("dp", "tensor"), None), P("dp"), P("dp"), P(), P(), P(),
        P(None, None, None, "tensor"), P(None, "tensor", None), P(), P(), P(),
        P(None, None, "tensor"), P(None, "tensor"), P(None, "tensor", None), P(),
        P(("dp", "tensor"), None),
    )
    return jax.shard_map(
        local,
        mesh=mesh,
        in_specs=placed,
        out_specs=(
            P(("dp", "tensor"), None), P(("dp", "tensor"), None), P(None, "dp"), P(None, "dp"), P(None, "dp"),
            P(None, "dp", None, "tensor"), P(None, "tensor", "dp"), P(None, "dp"), P(None, "dp"), P(None, "dp"),
            P(None, "dp", "tensor"), P(None, ("tensor", "dp")), P(None, "tensor", "dp"), P(None, "dp"),
        ),
        check_vma=False,
    )
```

```python
import functools

import jax
import jax.numpy as jnp
from jax import lax
from jax.experimental import pallas as pl
from jax.experimental.pallas import tpu as pltpu
from jax.sharding import PartitionSpec as P

HEAD_DIM = 64
EPSILON = 1e-05
NEGATIVE = -1e30
MESH = pl.DeviceIdType.MESH
BF = jnp.bfloat16
F32 = jnp.float32
INV_SQRT2 = 0.7071067811865476
INV_SQRT2PI = 0.3989422804014327

NN = (((1,), (0,)), ((), ()))
NT = (((1,), (1,)), ((), ()))
TN = (((0,), (0,)), ((), ()))


def mm(a, b, dims=NN):
    return lax.dot_general(a, b, dims, preferred_element_type=F32)


def step_kernel(dim, *refs):
    (
        ts_ref, bs_ref, g1_in, b1_in, bo_in, g2_in, b2_in, bd_in, bup_in,
        tok_in, cot_in, table_h, wqkv_h, wout_h, wup_h, wdown_h,
        out_o, gtok_o, smallx_o, g_o,
        wqkv, wout, wup, wdown, tokf, cotf,
        a_b, a2_b, g_b, gp_b, qkvT, kv_b, oT_b, lse_b, h_b, m_b,
        df_b, dz_b, dh_b, doT_b, dqT_b, dkv_acc,
        ysend, yrecv, csend, crecv, part, s_b, p_b, ds_b, gstage,
        small, smallr, smallx, smallp, emb_b,
        send1, recv1, own1, send2, recv2, fstage,
        wsem, tsem_s, tsem_r, ysem_s, ysem_r, casem_s, casem_r, cpsem_s, cpsem_r,
        lsem, osem, gsem, ssem, x1s, x1r,
        r1s, r1r, r2s, r2r, turned,
    ) = refs
    D, FL, HL, R, L = dim["D"], dim["FL"], dim["HL"], dim["R"], dim["L"]
    N, NI, NO, PER, FUSED = dim["N"], dim["NI"], dim["NO"], dim["PER"], dim["FUSED"]
    HP = HL
    vecs = (g1_in, b1_in, bo_in, g2_in, b2_in, bd_in)

    def vrow(i, l):
        return vecs[i][l : l + 1, :].astype(F32)

    T = 4 * R
    NH = HL // HEAD_DIM
    CH = 2 * R
    NB = D // 256
    FB = FL // 256
    t = lax.axis_index("tensor")
    d = lax.axis_index("dp")
    di = lax.rem(d, NI)
    do_ = lax.div(d, NI)
    y = lax.div(t, 2)
    c = lax.rem(t, 2)
    ypeer = lax.rem(t + 2, 4)
    cpeer = t + 1 - 2 * c
    dpeer = lax.rem(cpeer + 2, 4)

    def own(r):
        return pl.multiple_of(R * (2 * r + c), R)

    def oth(r):
        return pl.multiple_of(R * (2 * r + 1 - c), R)

    def remote(src, dst, ss, rs, peer):
        return pltpu.make_async_remote_copy(
            src_ref=src, dst_ref=dst, send_sem=ss, recv_sem=rs,
            device_id={"tensor": peer}, device_id_type=MESH)

    def dp_remote(src, dst, ss, rs, peer):
        return pltpu.make_async_remote_copy(
            src_ref=src, dst_ref=dst, send_sem=ss, recv_sem=rs,
            device_id={"dp": peer}, device_id_type=MESH)

    bar = pltpu.get_barrier_semaphore()

    def greet(k, cy):
        pl.semaphore_signal(bar, inc=1, device_id={"dp": lax.rem(d + k, N)}, device_id_type=MESH)
        return cy

    lax.fori_loop(1, N, greet, 0)
    pl.semaphore_signal(bar, inc=1, device_id={"tensor": ypeer}, device_id_type=MESH)
    pl.semaphore_signal(bar, inc=1, device_id={"tensor": cpeer}, device_id_type=MESH)
    pl.semaphore_signal(bar, inc=1, device_id={"tensor": dpeer}, device_id_type=MESH)

    loc = [pltpu.make_async_copy(tok_in, tokf.at[y], lsem.at[0]),
           pltpu.make_async_copy(cot_in, cotf.at[y], lsem.at[1]),
           pltpu.make_async_copy(table_h, df_b.at[pl.ds(0, dim["TS"]), :], lsem.at[2])]
    for cp in loc:
        cp.start()
    wcopies = []
    for l in range(L):
        row = []
        for i, (src, dst) in enumerate(((wqkv_h, wqkv), (wout_h, wout), (wup_h, wup), (wdown_h, wdown))):
            cp = pltpu.make_async_copy(src.at[l], dst.at[l], wsem.at[l, i])
            cp.start()
            row.append(cp)
        wcopies.append(row)
    pl.semaphore_wait(bar, N + 2)
    tcp = [remote(tok_in, tokf.at[y], tsem_s.at[0], tsem_r.at[0], ypeer),
           remote(cot_in, cotf.at[y], tsem_s.at[1], tsem_r.at[1], ypeer)]
    tcp[0].start()

    small[...] = jnp.zeros_like(small)
    bs = bs_ref[0]
    loc[2].wait()
    pick = (lax.broadcasted_iota(jnp.int32, (8, dim["TS"]), 1) == ts_ref[0]).astype(BF)
    emb_b[...] = mm(pick, df_b[0 : dim["TS"], :])

    def y_copy(par, r, i):
        rows = pl.ds(i, BLK)
        b = i // BLK
        return remote(ysend.at[par, r, rows, :], yrecv.at[par, r, rows, :],
                      ysem_s.at[par, r, b], ysem_r.at[par, r, b], ypeer)

    def tile_copy(buf, r, i, q):
        rows = pl.ds(pl.multiple_of(own(r) + i, BLK), BLK)
        b = i // BLK
        return remote(buf.at[rows, :], buf.at[rows, :], casem_s.at[q, b], casem_r.at[q, b], cpeer)

    class Tile:
        def __init__(self, buf, r, q=None):
            self.copy = lambda i: tile_copy(buf, r, i, r if q is None else q)

        def wait_recv(self):
            for i in range(0, R, BLK):
                self.copy(i).wait_recv()

        def wait_send(self):
            for i in range(0, R, BLK):
                self.copy(i).wait_send()

    def part_copy(r):
        return remote(csend.at[r], crecv.at[r], cpsem_s.at[r], cpsem_r.at[r], cpeer)

    BLK = dim["BLK"]

    def rowloop(fn, init=0):
        return lax.fori_loop(0, R // BLK, lambda i, cy: fn(pl.multiple_of(i * BLK, BLK), cy), init)

    def ln_stats(x):
        mean = jnp.sum(x, axis=-1, keepdims=True) * (1.0 / D)
        xc = x - mean
        var = jnp.sum(xc * xc, axis=-1, keepdims=True) * (1.0 / D)
        return xc, lax.rsqrt(var + EPSILON)

    def enter_fwd(l, r, src, gi, dst_h, dst_a, par=None):
        gain = vrow(gi, l)
        bias = vrow(gi + 1, l)
        cp = Tile(dst_a.at[l], r)

        def blk(i, cy):
            if par is not None:
                wait_y(par, r, i)
            x = src(i)
            dst_h[l, r, pl.ds(i, BLK), :] = x
            xc, rstd = ln_stats(x)
            dst_a[l, pl.ds(pl.multiple_of(own(r) + i, BLK), BLK), :] = (xc * rstd * gain + bias).astype(BF)
            cp.copy(i).start()
            return cy

        rowloop(blk)
        return cp

    def ysum(par, r, i):
        return ysend[par, r, pl.ds(i, BLK), :].astype(F32) + yrecv[par, r, pl.ds(i, BLK), :].astype(F32)

    def wait_y(par, r, i):
        cp = y_copy(par, r, i)
        cp.wait_send()
        cp.wait_recv()

    def wait_mine(par, i):
        y_copy(par, 1 - y, i).wait_send()
        y_copy(par, y, i).wait_recv()

    def send_partner(r, fill):
        fill(csend.at[r])
        cp = part_copy(r)
        cp.start()
        return cp

    def combine(par, r, cp, last=False):
        cp.wait_recv()

        def blk(i, cy):
            v = part[pl.ds(i, BLK), :] + crecv[r, pl.ds(i, BLK), :].astype(F32)
            ysend[par, r, pl.ds(i, BLK), :] = v.astype(BF)
            if last:
                @pl.when(y == 1 - r)
                def _():
                    y_copy(par, r, i).start()
            else:
                y_copy(par, r, i).start()
            return cy

        rowloop(blk)
        cp.wait_send()

    def qkv_tile(l, q0):
        q = mm(wqkv[l, 0:HP, :], a_b[l, pl.ds(q0, R), :], NT).astype(BF)
        qkvT[l, 0:HP, pl.ds(q0, R)] = q * jnp.asarray(HEAD_DIM ** -0.5, BF)
        for cc in (1, 2):
            v = mm(wqkv[l, cc * HP : cc * HP + HP, :], a_b[l, pl.ds(q0, R), :], NT)
            qkvT[l, cc * HP : cc * HP + HP, pl.ds(q0, R)] = v.astype(BF)
            kv_b[l, cc - 1, pl.ds(q0, R), :] = v.T.astype(BF)

    def hmask(h):
        rows = lax.broadcasted_iota(jnp.int32, (HP, R), 0)
        return (rows >= h * HEAD_DIM) & (rows < (h + 1) * HEAD_DIM)

    def visible(r, kb, q0):
        key = lax.broadcasted_iota(jnp.int32, (R, R), 0) + (CH * r + kb * R)
        qry = lax.broadcasted_iota(jnp.int32, (1, R), 1) + q0
        return key <= (qry | (bs - 1))

    def att_fwd_tile(l, r, q0):
        KB = 2 * (r + 1)

        def head(h, cy):
            qm = jnp.where(hmask(h), qkvT[l, 0:HP, pl.ds(q0, R)].astype(F32), 0.0).astype(BF)
            top = None
            for kb in range(KB):
                s = mm(kv_b[l, 0, kb * R : kb * R + R, :], qm)
                if kb >= 2 * r:
                    s = jnp.where(visible(r, kb - 2 * r, q0), s, NEGATIVE)
                s_b[kb * R : kb * R + R, :] = s
                mx = jnp.max(s, axis=0, keepdims=True)
                top = mx if top is None else jnp.maximum(top, mx)
            tot = None
            for kb in range(KB):
                e = jnp.exp(s_b[kb * R : kb * R + R, :] - top)
                p_b[kb * R : kb * R + R, :] = e.astype(BF)
                sm = jnp.sum(e, axis=0, keepdims=True)
                tot = sm if tot is None else tot + sm
            hr = pl.multiple_of(h * HEAD_DIM, HEAD_DIM)
            o = mm(qkvT[l, pl.ds(pl.multiple_of(2 * HP + hr, HEAD_DIM), HEAD_DIM), 0 : KB * R], p_b[0 : KB * R, :])
            oT_b[l, pl.ds(hr, HEAD_DIM), pl.ds(q0, R)] = (o * (1.0 / tot)).astype(BF)
            lse_b[l, pl.ds(h, 1), pl.ds(q0, R)] = top + jnp.log(tot)
            return cy

        lax.fori_loop(0, NH, head, 0)

    def nblocks(fn, n):
        for i in range(n):
            fn(i * 256)

    def out_tile(l, q0, dst):
        o = oT_b[l, :, pl.ds(q0, R)].astype(F32).T.astype(BF)

        def one(n):
            dst[:, n : n + 256] = mm(o, wout[l, :, n : n + 256]).astype(dst.dtype)

        nblocks(one, NB)

    def up_tile(l, q0):
        def one(n, cy):
            n = pl.multiple_of(n * 256, 256)
            u = mm(a2_b[l, pl.ds(q0, R), :], wup[l, :, pl.ds(n, 256)]) + bup_in[l : l + 1, pl.ds(n, 256)].astype(F32)
            phi = 0.5 * (1.0 + lax.erf(u * INV_SQRT2))
            g_b[l, pl.ds(q0, R), pl.ds(n, 256)] = (u * phi).astype(BF)
            gp = phi + u * (jnp.exp(u * u * -0.5) * INV_SQRT2PI)
            gp_b[l, pl.ds(q0, R), pl.ds(n, 256)] = gp.astype(BF)
            return cy

        lax.fori_loop(0, FB, one, 0)

    def down_tile(l, q0, dst):
        def one(n):
            dst[:, n : n + 256] = mm(g_b[l, pl.ds(q0, R), :], wdown[l, :, n : n + 256]).astype(dst.dtype)

        nblocks(one, NB)

    def own_first(r, tile_cp, fn, between=None):
        def tile(i, cy):
            if tile_cp is not None:
                @pl.when(i == 1)
                def _():
                    tile_cp.wait_recv()
                    if between is not None:
                        between()

            fn(pl.multiple_of(R * (2 * r + c + i * (1 - 2 * c)), R))
            return cy

        lax.fori_loop(0, 2, tile, 0)

    def att_fwd(l, r, tile_cp):
        own_first(r, tile_cp, lambda q0: qkv_tile(l, q0))
        cp = part_copy(r)

        def tile(i, cy):
            att_fwd_tile(l, r, pl.multiple_of(R * (2 * r + 1 - c + i * (2 * c - 1)), R))

            @pl.when(i == 0)
            def _():
                out_tile(l, oth(r), csend.at[r])
                cp.start()

            return cy

        lax.fori_loop(0, 2, tile, 0)
        out_tile(l, own(r), part)
        tile_cp.wait_send()
        combine(0, r, cp)

    def ffn_fwd(l, r, tile_cp):
        own_first(r, tile_cp, lambda q0: up_tile(l, q0))
        cp = send_partner(r, lambda ref: down_tile(l, oth(r), ref))
        down_tile(l, own(r), part)
        tile_cp.wait_send()
        combine(1, r, cp, l == L - 1)

    def finish_output():
        bd = vrow(5, L - 1)

        def blk(i, cy):
            wait_mine(1, i)
            v = m_b[L - 1, y, pl.ds(i, BLK), :] + (ysum(1, y, i) + bd)
            tokf[y, pl.ds(i, BLK), :] = v.astype(BF)
            return cy

        rowloop(blk)

    def ln_bwd(l, r, par, gi, xbuf, emit, mine=False):
        gain = vrow(gi, l)

        def blk(i, cy):
            dg, db = cy
            if mine:
                wait_mine(par, i)
            else:
                wait_y(par, r, i)
            x = xbuf[l, r, pl.ds(i, BLK), :]
            dy = ysum(par, r, i)
            xc, rstd = ln_stats(x)
            xh = xc * rstd
            t1 = dy * gain
            m1 = jnp.sum(t1, axis=-1, keepdims=True) * (1.0 / D)
            m2 = jnp.sum(t1 * xh, axis=-1, keepdims=True) * (1.0 / D)
            dx = rstd * (t1 - m1 - xh * m2)
            emit(i, dx)
            dg = dg + jnp.sum(dy * xh, axis=0, keepdims=True)
            db = db + jnp.sum(dy, axis=0, keepdims=True)
            return (dg, db)

        z = jnp.zeros((1, D), F32)
        dg, db = rowloop(blk, (z, z))
        small[l, gi : gi + 1, :] = small[l, gi : gi + 1, :] + dg
        small[l, gi + 1 : gi + 2, :] = small[l, gi + 1 : gi + 2, :] + db

    def colsum_own(buf, r, l, row):
        def blk(i, cy):
            return cy + jnp.sum(buf[pl.ds(pl.multiple_of(own(r) + i, BLK), BLK), :].astype(F32), axis=0, keepdims=True)

        v = rowloop(blk, jnp.zeros((1, D), F32))
        small[l, row : row + 1, :] = small[l, row : row + 1, :] + v

    def enter_b1(l, r):
        cp = Tile(df_b, r, 2 + r if l == L - 1 else r)
        if l == L - 1:
            def blk(i, cy):
                v = cotf[r, pl.ds(i, BLK), :]
                dh_b[r, pl.ds(i, BLK), :] = v.astype(F32)
                df_b[pl.ds(pl.multiple_of(own(r) + i, BLK), BLK), :] = v
                cp.copy(i).start()
                return cy

            rowloop(blk)
        else:
            def emit(i, dx):
                v = dh_b[r, pl.ds(i, BLK), :] + dx
                dh_b[r, pl.ds(i, BLK), :] = v
                df_b[pl.ds(pl.multiple_of(own(r) + i, BLK), BLK), :] = v.astype(BF)
                cp.copy(i).start()

            ln_bwd(l + 1, r, 0, 0, h_b, emit)
        colsum_own(df_b, r, l, 5)
        return cp

    def du_tile(l, q0):
        def one(n, cy):
            n = pl.multiple_of(n * 256, 256)
            dg = mm(df_b[pl.ds(q0, R), :], wdown[l, pl.ds(n, 256), :], NT)
            du = (dg * gp_b[l, pl.ds(q0, R), pl.ds(n, 256)].astype(F32)).astype(BF)
            gp_b[l, pl.ds(q0, R), pl.ds(n, 256)] = du
            small[l, 7:8, pl.ds(n, 256)] = small[l, 7:8, pl.ds(n, 256)] + jnp.sum(du.astype(F32), axis=0, keepdims=True)
            return cy

        lax.fori_loop(0, FB, one, 0)

    def da2_tile(l, q0, dst):
        def one(n):
            dst[:, n : n + 256] = mm(gp_b[l, pl.ds(q0, R), :], wup[l, n : n + 256, :], NT).astype(dst.dtype)

        nblocks(one, NB)

    def ffn_bwd(l, r, tile_cp):
        own_first(r, tile_cp, lambda q0: du_tile(l, q0))
        if l == L - 1 and r == 1:
            pl.semaphore_wait(turned, 1)
        cp = send_partner(r, lambda ref: da2_tile(l, oth(r), ref))
        da2_tile(l, own(r), part)
        if tile_cp is not None:
            tile_cp.wait_send()
        combine(2, r, cp)

    def enter_b2(l, r):
        cp = Tile(dz_b, r)

        def emit(i, dx):
            v = dh_b[r, pl.ds(i, BLK), :] + dx
            dh_b[r, pl.ds(i, BLK), :] = v
            dz_b[pl.ds(pl.multiple_of(own(r) + i, BLK), BLK), :] = v.astype(BF)
            cp.copy(i).start()

        ln_bwd(l, r, 2, 3, m_b, emit)
        colsum_own(dz_b, r, l, 2)
        return cp

    def do_tile(l, q0):
        doT_b[:, pl.ds(q0, R)] = mm(wout[l], dz_b[pl.ds(q0, R), :], NT).astype(BF)

    def att_bwd_tile(l, r, q0):
        KB = 2 * (r + 1)
        KN = KB * R

        def head(h, cy):
            hr = pl.multiple_of(h * HEAD_DIM, HEAD_DIM)
            hm = hmask(h)
            qm = jnp.where(hm, qkvT[l, 0:HP, pl.ds(q0, R)].astype(F32), 0.0).astype(BF)
            dom = jnp.where(hm, doT_b[:, pl.ds(q0, R)].astype(F32), 0.0).astype(BF)
            do_h = doT_b[pl.ds(hr, HEAD_DIM), pl.ds(q0, R)]
            q_h = qkvT[l, pl.ds(hr, HEAD_DIM), pl.ds(q0, R)]
            o_h = oT_b[l, pl.ds(hr, HEAD_DIM), pl.ds(q0, R)]
            dsum = jnp.sum(do_h.astype(F32) * o_h.astype(F32), axis=0, keepdims=True)
            lse = lse_b[l, pl.ds(h, 1), pl.ds(q0, R)]
            for kb in range(KB):
                ks = slice(kb * R, kb * R + R)
                s = mm(kv_b[l, 0, ks, :], qm)
                p = jnp.exp(s - lse)
                if kb >= 2 * r:
                    p = jnp.where(visible(r, kb - 2 * r, q0), p, 0.0)
                p_b[ks, :] = p.astype(BF)
                dp = mm(kv_b[l, 1, ks, :], dom)
                ds_b[ks, :] = (p * (dp - dsum)).astype(BF)
            dkv_acc[1, pl.ds(hr, HEAD_DIM), 0:KN] = dkv_acc[1, pl.ds(hr, HEAD_DIM), 0:KN] + mm(do_h, p_b[0:KN, :], NT)
            dkv_acc[0, pl.ds(hr, HEAD_DIM), 0:KN] = dkv_acc[0, pl.ds(hr, HEAD_DIM), 0:KN] + mm(q_h, ds_b[0:KN, :], NT)
            k_h = qkvT[l, pl.ds(pl.multiple_of(HP + hr, HEAD_DIM), HEAD_DIM), 0:KN]
            dq = mm(k_h, ds_b[0:KN, :]) * (HEAD_DIM ** -0.5)
            dqT_b[pl.ds(hr, HEAD_DIM), pl.ds(q0, R)] = dq.astype(BF)
            return cy

        lax.fori_loop(0, NH, head, 0)

    def da_tile(l, q0, dst):
        dqkv = dqT_b[:, pl.ds(q0, R)].astype(F32).T.astype(BF)

        def one(n):
            dst[:, n : n + 256] = mm(dqkv, wqkv[l, :, n : n + 256]).astype(dst.dtype)

        nblocks(one, NB)

    def att_bwd(l, r, tile_cp, between=None):
        def both(q0):
            do_tile(l, q0)
            att_bwd_tile(l, r, q0)

        own_first(r, tile_cp, both, between)
        cs = slice(CH * r, CH * r + CH)
        for j in range(2):
            dqT_b[HP * (j + 1) : HP * (j + 1) + HL, cs] = dkv_acc[j, 0:HL, cs].astype(BF)
        cp = send_partner(r, lambda ref: da_tile(l, oth(r), ref))
        da_tile(l, own(r), part)
        tile_cp.wait_send()
        combine(0, r, cp, l == 0)

    WHOLE = (0, FL, 0)
    HALF = ((0, FL // 2, 0), (FL // 2, FL - FL // 2, 3))
    THIRD = tuple((i * 256, 256, 3 * i) for i in range(FL // 256))
    PARTS = THIRD[:2] + ((512, 128, 6), (640, 128, 9))

    def r1_copy(j, k, span):
        c0, w, extra = span
        q = j + extra
        peer = do_ * NI + lax.rem(di + k, NI)
        return dp_remote(send1.at[j, k - 1, :, c0 : c0 + w], recv1.at[j, k - 1, :, c0 : c0 + w],
                         r1s.at[q, k - 1], r1r.at[q, k - 1], peer)

    def r2_copy(j, k, span):
        c0, w, extra = span
        q = j + extra
        peer = lax.rem(do_ + k, NO) * NI + di
        return dp_remote(send2.at[j, k - 1, :, c0 : c0 + w], recv2.at[j, k - 1, :, c0 : c0 + w],
                         r2s.at[q, k - 1], r2r.at[q, k - 1], peer)

    def g_copy(l, j, span):
        c0, w, extra = span
        q = l * 12 + j + extra
        return pltpu.make_async_copy(fstage.at[l, j, :, c0 : c0 + w], g_o.at[l, j, :, c0 : c0 + w], gsem.at[q])

    def piece(q):
        return pl.ds(pl.multiple_of(q * PER, PER), PER)

    def rs_start(l, j, span=WHOLE):
        c0, w, _ = span
        cols = slice(c0, c0 + w)
        if not FUSED:
            cp = pltpu.make_async_copy(gstage.at[:, cols], g_o.at[l, j, :, cols], gsem.at[0])
            cp.start()
            cp.wait()
            return
        for k in range(1, NI):
            for oo in range(NO):
                send1[j, k - 1, oo * PER : oo * PER + PER, cols] = gstage[piece(oo * NI + lax.rem(di + k, NI)), cols].astype(BF)
            r1_copy(j, k, span).start()
        for oo in range(NO):
            own1[j, oo * PER : oo * PER + PER, cols] = gstage[piece(oo * NI + di), cols]

    def rs_mid(l, j, span=WHOLE):
        c0, w, _ = span
        cols = slice(c0, c0 + w)
        if not FUSED:
            return
        for k in range(1, NI):
            cp = r1_copy(j, k, span)
            cp.wait_send()
            cp.wait_recv()
        for kk in range(NO - 1, -1, -1):
            rows = piece(lax.rem(do_ + kk, NO))
            v = own1[j, rows, cols]
            for k in range(1, NI):
                v = v + recv1[j, k - 1, rows, cols].astype(F32)
            if kk == 0:
                own1[j, rows, cols] = v
            else:
                send2[j, kk - 1, :, cols] = v.astype(BF)
                r2_copy(j, kk, span).start()

    def rs_fin(l, j, span=WHOLE):
        c0, w, _ = span
        cols = slice(c0, c0 + w)
        if not FUSED:
            return
        v = own1[j, piece(do_), cols]
        for kk in range(1, NO):
            cp = r2_copy(j, kk, span)
            cp.wait_send()
            cp.wait_recv()
            v = v + recv2[j, kk - 1, :, cols].astype(F32)
        fstage[l, j, :, cols] = v
        g_copy(l, j, span).start()

    def wgrad_ffn(l, lhs, rhs, rows=slice(None), add=False):
        def one(n, cy):
            ns = pl.ds(pl.multiple_of(n * 256, 256), 256)
            lt = lhs[rows, ns].astype(F32).T.astype(BF)
            for f in range(FB):
                fs = slice(f * 256, f * 256 + 256)
                v = mm(lt, rhs[rows, fs])
                gstage[ns, fs] = gstage[ns, fs] + v if add else v
            return cy

        lax.fori_loop(0, NB, one, 0)

    def wgrad_att(l, span):
        lo, hi = span[0], span[0] + span[1]
        q = min(hi, 3 * HL)

        def one(n, cy):
            ns = pl.ds(pl.multiple_of(n * 256, 256), 256)
            s_b[lo:q, :] = mm(dqT_b[lo:q, :], a_b[l, :, ns])
            if hi > q:
                s_b[q:hi, :] = mm(oT_b[l], dz_b[:, ns])
            gstage[ns, lo:hi] = s_b[lo:hi, :].T
            return cy

        lax.fori_loop(0, NB, one, 0)

    for l in range(L):
        for r in range(2):
            if l == 0:
                if r == 0:
                    for cp in (loc[0], wcopies[0][0]):
                        cp.wait()
                    tcp[0].wait()
                    tcp[1].start()
                src = lambda i, r=r: tokf[r, pl.ds(i, BLK), :].astype(F32) + emb_b[0:1, :]
            else:
                bd = vrow(5, l - 1)
                src = lambda i, r=r, l=l, bd=bd: m_b[l - 1, r, pl.ds(i, BLK), :] + (ysum(1, r, i) + bd)
            if r == 0 and l > 0:
                wcopies[l][0].wait()
            cp = enter_fwd(l, r, src, 0, h_b, a_b, 1 if l > 0 else None)
            if r == 0:
                wcopies[l][1].wait()
            att_fwd(l, r, cp)
        for r in range(2):
            if l == L - 1 and r == 0:
                loc[1].wait()
                tcp[1].wait()
                b1 = [enter_b1(l, 0), enter_b1(l, 1)]
            elif l == L - 1:
                b1[0].wait_recv()
                wgrad_ffn(l, df_b, g_b.at[l], slice(0, CH))
            bo = vrow(2, l)
            src = lambda i, r=r, l=l, bo=bo: h_b[l, r, pl.ds(i, BLK), :] + (ysum(0, r, i) + bo)
            if r == 0:
                wcopies[l][2].wait()
                wcopies[l][3].wait()
            cp = enter_fwd(l, r, src, 3, m_b, a2_b, 0)
            ffn_fwd(l, r, cp)

    pl.semaphore_signal(turned, inc=1, device_id={"tensor": cpeer}, device_id_type=MESH)
    b1[1].wait_recv()
    wgrad_ffn(L - 1, df_b, g_b.at[L - 1], slice(CH, T), True)
    rs_start(L - 1, 2)
    for cp in b1:
        cp.wait_send()
    def many(fn, l, j, spans):
        for span in spans:
            fn(l, j, span)

    for l in range(L - 1, -1, -1):
        last = l == L - 1
        spans = (WHOLE,) if last else HALF
        ends = HALF if l > 0 else THIRD
        if last:
            for r in (1, 0):
                ffn_bwd(l, r, None)
            finish_output()
        else:
            ffn_bwd(l, 1, enter_b1(l, 1))
            many(rs_fin, l + 1, 2, (WHOLE,) if l + 1 == L - 1 else HALF)
            rs_mid(l + 1, 0, HALF[0])
            cp = enter_b1(l, 0)
            cp.wait_recv()
            wgrad_ffn(l, df_b, g_b.at[l])
            many(rs_start, l, 2, spans)
            cp.wait_send()
            many(rs_fin, l + 1, 1, (WHOLE,) if l + 1 == L - 1 else HALF)
            rs_mid(l + 1, 0, HALF[1])
            ffn_bwd(l, 0, None)
        wgrad_ffn(l, a2_b.at[l], gp_b.at[l])
        many(rs_start, l, 1, spans)
        dkv_acc[...] = jnp.zeros_like(dkv_acc)
        cp = enter_b2(l, 1)
        if not last:
            many(rs_fin, l + 1, 0, HALF)
        rs_mid(l, 2, spans[0])
        att_bwd(l, 1, cp, None if last else lambda l=l, span=HALF[1]: rs_mid(l, 2, span))
        cp = enter_b2(l, 0)
        att_bwd(l, 0, cp, lambda l=l, span=spans[0]: rs_mid(l, 1, span))
        for i, span in enumerate(ends):
            wgrad_att(l, span)
            if not last and i == 0:
                rs_mid(l, 1, HALF[1])
            many(rs_start, l, 0, PARTS[2:] if not last and i == 2 else (span,))
    ocp = pltpu.make_async_copy(tokf.at[y], out_o, osem.at[0])
    ocp.start()
    many(rs_fin, 0, 2, HALF)
    rs_mid(0, 0, PARTS[0])

    def emit(i, dx):
        v = dh_b[y, pl.ds(i, BLK), :] + dx
        dh_b[y, pl.ds(i, BLK), :] = v
        small[0, 6:7, :] = small[0, 6:7, :] + jnp.sum(v, axis=0, keepdims=True)

    ln_bwd(0, y, 0, 0, h_b, emit, True)
    gcp = pltpu.make_async_copy(dh_b.at[y], gtok_o, osem.at[1])
    gcp.start()
    scps = [remote(small, smallr.at[0:L], ssem.at[0], ssem.at[3], cpeer),
            remote(small.at[0], smallr.at[L], ssem.at[1], ssem.at[4], ypeer),
            remote(small.at[0], smallr.at[L + 1], ssem.at[2], ssem.at[5], dpeer)]
    for scp in scps:
        scp.start()
    many(rs_mid, 0, 0, PARTS[1:])
    for scp in scps:
        scp.wait()
    which = lax.broadcasted_iota(jnp.int32, (8, D), 0)
    small[0] = small[0] + jnp.where((which < 2) | (which == 6), smallr[L] + smallr[L + 1], 0.0)
    for l in range(L):
        small[l] = small[l] + jnp.where(which < 7, smallr[l], 0.0)
    small[1, 6:7, :] = jnp.full((1, D), ts_ref[0].astype(F32), F32)

    def x_copy(k):
        return dp_remote(smallp.at[k], smallx.at[d], x1s.at[k], x1r.at[k], lax.rem(d + k, N))

    def columns(k):
        turn = lax.rem(D - PER * lax.rem(d + k, N), D)
        return [pltpu.roll(small[l], turn, 1)[:, 0 : smallx.shape[3]] for l in range(L)]

    def x_go(k, cy):
        for l, v in enumerate(columns(k)):
            smallp[k, l] = v
        x_copy(k).start()
        return cy

    def x_wait(k, cy):
        cp = x_copy(k)
        cp.wait_send()
        cp.wait_recv()
        return cy

    lax.fori_loop(1, N, x_go, 0)
    for l, v in enumerate(columns(0)):
        smallx[d, l] = v
    many(rs_fin, 0, 1, HALF)
    many(rs_fin, 0, 0, PARTS[:-1])
    lax.fori_loop(1, N, x_wait, 0)
    smallx_o[...] = smallx[...]
    rs_fin(0, 0, PARTS[-1])
    ocp.wait()
    gcp.wait()
    if FUSED:
        for l in range(L):
            for j in range(3):
                for span in PARTS if l == 0 and j == 0 else HALF if l < L - 1 or j == 0 else (WHOLE,):
                    g_copy(l, j, span).wait()


def finish_kernel(dim, out_i, gtok_i, sx, g_i, out_o, gtok_o, table_o, dg1, db1, gq, go, dbo, dg2, db2, gup, dbup, gdown, dbd,
                  g_b, out_b, gtok_b, rows_b, sem_i, sem_o):
    FL, HL, L, PER, N, TS = dim["FL"], dim["HL"], dim["L"], dim["PER"], dim["N"], dim["TS"]
    ins = []
    for j in range(3):
        for l in range(L):
            ins.append(pltpu.make_async_copy(g_i.at[l, j], g_b.at[l, j], sem_i.at[l * 3 + j]))
    order = ((out_i, out_b, out_o), (gtok_i, gtok_b, gtok_o))
    for i, (src, buf, _) in enumerate(order):
        ins.append(pltpu.make_async_copy(src, buf, sem_i.at[3 * L + i]))
    for cp in ins:
        cp.start()
    for l in range(L):
        tot = sx[0, l]
        for q in range(1, N):
            tot = tot + sx[q, l]
        for i, ref in enumerate((dg1, db1, dbo, dg2, db2, dbd)):
            ref[l : l + 1, :] = tot[i : i + 1, 0:PER]
        dbup[l : l + 1, :] = tot[7:8, 0:PER]
    for q in range(N):
        rows_b[0, q : q + 1, :] = sx[q, 0, 6:7, :]
        rows_b[1, q : q + 1, :] = sx[q, 1, 6:7, :]
    step = rows_b[1, :, 0:1]
    pick = jnp.where(lax.broadcasted_iota(jnp.int32, (N, TS), 1).astype(F32) == step, 1.0, 0.0)
    table_o[...] = lax.dot_general(rows_b[0], pick, TN, precision=lax.Precision.HIGHEST, preferred_element_type=F32)[0:PER, :]
    for l in range(L):
        ins[l].wait()
        ga = g_b[l, 0]
        for cc in range(3):
            gq[l, cc] = ga[:, cc * HL : cc * HL + HL]
        gt = jnp.concatenate([ga, jnp.zeros((-PER % 128, 4 * HL), F32)], axis=0).T
        go[l] = gt[3 * HL : 4 * HL, 0:PER]
    outs = []
    for j, ref in ((1, gup), (2, gdown)):
        for l in range(L):
            ins[j * L + l].wait()
            cp = pltpu.make_async_copy(g_b.at[l, j], ref.at[l], sem_o.at[l * 2 + j - 1])
            cp.start()
            outs.append(cp)
    for i, (_, buf, dst) in enumerate(order):
        ins[3 * L + i].wait()
        cp = pltpu.make_async_copy(buf, dst, sem_o.at[2 * L + i])
        cp.start()
        outs.append(cp)
    for cp in outs:
        cp.wait()


def split_of(n):
    inner = 2 ** ((n.bit_length() - 1) // 2)
    return inner, n // inner


def run_step(ts, bs, vecs, bup, tok, cot, table, wqkv, wout, wup, wdown):
    R, D = tok.shape
    L, _, FL = wup.shape
    HL = wout.shape[1]
    N = lax.axis_size("dp")
    NI, NO = split_of(N)
    PER = D // N
    FUSED = PER % 16 == 0
    assert lax.axis_size("tensor") == 4 and ts.shape[0] == 1 and FL == D == 4 * HL and L > 1 and R == 256 and FL == 768
    T = 4 * R
    W = -(-PER // 128) * 128
    BLK = min(R, 128)
    HB = R // BLK
    dim = dict(D=D, FL=FL, HL=HL, R=R, L=L, BLK=BLK, W=W, N=N, NI=NI, NO=NO, PER=PER, FUSED=FUSED, TS=table.shape[0])
    vm = pl.BlockSpec(memory_space=pltpu.VMEM)
    sm = pl.BlockSpec(memory_space=pltpu.SMEM)
    any_ = pl.BlockSpec(memory_space=pl.ANY)
    dma = pltpu.SemaphoreType.DMA
    V = pltpu.VMEM
    J = 3 if FUSED else 1
    PR = PER if FUSED else 16
    ones = max(NI - 1, 1)
    outs = max(NO - 1, 1)
    kept = (L, 3, PER, FL) if FUSED else (L, 3, D, FL)
    return dim, pl.pallas_call(
        functools.partial(step_kernel, dim),
        out_shape=(
            jax.ShapeDtypeStruct((R, D), BF),
            jax.ShapeDtypeStruct((R, D), F32),
            jax.ShapeDtypeStruct((N, L, 8, W), F32),
            jax.ShapeDtypeStruct(kept, F32),
        ),
        in_specs=[sm, sm] + [vm] * 7 + [any_] * 7,
        out_specs=(any_, any_, vm, any_),
        scratch_shapes=[
            V((L, 3 * HL, D), BF), V((L, HL, D), BF), V((L, D, FL), BF), V((L, FL, D), BF),
            V((2, R, D), BF), V((2, R, D), BF),
            V((L, T, D), BF), V((L, T, D), BF), V((L, T, FL), BF), V((L, T, FL), BF),
            V((L, 3 * HL, T), BF), V((L, 2, T, HL), BF), V((L, HL, T), BF), V((L, 8, T), F32),
            V((L, 2, R, D), F32), V((L, 2, R, D), F32),
            V((T, D), BF), V((T, D), BF), V((2, R, D), F32),
            V((HL, T), BF), V((3 * HL, T), BF), V((2, HL, T), F32),
            V((3, 2, R, D), BF), V((3, 2, R, D), BF), V((2, R, D), BF), V((2, R, D), BF),
            V((R, D), F32), V((T, R), F32), V((T, R), BF), V((T, R), BF), V((D, FL), F32),
            V((L, 8, D), F32), V((L + 2, 8, D), F32), V((N, L, 8, W), F32), V((N, L, 8, W), F32), V((8, D), F32),
            V((J, ones, NO * PR, FL), BF), V((J, ones, NO * PR, FL), BF), V((J, NO * PR, FL), F32),
            V((J, outs, PR, FL), BF), V((J, outs, PR, FL), BF), V((L, J, PR, FL), F32),
            dma((L, 4)), dma((2,)), dma((2,)), dma((3, 2, HB)), dma((3, 2, HB)),
            dma((4, HB)), dma((4, HB)), dma((2,)), dma((2,)),
            dma((3,)), dma((2,)), dma((12 * L,)), dma((6,)), dma((N,)), dma((N,)),
            dma((12, ones)), dma((12, ones)), dma((12, outs)), dma((12, outs)), pltpu.SemaphoreType.REGULAR,
        ],
        compiler_params=pltpu.CompilerParams(
            collective_id=0, has_side_effects=True, vmem_limit_bytes=67043328),
        name="layers",
    )(ts, bs, *vecs, bup, tok, cot, table, wqkv, wout, wup, wdown)


def local(tokens, timestep, block_size, table, ln1_gain, ln1_bias, w_qkv, w_out, b_out,
          ln2_gain, ln2_bias, w_up, b_up, w_down, b_down, cotangent):
    L, D, _, HL = w_qkv.shape
    wq = jnp.transpose(w_qkv, (0, 2, 3, 1)).reshape(L, 3 * HL, D)
    vecs = (ln1_gain, ln1_bias, b_out, ln2_gain, ln2_bias, b_down)
    dim, (out, gtok, sx, g) = run_step(
        timestep, block_size, vecs, b_up, tokens, cotangent, table, wq, w_out, w_up, w_down)
    PER, FL, TS = dim["PER"], dim["FL"], dim["TS"]
    if not dim["FUSED"]:
        g = lax.psum_scatter(g, "dp", scatter_dimension=2, tiled=True)
    vec = jax.ShapeDtypeStruct((L, PER), F32)
    big = jax.ShapeDtypeStruct((L, PER, FL), F32)
    vm = pl.BlockSpec(memory_space=pltpu.VMEM)
    any_ = pl.BlockSpec(memory_space=pl.ANY)
    N, W = dim["N"], dim["W"]
    got = pl.pallas_call(
        functools.partial(finish_kernel, dim),
        out_shape=(
            jax.ShapeDtypeStruct(out.shape, BF), jax.ShapeDtypeStruct(gtok.shape, F32),
            jax.ShapeDtypeStruct((PER, TS), F32), vec, vec,
            jax.ShapeDtypeStruct((L, 3, PER, HL), F32), jax.ShapeDtypeStruct((L, HL, PER), F32),
            vec, vec, vec, big, vec, big, vec),
        in_specs=[any_, any_, vm, any_],
        out_specs=(any_, any_) + (vm,) * 8 + (any_, vm, any_, vm),
        scratch_shapes=[
            pltpu.VMEM((L, 3, PER, FL), F32), pltpu.VMEM(out.shape, BF), pltpu.VMEM(gtok.shape, F32),
            pltpu.VMEM((2, N, W), F32), pltpu.SemaphoreType.DMA((3 * L + 2,)), pltpu.SemaphoreType.DMA((2 * L + 2,))],
        name="finish",
    )(out, gtok, sx, g)
    got = list(got)
    got[2] = jnp.transpose(got[2])
    got[5] = jnp.transpose(got[5], (0, 2, 1, 3))
    got[12] = jnp.transpose(got[12], (0, 2, 1))
    return tuple(got)


def solution(mesh):
    placed = (
        P(("dp", "tensor"), None), P("dp"), P("dp"), P(), P(), P(),
        P(None, None, None, "tensor"), P(None, "tensor", None), P(), P(), P(),
        P(None, None, "tensor"), P(None, "tensor"), P(None, "tensor", None), P(),
        P(("dp", "tensor"), None),
    )
    return jax.shard_map(
        local,
        mesh=mesh,
        in_specs=placed,
        out_specs=(
            P(("dp", "tensor"), None), P(("dp", "tensor"), None), P(None, "dp"), P(None, "dp"), P(None, "dp"),
            P(None, "dp", None, "tensor"), P(None, "tensor", "dp"), P(None, "dp"), P(None, "dp"), P(None, "dp"),
            P(None, "dp", "tensor"), P(None, ("tensor", "dp")), P(None, "tensor", "dp"), P(None, "dp"),
        ),
        check_vma=False,
    )
```
